512 devices in a mesh: group: 16 (over z, core), member: 32 (over y, x).
Axes of the slice: x: 4, y: 8, z: 8, core: 2. Of those that a mesh axis runs over, the one named last changes fastest.
Arguments:
- tokens: bfloat16 [8192, 7168], P('group', 'member'), may hold values from -6 to 6
- grad_output: bfloat16 [8192, 7168], P('group', 'member'), may hold values from -6 to 6
- gate_prob: bfloat16 [8192, 16], P('group'), may hold values from 0.099609375 to 1
- w_gate: bfloat16 [16, 7168, 1024], P('group', 'member'), may hold values from -0.0625 to 0.0625
- w_up: bfloat16 [16, 7168, 1024], P('group', 'member'), may hold values from -0.0625 to 0.0625
- w_down: bfloat16 [16, 1024, 7168], P('group', None, 'member'), may hold values from -0.1875 to 0.1875
- expert_slot: int32 [16], replicated, may hold values from 0 to 15, each once
- block_counts: int32 [16, 16], replicated, may hold values from 0 to 10, as said below
- block_lists: int32 [16, 16, 10], P('group'), may hold values from 0 to 15, as said below
Outputs:
- layer_output: bfloat16 [8192, 7168], P('group', 'member')
- grad_input: bfloat16 [8192, 7168], P('group', 'member')
- grad_w_gate: bfloat16 [16, 7168, 1024], P('group', 'member')
- grad_w_up: bfloat16 [16, 7168, 1024], P('group', 'member')
- grad_w_down: bfloat16 [16, 1024, 7168], P('group', None, 'member')
The draws below stay inside these ranges and needn't reach their ends.
Inputs may be any that keep to these rules, and one draw needn't show every extreme that they name: `block_counts`: each group sends blocks to 1 to 2 experts and some group to exactly 2; each expert receives blocks from 1 to 2 groups and some expert from exactly 2; some count equals 10. `block_lists`: the first block_counts[g, e] entries of a list are distinct blocks of group g; later entries are block numbers that play no part. `expert_slot`: a permutation of the slots; slot s lies on group s.
All inputs are finite; a program needn't handle non-finite values.
Results may differ from the reference program's by a relative error of at most 0.034.
Values may be sent and summed in bfloat16 or wider, within the bound.
No kernel may reach another device: no remote copies, remote signals or barrier semaphores. Data moves between devices by JAX's collectives and lax.ppermute only.
A program may use at most 64 MiB of HBM per device.

```python
import math
import jax
import jax.numpy as jnp
from jax import lax

D = 7168
F = 1024
MAXE = 2
MAXB = 10
BLK = 32
NBLK = 16
EXPERTS = 16
TOKENS = 8192
N_GROUP = 16
N_MEMBER = 32


def routing_draw(key):
    first, second, third, fourth, fifth = jax.random.split(jax.random.fold_in(key, 7), 5)
    order = jax.random.permutation(first, EXPERTS)
    cycle = jax.random.permutation(fifth, N_GROUP).astype(jnp.int32)
    position = jnp.zeros((N_GROUP,), jnp.int32).at[cycle].set(jnp.arange(N_GROUP, dtype=jnp.int32))
    layer = jnp.arange(MAXE, dtype=jnp.int32)[:, None]
    group_ids = jnp.arange(N_GROUP, dtype=jnp.int32)[None, :]
    active = jax.random.randint(second, (MAXE, N_GROUP), 0, 2)
    forced = (layer == 0) | (group_ids == cycle[0])
    active = jnp.where(forced, 1, active)
    amounts = jax.random.randint(third, (MAXE, N_GROUP), 1, MAXB + 1)
    amounts = jnp.where((layer == 0) & (group_ids == 0), MAXB, amounts)
    partner = cycle[(position[None, :] + layer) % N_GROUP]
    chosen = order[partner]
    matched = (chosen[:, :, None] == jnp.arange(EXPERTS)[None, None, :]).astype(jnp.int32)
    counts = jnp.sum(matched * (active * amounts)[:, :, None], axis=0)
    keys = jax.random.split(fourth, N_GROUP * EXPERTS)
    lists = jax.vmap(lambda single: jax.random.permutation(single, NBLK)[:MAXB])(keys)
    return (counts.astype(jnp.int32), lists.reshape(N_GROUP, EXPERTS, MAXB).astype(jnp.int32))


def draw_block_counts(key, part):
    return routing_draw(key)[0]


def draw_block_lists(key, part):
    return routing_draw(key)[1]


def levels(rng, dims, shards, low, top_value):
    gain, own = 1.0, jax.random.fold_in(rng, 6)
    for dim, parts in shards:
        draws = jnp.exp(jax.random.uniform(jax.random.fold_in(own, dim), (parts,), jnp.float32, low / len(shards), top_value / len(shards)))
        gain = gain * jnp.repeat(draws, dims[dim] // parts).reshape([-1 if axis == dim else 1 for axis in range(len(dims))])
    return gain


def gaussian(stream_key, shape, width, reach, cuts=(), kind=jnp.bfloat16):
    drawn = width * jax.random.normal(stream_key, shape, jnp.float32)
    if cuts:
        drawn = drawn * levels(stream_key, shape, cuts, -0.22, 0.18)
    return jnp.clip(drawn, -reach, reach).astype(kind)


def setup_inputs(seed: int = 0) -> dict:
    seeds = jax.random.split(jax.random.key(seed), 10)
    tokens = gaussian(seeds[0], (TOKENS, D), 1.0, 6.0, ((0, 16), (1, 32)))
    grad_output = gaussian(seeds[1], (TOKENS, D), 1.0, 6.0, ((0, 16), (1, 32)))
    gate_prob = jnp.clip(jnp.exp(math.log(1.0) - 2.306499 * jax.random.uniform(seeds[2], (TOKENS, EXPERTS), jnp.float32) ** levels(seeds[2], (TOKENS, EXPERTS), ((0, 16),), -0.2, 0.2)), 0.099609375, 1.0).astype(jnp.bfloat16)
    w_gate = gaussian(seeds[3], (EXPERTS, D, F), D ** -0.5, 0.0625, ((0, 16), (1, 32)))
    w_up = gaussian(seeds[4], (EXPERTS, D, F), D ** -0.5, 0.0625, ((0, 16), (1, 32)))
    w_down = gaussian(seeds[5], (EXPERTS, F, D), F ** -0.5, 0.1875, ((0, 16), (2, 32)))
    expert_slot = jax.random.permutation(seeds[6], EXPERTS).astype(jnp.int32)
    block_counts = draw_block_counts(jax.random.fold_in(seeds[9], 71), 0)
    block_lists = draw_block_lists(jax.random.fold_in(seeds[9], 71), 0)
    return {"tokens": tokens, "grad_output": grad_output, "gate_prob": gate_prob, "w_gate": w_gate, "w_up": w_up, "w_down": w_down, "expert_slot": expert_slot, "block_counts": block_counts, "block_lists": block_lists}


def member_sum(left_operand, right_operand):
    count_value = left_operand.shape[0]
    share_portion = D // N_MEMBER
    part_pieces = jnp.einsum("glb,lbv->lgv", left_operand.astype(jnp.float32).reshape(count_value, N_MEMBER, share_portion), right_operand.astype(jnp.float32).reshape(N_MEMBER, share_portion, right_operand.shape[1]))
    part_pieces = lax.optimization_barrier(part_pieces.astype(jnp.bfloat16))
    return jnp.sum(part_pieces.astype(jnp.float32), axis=0)


def expert_ref(input_rows, rows_dy, rows_p, gate_w, up_w, down_w):
    gate = member_sum(input_rows, gate_w)
    up = member_sum(input_rows, up_w)
    sigma = jax.nn.sigmoid(gate)
    hidden_state = (gate * sigma * up).astype(jnp.bfloat16)
    outcome = (rows_p[:, None] * jnp.dot(hidden_state, down_w, preferred_element_type=jnp.float32)).astype(jnp.bfloat16)
    gradient_rows = (rows_p[:, None] * rows_dy.astype(jnp.float32)).astype(jnp.bfloat16)
    grad_hidden = member_sum(gradient_rows, down_w.T)
    gate_gradient = (grad_hidden * up * sigma * (1.0 + gate * (1.0 - sigma))).astype(jnp.bfloat16)
    up_gradient = (grad_hidden * gate * sigma).astype(jnp.bfloat16)
    rows_dx = (jnp.dot(gate_gradient, gate_w.T, preferred_element_type=jnp.float32) + jnp.dot(up_gradient, up_w.T, preferred_element_type=jnp.float32)).astype(jnp.bfloat16)
    part_gate = jnp.dot(input_rows.T, gate_gradient, preferred_element_type=jnp.float32).astype(jnp.bfloat16)
    part_up = jnp.dot(input_rows.T, up_gradient, preferred_element_type=jnp.float32).astype(jnp.bfloat16)
    part_down = jnp.dot(hidden_state.T, gradient_rows, preferred_element_type=jnp.float32).astype(jnp.bfloat16)
    return outcome, rows_dx, part_gate, part_up, part_down


def reference(tokens, grad_output, gate_prob, w_gate, w_up, w_down, expert_slot, block_counts, block_lists):
    in_use = (block_counts > 0).astype(jnp.int32)
    slot_ids = jnp.arange(EXPERTS, dtype=jnp.int32)
    slot_expert = jnp.sum(slot_ids[None, :] * (expert_slot[None, :] == slot_ids[:, None]).astype(jnp.int32), axis=1).astype(jnp.int32)
    tok_blocks = tokens.reshape(N_GROUP, NBLK, BLK, D)
    grad_blocks = grad_output.reshape(N_GROUP, NBLK, BLK, D)
    prob_blocks = gate_prob.reshape(N_GROUP, NBLK, BLK, EXPERTS)
    group_ids = jnp.arange(N_GROUP, dtype=jnp.int32)
    block_ids = jnp.arange(NBLK, dtype=jnp.int32)
    entry_ids = jnp.arange(MAXB, dtype=jnp.int32)

    def per_slot(carry, slot_id):
        out_total, dx_total = carry
        expert_id = slot_expert[slot_id]
        users = in_use[:, expert_id]
        use_rank = jnp.cumsum(users) - 1
        gate_w = w_gate[slot_id]
        up_w = w_up[slot_id]
        down_w = w_down[slot_id]
        total_gate = jnp.zeros((D, F), jnp.float32)
        total_up = jnp.zeros((D, F), jnp.float32)
        total_down = jnp.zeros((F, D), jnp.float32)
        for user in range(MAXE):
            chosen = users * (use_rank == user).astype(jnp.int32)
            valid = jnp.sum(chosen)
            group_id = jnp.sum(chosen * group_ids).astype(jnp.int32)
            count_value = block_counts[group_id, expert_id] * valid
            listed = block_lists[group_id, expert_id].astype(jnp.int32)
            keep_rows = (entry_ids < count_value).astype(jnp.int32)
            input_rows = (tok_blocks[group_id][listed] * keep_rows[:, None, None].astype(jnp.bfloat16)).reshape(MAXB * BLK, D)
            rows_dy = grad_blocks[group_id][listed].reshape(MAXB * BLK, D)
            rows_p = (prob_blocks[group_id][listed][:, :, expert_id].astype(jnp.float32) * keep_rows[:, None].astype(jnp.float32)).reshape(MAXB * BLK)
            outcome, rows_dx, part_gate, part_up, part_down = expert_ref(input_rows, rows_dy, rows_p, gate_w, up_w, down_w)
            placing = ((listed[:, None] == block_ids[None, :]) & (keep_rows[:, None] > 0)).astype(jnp.float32)
            out_total = out_total.at[group_id].add(jnp.einsum("bk,btd->ktd", placing, outcome.astype(jnp.float32).reshape(MAXB, BLK, D)))
            dx_total = dx_total.at[group_id].add(jnp.einsum("bk,btd->ktd", placing, rows_dx.astype(jnp.float32).reshape(MAXB, BLK, D)))
            total_gate = total_gate + part_gate.astype(jnp.float32)
            total_up = total_up + part_up.astype(jnp.float32)
            total_down = total_down + part_down.astype(jnp.float32)
        return (out_total, dx_total), (total_gate.astype(jnp.bfloat16), total_up.astype(jnp.bfloat16), total_down.astype(jnp.bfloat16))

    start = (jnp.zeros((N_GROUP, NBLK, BLK, D), jnp.float32), jnp.zeros((N_GROUP, NBLK, BLK, D), jnp.float32))
    (out_total, dx_total), (grad_w_gate, grad_w_up, grad_w_down) = lax.scan(per_slot, start, slot_ids)
    layer_output = out_total.reshape(N_GROUP * NBLK * BLK, D).astype(jnp.bfloat16)
    grad_input = dx_total.reshape(N_GROUP * NBLK * BLK, D).astype(jnp.bfloat16)
    return (layer_output, grad_input, grad_w_gate, grad_w_up, grad_w_down)
```

```python
import jax
import jax.numpy as jnp
from jax import lax
from jax.experimental import pallas as pl
from jax.experimental.pallas import tpu as pltpu
from jax.sharding import Mesh, PartitionSpec as P

BLK = 32
USERS = 2
LANES = 512
P_LANE = 224
DY_LANE = 256
LIST_LANE = 480
GROUP = ("z", "core")
F32 = jnp.float32
BF16 = jnp.bfloat16
VMEM_LIMIT = 56 * 1024 * 1024


def dot(a, b, ca, cb):
    return lax.dot_general(a, b, (((ca,), (cb,)), ((), ())), preferred_element_type=F32)


def call(kernel, out_shape, args, **kw):
    return pl.pallas_call(
        kernel,
        out_shape=out_shape,
        compiler_params=pltpu.CompilerParams(vmem_limit_bytes=VMEM_LIMIT),
        **kw,
    )(*args)


def token_permutation(rows):
    o = lax.broadcasted_iota(jnp.int32, (rows, rows), 0)
    t = lax.broadcasted_iota(jnp.int32, (rows, rows), 1)
    source = ((o >> 1) & 15) * BLK + (o >> 5) * 2 + (o & 1)
    return (t == source).astype(BF16)


def pack_kernel(tok_ref, dy_ref, prob_ref, list_ref, out_ref, all_ref):
    width = tok_ref.shape[0]
    all_ref[...] = jnp.zeros_like(all_ref)
    all_ref[0:width] = tok_ref[...]
    all_ref[P_LANE : P_LANE + 16] = prob_ref[...]
    all_ref[DY_LANE : DY_LANE + width] = dy_ref[...]
    packed = dot(token_permutation(LANES), all_ref[...], 1, 1)
    packed = packed.reshape(out_ref.shape) + list_ref[...].astype(F32)[None]
    out_ref[...] = packed.astype(BF16)


def select_kernel(rows_ref, info_ref, out_ref, pick_ref):
    rows = rows_ref[...]
    total = info_ref.shape[0]
    columns = lax.broadcasted_iota(jnp.int32, (total, rows.shape[0]), 1)
    list_rows = (columns == info_ref[:, 0:1]).astype(BF16)
    lists = dot(list_rows, rows[:, 384:512], 1, 0)
    lanes = lax.broadcasted_iota(jnp.int32, lists.shape, 1) + 384
    block = jnp.sum(jnp.where(lanes == info_ref[:, 2:3], lists, 0.0), axis=1, keepdims=True)
    column = info_ref[:, 1:2] + 2 * block.astype(jnp.int32)
    pick = (columns == column).astype(BF16)
    pick_ref[...] = pick
    out_ref[...] = dot(pick, rows, 1, 0).astype(BF16)


def row_prob(rows, mark):
    return jnp.sum(rows[:, 0:256].astype(F32) * mark, axis=1, keepdims=True)


def hidden_kernel(rows_ref, panel_ref, mark_ref, out_ref, acc_ref):
    step = pl.program_id(0)
    rows = rows_ref[0]
    count = rows.shape[0]
    hid = panel_ref.shape[2]
    x = rows[:, 0:P_LANE]
    prob = row_prob(rows, mark_ref[...])
    grad = (prob * rows[:, DY_LANE : DY_LANE + P_LANE].astype(F32)).astype(BF16)

    @pl.when(step == 0)
    def _():
        acc_ref[...] = jnp.zeros_like(acc_ref)

    acc_ref[0] += dot(x, panel_ref[0, 0:224], 1, 0)
    acc_ref[1] += dot(x, panel_ref[0, 224:448], 1, 0)
    acc_ref[2] += dot(grad, panel_ref[0, 448:672], 1, 0)

    @pl.when(step == pl.num_programs(0) - 1)
    def _():
        for part in range(3):
            for piece in range(hid // 128):
                out_ref[piece, part * count : (part + 1) * count] = acc_ref[
                    part, :, piece * 128 : (piece + 1) * 128
                ].astype(BF16)


def point_kernel(parts_ref, out_ref):
    count = out_ref.shape[0] // 3
    total = jnp.sum(parts_ref[...].astype(F32), axis=0)
    gate, up, grad = total[0:count], total[count : 2 * count], total[2 * count :]
    sigma = jax.nn.sigmoid(gate)
    out_ref[0:count] = (gate * sigma * up).astype(BF16)
    out_ref[count : 2 * count] = (grad * up * sigma * (1.0 + gate * (1.0 - sigma))).astype(BF16)
    out_ref[2 * count :] = (grad * gate * sigma).astype(BF16)


def hidden_parts(act_ref):
    count = act_ref.shape[1] // 3
    return [
        jnp.concatenate(
            [act_ref[k, i * count : (i + 1) * count] for k in range(act_ref.shape[0])], axis=1
        )
        for i in range(3)
    ]


def result_kernel(act_ref, panel_ref, rows_ref, mark_ref, out_ref):
    hidden, gate_grad, up_grad = hidden_parts(act_ref)
    prob = row_prob(rows_ref[0], mark_ref[...])
    outcome = prob * dot(hidden, panel_ref[0, 448:672], 1, 1)
    dx = dot(gate_grad, panel_ref[0, 0:224], 1, 1) + dot(up_grad, panel_ref[0, 224:448], 1, 1)
    out_ref[0] = jnp.zeros_like(out_ref[0])
    out_ref[0, :, 0:P_LANE] = outcome.astype(BF16)
    out_ref[0, :, DY_LANE : DY_LANE + P_LANE] = dx.astype(BF16)


def weight_kernel(act_ref, rows_ref, mark_ref, out_ref):
    hidden, gate_grad, up_grad = hidden_parts(act_ref)
    rows = rows_ref[0]
    x = rows[:, 0:P_LANE]
    prob = row_prob(rows, mark_ref[...])
    grad = (prob * rows[:, DY_LANE : DY_LANE + P_LANE].astype(F32)).astype(BF16)
    out_ref[0, 0:224] = dot(x, gate_grad, 0, 0).astype(BF16)
    out_ref[0, 224:448] = dot(x, up_grad, 0, 0).astype(BF16)
    out_ref[0, 448:672] = dot(grad, hidden, 0, 0).astype(BF16)


def combine_kernel(pick_ref, rows_ref, out_ref):
    out_ref[...] = dot(pick_ref[...], rows_ref[...], 0, 0).astype(BF16)


def unpack_kernel(rows_ref, out_ref, dx_ref):
    result = dot(rows_ref[...], token_permutation(LANES), 0, 0).astype(BF16)
    out_ref[...] = result[0:P_LANE]
    dx_ref[...] = result[DY_LANE : DY_LANE + P_LANE]


def routing_info(expert_slot, block_counts, entries):
    groups, experts = block_counts.shape
    ids = jnp.arange(experts, dtype=jnp.int32)
    slot_is = (expert_slot[:, None] == ids[None, :]).astype(jnp.int32)
    slot_expert = jnp.sum(slot_is * ids[:, None], axis=0)
    counts = jnp.sum(block_counts[:, :, None] * slot_is[None], axis=1)
    used = (counts > 0).astype(jnp.int32)
    before = (ids[:, None] < ids[None, :]).astype(jnp.int32)
    rank = jnp.sum(used[:, None, :] * before[:, :, None], axis=0)
    user_ids = jnp.arange(USERS, dtype=jnp.int32)
    chosen = used[:, :, None] * (rank[:, :, None] == user_ids).astype(jnp.int32)
    user_group = jnp.sum(chosen * ids[:, None, None], axis=0)
    user_count = jnp.sum(chosen * counts[:, :, None], axis=0)
    shape = (groups, USERS, entries, 2)
    entry = lax.broadcasted_iota(jnp.int32, shape, 2)
    row = lax.broadcasted_iota(jnp.int32, shape, 3)
    group = user_group[:, :, None, None]
    list_row = jnp.broadcast_to(group * BLK + slot_expert[:, None, None, None], shape)
    base = jnp.where(entry < user_count[:, :, None, None], group * BLK + row, -100000)
    info = jnp.stack([list_row, base, entry + LIST_LANE], axis=-1)
    return info.reshape(-1, 3), slot_expert


def exchange(array, axis):
    return lax.all_to_all(array, axis, split_axis=0, concat_axis=0, tiled=True)


def body(
    tokens, grad_output, gate_prob, w_gate, w_up, w_down, expert_slot, block_counts, block_lists
):
    groups = lax.axis_size(GROUP)
    share_y = lax.axis_size("y")
    share_x = lax.axis_size("x")
    width = tokens.shape[1]
    hid = w_gate.shape[2]
    entries = block_lists.shape[2]
    picked = USERS * entries * 2
    total = groups * picked
    count = total // share_x

    panels = jnp.concatenate([w_gate[0], w_up[0], w_down[0].T], axis=0)
    panels = lax.all_gather(panels, "x", axis=0, tiled=False)

    lists = lax.pad(
        block_lists[0].astype(BF16),
        jnp.zeros((), BF16),
        ((0, BLK - 16, 0), (LIST_LANE, LANES - LIST_LANE - entries, 0)),
    )
    packed = call(
        pack_kernel,
        jax.ShapeDtypeStruct((groups, BLK, LANES), BF16),
        (tokens.T, grad_output.T, gate_prob.T, lists),
        scratch_shapes=[pltpu.VMEM((LANES, LANES), BF16)],
    )
    info, slot_expert = routing_info(expert_slot, block_counts, entries)
    expert = lax.dynamic_index_in_dim(slot_expert, lax.axis_index(GROUP), 0, keepdims=False)
    mark = (jnp.arange(256, dtype=jnp.int32) == P_LANE + expert).astype(F32)[None]
    spread = exchange(packed, GROUP).reshape(groups * BLK, LANES)
    sent, pick = call(
        select_kernel,
        (
            jax.ShapeDtypeStruct((total, LANES), BF16),
            jax.ShapeDtypeStruct((total, groups * BLK), BF16),
        ),
        (spread, info),
    )
    got = exchange(sent.reshape(groups, picked, LANES), GROUP)
    rows = exchange(got.reshape(share_x, count, LANES), "x")

    row_spec = pl.BlockSpec((1, count, LANES), lambda i: (i, 0, 0))
    panel_spec = pl.BlockSpec((1, 3 * width, hid), lambda i: (i, 0, 0))
    mark_spec = pl.BlockSpec((1, 256), lambda i: (0, 0))
    act_shape = (share_y, 3 * count, hid // share_y)
    act_spec = pl.BlockSpec(act_shape, lambda i: (0, 0, 0))
    parts = call(
        hidden_kernel,
        jax.ShapeDtypeStruct(act_shape, BF16),
        (rows, panels, mark),
        grid=(share_x,),
        in_specs=[row_spec, panel_spec, mark_spec],
        out_specs=act_spec,
        scratch_shapes=[pltpu.VMEM((3, count, hid), F32)],
    )
    parts = exchange(parts, "y")
    act = call(point_kernel, jax.ShapeDtypeStruct(act_shape[1:], BF16), (parts,))
    act = lax.all_gather(act, "y", axis=0, tiled=False)
    results = call(
        result_kernel,
        jax.ShapeDtypeStruct((share_x, count, LANES), BF16),
        (act, panels, rows, mark),
        grid=(share_x,),
        in_specs=[act_spec, panel_spec, row_spec, mark_spec],
        out_specs=row_spec,
    )
    weights = call(
        weight_kernel,
        jax.ShapeDtypeStruct((share_x, 3 * width, hid), BF16),
        (act, rows, mark),
        grid=(share_x,),
        in_specs=[act_spec, row_spec, mark_spec],
        out_specs=panel_spec,
    )
    weights = lax.psum_scatter(weights, "x", scatter_dimension=0, tiled=False)
    back = exchange(results, "x").reshape(groups, picked, LANES)
    back = exchange(back, GROUP).reshape(total, LANES)
    summed = call(combine_kernel, jax.ShapeDtypeStruct((groups * BLK, LANES), BF16), (pick, back))
    home = exchange(summed.reshape(groups, BLK, LANES), GROUP).reshape(groups * BLK, LANES)
    out, dx = call(
        unpack_kernel,
        (jax.ShapeDtypeStruct((width, groups * BLK), BF16),) * 2,
        (home,),
    )
    return (
        out.T,
        dx.T,
        weights[None, 0:width],
        weights[None, width : 2 * width],
        weights[2 * width :].T[None],
    )


def solution(mesh):
    devices = mesh.devices.reshape(8, 2, 8, 4)
    inner = Mesh(devices, ("z", "core", "y", "x"))
    member = ("y", "x")
    in_specs = (
        P(GROUP, member),
        P(GROUP, member),
        P(GROUP, None),
        P(GROUP, member, None),
        P(GROUP, member, None),
        P(GROUP, None, member),
        P(),
        P(),
        P(GROUP, None, None),
    )
    out_specs = (
        P(GROUP, member),
        P(GROUP, member),
        P(GROUP, member, None),
        P(GROUP, member, None),
        P(GROUP, None, member),
    )
    return jax.shard_map(body, mesh=inner, in_specs=in_specs, out_specs=out_specs, check_vma=False)
```

```python
import jax
import jax.numpy as jnp
from jax import lax
from jax.experimental import pallas as pl
from jax.experimental.pallas import tpu as pltpu
from jax.sharding import Mesh, PartitionSpec as P

BLK = 32
USERS = 2
LANES = 512
P_LANE = 224
DY_LANE = 256
LIST_LANE = 480
GROUP = ("z", "core")
OWNERS = ("x", "z", "core")
F32 = jnp.float32
BF16 = jnp.bfloat16
VMEM_LIMIT = 24 * 1024 * 1024
VMEM_LARGE = 56 * 1024 * 1024


def dot(a, b, ca, cb):
    return lax.dot_general(a, b, (((ca,), (cb,)), ((), ())), preferred_element_type=F32)


def call(kernel, out_shape, args, limit=VMEM_LIMIT, **kw):
    return pl.pallas_call(
        kernel,
        out_shape=out_shape,
        compiler_params=pltpu.CompilerParams(vmem_limit_bytes=limit),
        **kw,
    )(*args)


def token_permutation(rows):
    o = lax.broadcasted_iota(jnp.int32, (rows, rows), 0)
    t = lax.broadcasted_iota(jnp.int32, (rows, rows), 1)
    source = ((o >> 1) & 15) * BLK + (o >> 5) * 2 + (o & 1)
    return (t == source).astype(BF16)


def pack_kernel(tok_ref, dy_ref, prob_ref, list_ref, out_ref, all_ref):
    width = tok_ref.shape[0]
    all_ref[...] = jnp.zeros_like(all_ref)
    all_ref[0:width] = tok_ref[...]
    all_ref[P_LANE : P_LANE + 16] = prob_ref[...]
    all_ref[DY_LANE : DY_LANE + width] = dy_ref[...]
    packed = dot(token_permutation(LANES), all_ref[...], 1, 1)
    packed = packed.reshape(out_ref.shape) + list_ref[...].astype(F32)[None]
    out_ref[...] = packed.astype(BF16)


def split_lanes(tmp_ref, rows):
    count = rows.shape[0]
    for c in range(4):
        tmp_ref[pl.ds(c, count, stride=4), :] = rows[:, c * 128 : (c + 1) * 128]
    return tmp_ref[...].astype(BF16)


def join_lanes(tmp_ref, tiles):
    tmp_ref[...] = tiles.astype(F32)
    count = tmp_ref.shape[0] // 4
    return jnp.concatenate([tmp_ref[pl.ds(c, count, stride=4), :] for c in range(4)], axis=1)


def select_kernel(rows_ref, info_ref, out_ref, pick_ref, tmp_ref):
    rows = rows_ref[...]
    total = info_ref.shape[0]
    columns = lax.broadcasted_iota(jnp.int32, (total, rows.shape[0]), 1)
    list_rows = (columns == info_ref[:, 0:1]).astype(BF16)
    lists = dot(list_rows, rows[:, 384:512], 1, 0)
    lanes = lax.broadcasted_iota(jnp.int32, lists.shape, 1) + 384
    block = jnp.sum(jnp.where(lanes == info_ref[:, 2:3], lists, 0.0), axis=1, keepdims=True)
    column = info_ref[:, 1:2] + 2 * block.astype(jnp.int32)
    pick = (columns == column).astype(BF16)
    pick_ref[...] = pick
    out_ref[...] = split_lanes(tmp_ref, dot(pick, rows, 1, 0))


def hidden_kernel(x_ref, tiles_ref, mark_ref, gate_ref, *refs):
    down_refs, (out_ref, rows_ref, prob_ref, acc_ref, tmp_ref) = refs[:4], refs[4:]
    step = pl.program_id(0)
    rows = join_lanes(tmp_ref, tiles_ref[0])
    count = rows.shape[0]
    hid = gate_ref.shape[2]
    width = gate_ref.shape[1] // 2
    prob = jnp.sum(rows[:, 0:256] * mark_ref[...], axis=1, keepdims=True)
    x = rows[:, 0:256].astype(BF16)
    grad = (prob * rows[:, DY_LANE:LANES]).astype(BF16)
    rows_ref[0, :, 0:DY_LANE] = x
    rows_ref[0, :, DY_LANE:LANES] = grad
    prob_ref[...] = jnp.broadcast_to(prob, prob_ref.shape)
    x = x[:, 0:width]
    grad = grad[:, 0:width]

    @pl.when(step == 0)
    def _():
        acc_ref[...] = jnp.zeros_like(acc_ref)

    acc_ref[0] += dot(x, gate_ref[0, 0:width], 1, 0)
    acc_ref[1] += dot(x, gate_ref[0, width : 2 * width], 1, 0)
    for d in range(4):

        @pl.when(step == d)
        def _():
            acc_ref[2] += dot(grad, down_refs[d][...], 1, 0)

    @pl.when(step == pl.num_programs(0) - 1)
    def _():
        for part in range(3):
            for piece in range(hid // 128):
                out_ref[piece, part * count : (part + 1) * count] = acc_ref[
                    part, :, piece * 128 : (piece + 1) * 128
                ].astype(BF16)


def point_kernel(parts_ref, out_ref):
    count = out_ref.shape[0] // 3
    total = jnp.sum(parts_ref[...].astype(F32), axis=0)
    gate, up, grad = total[0:count], total[count : 2 * count], total[2 * count :]
    sigma = jax.nn.sigmoid(gate)
    out_ref[0:count] = (gate * sigma * up).astype(BF16)
    out_ref[count : 2 * count] = (grad * up * sigma * (1.0 + gate * (1.0 - sigma))).astype(BF16)
    out_ref[2 * count :] = (grad * gate * sigma).astype(BF16)


def hidden_parts(act_ref):
    count = act_ref.shape[1] // 3
    return [
        jnp.concatenate(
            [act_ref[k, i * count : (i + 1) * count] for k in range(act_ref.shape[0])], axis=1
        )
        for i in range(3)
    ]


def result_kernel(x_ref, act_ref, prob_ref, gate_ref, *refs):
    down_refs, (out_ref, res_ref, tmp_ref) = refs[:4], refs[4:]
    step = pl.program_id(0)
    width = gate_ref.shape[1] // 2
    hidden, gate_grad, up_grad = hidden_parts(act_ref)

    @pl.when(step == 0)
    def _():
        res_ref[...] = jnp.zeros_like(res_ref)

    for d in range(4):

        @pl.when(step == d)
        def _():
            outcome = prob_ref[:, 0:1] * dot(hidden, down_refs[d][...], 1, 1)
            res_ref[:, 0:width] = outcome

    dx = dot(gate_grad, gate_ref[0, 0:width], 1, 1)
    dx += dot(up_grad, gate_ref[0, width : 2 * width], 1, 1)
    res_ref[:, DY_LANE : DY_LANE + width] = dx
    out_ref[0] = split_lanes(tmp_ref, res_ref[...])


def gate_grad_kernel(act_ref, rows_ref, out_ref):
    _, gate_grad, up_grad = hidden_parts(act_ref)
    width = out_ref.shape[1] // 2
    x = rows_ref[0, :, 0:width]
    out_ref[0, 0:width] = dot(x, gate_grad, 0, 0).astype(BF16)
    out_ref[0, width : 2 * width] = dot(x, up_grad, 0, 0).astype(BF16)


def down_grad_kernel(x_ref, act_ref, rows_ref, *out_refs):
    hidden = hidden_parts(act_ref)[0]
    width = out_refs[0].shape[0]
    grad = rows_ref[0, :, DY_LANE : DY_LANE + width]
    for d in range(4):

        @pl.when(pl.program_id(0) == d)
        def _():
            out_refs[d][...] = dot(grad, hidden, 0, 0).astype(BF16)


def sum_kernel(*refs):
    total = refs[0][...].astype(F32)
    for ref in refs[1:-1]:
        total += ref[...].astype(F32)
    refs[-1][...] = total.astype(BF16)


def combine_kernel(pick_ref, tiles_ref, out_ref, tmp_ref):
    rows = join_lanes(tmp_ref, tiles_ref[...]).astype(BF16)
    out_ref[...] = dot(pick_ref[...], rows, 0, 0).astype(BF16)


def unpack_kernel(rows_ref, out_ref, dx_ref):
    result = dot(rows_ref[...], token_permutation(LANES), 0, 0).astype(BF16)
    out_ref[...] = result[0:P_LANE]
    dx_ref[...] = result[DY_LANE : DY_LANE + P_LANE]


def routing_info(expert_slot, block_counts, entries, share_x):
    groups, experts = block_counts.shape
    ids = jnp.arange(experts, dtype=jnp.int32)
    slot_is = (expert_slot[:, None] == ids[None, :]).astype(jnp.int32)
    slot_expert = jnp.sum(slot_is * ids[:, None], axis=0)
    counts = jnp.sum(block_counts[:, :, None] * slot_is[None], axis=1)
    used = (counts > 0).astype(jnp.int32)
    before = (ids[:, None] < ids[None, :]).astype(jnp.int32)
    rank = jnp.sum(used[:, None, :] * before[:, :, None], axis=0)
    user_ids = jnp.arange(USERS, dtype=jnp.int32)[:, None, None]
    chosen = used[None] * (rank[None] == user_ids).astype(jnp.int32)
    user_group = jnp.sum(chosen * ids[None, :, None], axis=1)
    user_count = jnp.sum(chosen * counts[None], axis=1)
    per_x = USERS * entries * 2 // share_x
    shape = (share_x, groups, per_x)
    member = lax.broadcasted_iota(jnp.int32, shape, 0) * per_x
    member = member + lax.broadcasted_iota(jnp.int32, shape, 2)
    first = member < entries * 2
    entry = (member >> 1) - jnp.where(first, 0, entries)
    group = jnp.where(first, user_group[0][None, :, None], user_group[1][None, :, None])
    limit = jnp.where(first, user_count[0][None, :, None], user_count[1][None, :, None])
    list_row = group * BLK + slot_expert[None, :, None]
    base = jnp.where(entry < limit, group * BLK + (member & 1), -100000)
    info = jnp.stack([list_row, base, entry + LIST_LANE], axis=-1)
    return info.reshape(-1, 3)


def exchange(array, axis):
    return lax.all_to_all(array, axis, split_axis=0, concat_axis=0, tiled=True)


def body(
    tokens, grad_output, gate_prob, w_gate, w_up, w_down, expert_slot, block_counts, block_lists
):
    groups = lax.axis_size(GROUP)
    share_y = lax.axis_size("y")
    share_x = lax.axis_size("x")
    width = tokens.shape[1]
    hid = w_gate.shape[2]
    entries = block_lists.shape[2]
    picked = USERS * entries * 2
    total = groups * picked
    count = total // share_x

    me_x = lax.axis_index("x")
    order = me_x[None].astype(jnp.int32)
    shifts = [[(i, (i + d) % share_x) for i in range(share_x)] for d in range(share_x)]

    gates = jnp.concatenate([w_gate[0], w_up[0]], axis=0)
    gates = lax.all_gather(gates, "x", axis=0, tiled=False)
    down = w_down[0].T
    downs = [down] + [lax.ppermute(down, "x", shifts[d]) for d in range(1, share_x)]

    lists = lax.pad(
        block_lists[0].astype(BF16),
        jnp.zeros((), BF16),
        ((0, BLK - 16, 0), (LIST_LANE, LANES - LIST_LANE - entries, 0)),
    )
    packed = call(
        pack_kernel,
        jax.ShapeDtypeStruct((groups, BLK, LANES), BF16),
        (tokens.T, grad_output.T, gate_prob.T, lists),
        scratch_shapes=[pltpu.VMEM((LANES, LANES), BF16)],
    )
    info = routing_info(expert_slot, block_counts, entries, share_x)
    mine = (expert_slot == lax.axis_index(GROUP)).astype(F32)
    mark = lax.pad(mine, jnp.zeros((), F32), ((P_LANE, 16, 0),))[None]
    spread = exchange(packed, GROUP).reshape(groups * BLK, LANES)
    sent, pick = call(
        select_kernel,
        (
            jax.ShapeDtypeStruct((4 * total, 128), BF16),
            jax.ShapeDtypeStruct((total, groups * BLK), BF16),
        ),
        (spread, info),
        scratch_shapes=[pltpu.VMEM((4 * total, 128), F32)],
    )
    pieces = (share_x * groups, 4 * picked // share_x, 128)
    tiles = exchange(sent.reshape(pieces), OWNERS).reshape(share_x, 4 * count, 128)

    def before(d, x):
        return (lax.rem(x[0] + share_x - d, share_x), 0, 0)

    def after(d, x):
        return (lax.rem(x[0] + d, share_x), 0, 0)

    def whole(*shape):
        return pl.BlockSpec(shape, lambda *_: (0,) * len(shape))

    tile_block = (1, 4 * count, 128)
    row_block = (1, count, LANES)
    gate_block = (1, 2 * width, hid)
    act_shape = (share_y, 3 * count, hid // share_y)
    parts, rows, prob = call(
        hidden_kernel,
        (
            jax.ShapeDtypeStruct(act_shape, BF16),
            jax.ShapeDtypeStruct((share_x, count, LANES), BF16),
            jax.ShapeDtypeStruct((count, 128), F32),
        ),
        (order, tiles, mark, gates, *downs),
        VMEM_LARGE,
        grid_spec=pltpu.PrefetchScalarGridSpec(
            num_scalar_prefetch=1,
            grid=(share_x,),
            in_specs=[
                pl.BlockSpec(tile_block, before),
                whole(1, 256),
                pl.BlockSpec(gate_block, before),
            ]
            + [whole(width, hid)] * 4,
            out_specs=[whole(*act_shape), pl.BlockSpec(row_block, before), whole(count, 128)],
            scratch_shapes=[
                pltpu.VMEM((3, count, hid), F32),
                pltpu.VMEM((4 * count, 128), F32),
            ],
        ),
    )
    parts = exchange(parts, "y")
    act = call(point_kernel, jax.ShapeDtypeStruct(act_shape[1:], BF16), (parts,))
    act = lax.all_gather(act, "y", axis=0, tiled=False)
    results = call(
        result_kernel,
        jax.ShapeDtypeStruct((share_x, 4 * count, 128), BF16),
        (order, act, prob, gates, *downs),
        VMEM_LARGE,
        grid_spec=pltpu.PrefetchScalarGridSpec(
            num_scalar_prefetch=1,
            grid=(share_x,),
            in_specs=[whole(*act_shape), whole(count, 128), pl.BlockSpec(gate_block, before)]
            + [whole(width, hid)] * 4,
            out_specs=pl.BlockSpec(tile_block, before),
            scratch_shapes=[pltpu.VMEM((count, LANES), F32), pltpu.VMEM((4 * count, 128), F32)],
        ),
    )
    late_act, results = lax.optimization_barrier((act, results))
    gate_grads = call(
        gate_grad_kernel,
        jax.ShapeDtypeStruct((share_x, 2 * width, hid), BF16),
        (late_act, rows),
        VMEM_LARGE,
        grid=(share_x,),
        in_specs=[whole(*act_shape), pl.BlockSpec(row_block, lambda i: (i, 0, 0))],
        out_specs=pl.BlockSpec(gate_block, lambda i: (i, 0, 0)),
    )
    gate_grads = lax.psum_scatter(gate_grads, "x", scatter_dimension=0, tiled=False)
    down_grads = call(
        down_grad_kernel,
        (jax.ShapeDtypeStruct((width, hid), BF16),) * 4,
        (order, late_act, rows),
        grid_spec=pltpu.PrefetchScalarGridSpec(
            num_scalar_prefetch=1,
            grid=(share_x,),
            in_specs=[whole(*act_shape), pl.BlockSpec(row_block, after)],
            out_specs=[whole(width, hid)] * 4,
        ),
    )
    down_grads = [down_grads[0]] + [
        lax.ppermute(down_grads[d], "x", shifts[d]) for d in range(1, share_x)
    ]
    down_grad = call(sum_kernel, jax.ShapeDtypeStruct((width, hid), BF16), down_grads)
    back = exchange(results.reshape(pieces), OWNERS).reshape(4 * total, 128)
    summed = call(
        combine_kernel,
        jax.ShapeDtypeStruct((groups * BLK, LANES), BF16),
        (pick, back),
        scratch_shapes=[pltpu.VMEM((4 * total, 128), F32)],
    )
    home = exchange(summed.reshape(groups, BLK, LANES), GROUP).reshape(groups * BLK, LANES)
    out, dx = call(
        unpack_kernel,
        (jax.ShapeDtypeStruct((width, groups * BLK), BF16),) * 2,
        (home,),
    )
    return (
        out.T,
        dx.T,
        gate_grads[None, 0:width],
        gate_grads[None, width:],
        down_grad.T[None],
    )


def solution(mesh):
    devices = mesh.devices.reshape(8, 2, 8, 4)
    inner = Mesh(devices, ("z", "core", "y", "x"))
    member = ("y", "x")
    in_specs = (
        P(GROUP, member),
        P(GROUP, member),
        P(GROUP, None),
        P(GROUP, member, None),
        P(GROUP, member, None),
        P(GROUP, None, member),
        P(),
        P(),
        P(GROUP, None, None),
    )
    out_specs = (
        P(GROUP, member),
        P(GROUP, member),
        P(GROUP, member, None),
        P(GROUP, member, None),
        P(GROUP, None, member),
    )
    return jax.shard_map(body, mesh=inner, in_specs=in_specs, out_specs=out_specs, check_vma=False)
```

```python
import jax
import jax.numpy as jnp
from jax import lax
from jax.experimental import pallas as pl
from jax.experimental.pallas import tpu as pltpu
from jax.sharding import Mesh, PartitionSpec as P

BLK = 32
USERS = 2
LANES = 512
P_LANE = 224
DY_LANE = 256
LIST_LANE = 480
GROUP = ("z", "core")
OWNERS = ("x", "z", "core")
F32 = jnp.float32
BF16 = jnp.bfloat16
VMEM_LIMIT = 24 * 1024 * 1024
VMEM_LARGE = 56 * 1024 * 1024


def dot(a, b, ca, cb):
    return lax.dot_general(a, b, (((ca,), (cb,)), ((), ())), preferred_element_type=F32)


def call(kernel, out_shape, args, limit=VMEM_LIMIT, **kw):
    return pl.pallas_call(
        kernel,
        out_shape=out_shape,
        compiler_params=pltpu.CompilerParams(vmem_limit_bytes=limit),
        **kw,
    )(*args)


def token_permutation(rows):
    o = lax.broadcasted_iota(jnp.int32, (rows, rows), 0)
    t = lax.broadcasted_iota(jnp.int32, (rows, rows), 1)
    source = ((o >> 1) & 15) * BLK + (o >> 5) * 2 + (o & 1)
    return (t == source).astype(BF16)


def pack_kernel(tok_ref, dy_ref, prob_ref, list_ref, out_ref, all_ref):
    width = tok_ref.shape[0]
    all_ref[...] = jnp.zeros_like(all_ref)
    all_ref[0:width] = tok_ref[...]
    all_ref[P_LANE : P_LANE + 16] = prob_ref[...]
    all_ref[DY_LANE : DY_LANE + width] = dy_ref[...]
    packed = dot(token_permutation(LANES), all_ref[...], 1, 1)
    packed = packed.reshape(out_ref.shape) + list_ref[...].astype(F32)[None]
    out_ref[...] = packed.astype(BF16)


def split_lanes(tmp_ref, rows):
    count = rows.shape[0]
    for c in range(4):
        tmp_ref[pl.ds(c, count, stride=4), :] = rows[:, c * 128 : (c + 1) * 128]
    return tmp_ref[...].astype(BF16)


def join_lanes(tmp_ref, tiles):
    tmp_ref[...] = tiles.astype(F32)
    count = tmp_ref.shape[0] // 4
    return jnp.concatenate([tmp_ref[pl.ds(c, count, stride=4), :] for c in range(4)], axis=1)


def select_kernel(rows_ref, info_ref, out_ref, pick_ref, tmp_ref):
    rows = rows_ref[...]
    total = info_ref.shape[0]
    columns = lax.broadcasted_iota(jnp.int32, (total, rows.shape[0]), 1)
    list_rows = (columns == info_ref[:, 0:1]).astype(BF16)
    lists = dot(list_rows, rows[:, 384:512], 1, 0)
    lanes = lax.broadcasted_iota(jnp.int32, lists.shape, 1) + 384
    block = jnp.sum(jnp.where(lanes == info_ref[:, 2:3], lists, 0.0), axis=1, keepdims=True)
    column = info_ref[:, 1:2] + 2 * block.astype(jnp.int32)
    pick = (columns == column).astype(BF16)
    pick_ref[...] = pick
    out_ref[...] = split_lanes(tmp_ref, dot(pick, rows, 1, 0))


def hidden_kernel(x_ref, tiles_ref, mark_ref, gate_ref, *refs):
    up_refs, down_refs, refs = refs[:4], refs[4:8], refs[8:]
    row_refs, (out_ref, prob_ref, acc_ref, tmp_ref) = refs[:4], refs[4:]
    step = pl.program_id(0)
    rows = join_lanes(tmp_ref, tiles_ref[0])
    count = rows.shape[0]
    width, hid = gate_ref.shape[1:]
    prob = jnp.sum(rows[:, 0:256] * mark_ref[...], axis=1, keepdims=True)
    x = rows[:, 0:256].astype(BF16)
    grad = (prob * rows[:, DY_LANE:LANES]).astype(BF16)
    prob_ref[...] = jnp.broadcast_to(prob, prob_ref.shape)

    @pl.when(step == 0)
    def _():
        acc_ref[...] = jnp.zeros_like(acc_ref)

    acc_ref[0] += dot(x[:, 0:width], gate_ref[0], 1, 0)
    for d in range(4):

        @pl.when(step == d)
        def _():
            row_refs[d][:, 0:DY_LANE] = x
            row_refs[d][:, DY_LANE:LANES] = grad
            acc_ref[1] += dot(x[:, 0:width], up_refs[d][...], 1, 0)
            acc_ref[2] += dot(grad[:, 0:width], down_refs[d][...], 1, 0)

    @pl.when(step == pl.num_programs(0) - 1)
    def _():
        for part in range(3):
            for piece in range(hid // 128):
                out_ref[piece, part * count : (part + 1) * count] = acc_ref[
                    part, :, piece * 128 : (piece + 1) * 128
                ].astype(BF16)


def point_kernel(parts_ref, out_ref):
    count = out_ref.shape[0] // 3
    total = jnp.sum(parts_ref[...].astype(F32), axis=0)
    gate, up, grad = total[0:count], total[count : 2 * count], total[2 * count :]
    sigma = jax.nn.sigmoid(gate)
    out_ref[0:count] = (gate * sigma * up).astype(BF16)
    out_ref[count : 2 * count] = (grad * up * sigma * (1.0 + gate * (1.0 - sigma))).astype(BF16)
    out_ref[2 * count :] = (grad * gate * sigma).astype(BF16)


def hidden_parts(act):
    count = act.shape[1] // 3
    return [
        jnp.concatenate([act[k, i * count : (i + 1) * count] for k in range(act.shape[0])], axis=1)
        for i in range(3)
    ]


def result_kernel(x_ref, act_ref, prob_ref, gate_ref, *refs):
    up_refs, down_refs, (out_ref, res_ref, tmp_ref) = refs[:4], refs[4:8], refs[8:]
    step = pl.program_id(0)
    width = gate_ref.shape[1]
    hidden, gate_grad, up_grad = hidden_parts(act_ref)

    @pl.when(step == 0)
    def _():
        res_ref[...] = jnp.zeros_like(res_ref)

    dx = dot(gate_grad, gate_ref[0], 1, 1)
    for d in range(4):

        @pl.when(step == d)
        def _():
            res_ref[:, 0:width] = prob_ref[:, 0:1] * dot(hidden, down_refs[d][...], 1, 1)
            res_ref[:, DY_LANE : DY_LANE + width] = dx + dot(up_grad, up_refs[d][...], 1, 1)

    out_ref[0] = split_lanes(tmp_ref, res_ref[...])


def weight_kernel(x_ref, act_ref, *refs):
    row_refs, out_refs, acc_ref = refs[:4], refs[4:7], refs[7]
    step = pl.program_id(0)
    width = out_refs[0].shape[0]
    hidden, gate_grad, up_grad = hidden_parts(act_ref.at[0])

    @pl.when(step == 0)
    def _():
        acc_ref[...] = jnp.zeros_like(acc_ref)

    for d in range(4):

        @pl.when(step == d)
        def _():
            x = row_refs[d][:, 0:width]
            grad = row_refs[d][:, DY_LANE : DY_LANE + width]
            acc_ref[0] += dot(x, gate_grad, 0, 0)
            acc_ref[1] += dot(x, up_grad, 0, 0)
            acc_ref[2] += dot(grad, hidden, 0, 0)

    @pl.when(step == pl.num_programs(0) - 1)
    def _():
        for part in range(3):
            out_refs[part][...] = acc_ref[part].astype(BF16)


def combine_kernel(pick_ref, tiles_ref, out_ref, tmp_ref):
    rows = join_lanes(tmp_ref, tiles_ref[...]).astype(BF16)
    out_ref[...] = dot(pick_ref[...], rows, 0, 0).astype(BF16)


def unpack_kernel(rows_ref, out_ref, dx_ref):
    result = dot(rows_ref[...], token_permutation(LANES), 0, 0).astype(BF16)
    out_ref[...] = result[0:P_LANE]
    dx_ref[...] = result[DY_LANE : DY_LANE + P_LANE]


def routing_info(expert_slot, block_counts, entries, share_x):
    groups, experts = block_counts.shape
    ids = jnp.arange(experts, dtype=jnp.int32)
    slot_is = (expert_slot[:, None] == ids[None, :]).astype(jnp.int32)
    slot_expert = jnp.sum(slot_is * ids[:, None], axis=0)
    counts = jnp.sum(block_counts[:, :, None] * slot_is[None], axis=1)
    used = (counts > 0).astype(jnp.int32)
    before = (ids[:, None] < ids[None, :]).astype(jnp.int32)
    rank = jnp.sum(used[:, None, :] * before[:, :, None], axis=0)
    user_ids = jnp.arange(USERS, dtype=jnp.int32)[:, None, None]
    chosen = used[None] * (rank[None] == user_ids).astype(jnp.int32)
    user_group = jnp.sum(chosen * ids[None, :, None], axis=1)
    user_count = jnp.sum(chosen * counts[None], axis=1)
    per_x = USERS * entries * 2 // share_x
    shape = (share_x, groups, per_x)
    member = lax.broadcasted_iota(jnp.int32, shape, 0) * per_x
    member = member + lax.broadcasted_iota(jnp.int32, shape, 2)
    first = member < entries * 2
    entry = (member >> 1) - jnp.where(first, 0, entries)
    group = jnp.where(first, user_group[0][None, :, None], user_group[1][None, :, None])
    limit = jnp.where(first, user_count[0][None, :, None], user_count[1][None, :, None])
    list_row = group * BLK + slot_expert[None, :, None]
    base = jnp.where(entry < limit, group * BLK + (member & 1), -100000)
    info = jnp.stack([list_row, base, entry + LIST_LANE], axis=-1)
    return info.reshape(-1, 3)


def exchange(array, axis):
    return lax.all_to_all(array, axis, split_axis=0, concat_axis=0, tiled=True)


def body(
    tokens, grad_output, gate_prob, w_gate, w_up, w_down, expert_slot, block_counts, block_lists
):
    groups = lax.axis_size(GROUP)
    share_y = lax.axis_size("y")
    share_x = lax.axis_size("x")
    width = tokens.shape[1]
    hid = w_gate.shape[2]
    entries = block_lists.shape[2]
    picked = USERS * entries * 2
    total = groups * picked
    count = total // share_x

    me_x = lax.axis_index("x")
    order = me_x[None].astype(jnp.int32)
    shifts = [[(i, (i + d) % share_x) for i in range(share_x)] for d in range(share_x)]

    def shift(array, d):
        return lax.ppermute(array, "x", shifts[d])

    gates = lax.all_gather(w_gate[0], "x", axis=0, tiled=False)
    up, down = w_up[0], w_down[0].T
    up_right, down_left = shift(up, 1), shift(down, 3)

    lists = lax.pad(
        block_lists[0].astype(BF16),
        jnp.zeros((), BF16),
        ((0, BLK - 16, 0), (LIST_LANE, LANES - LIST_LANE - entries, 0)),
    )
    packed = call(
        pack_kernel,
        jax.ShapeDtypeStruct((groups, BLK, LANES), BF16),
        (tokens.T, grad_output.T, gate_prob.T, lists),
        VMEM_LARGE,
        scratch_shapes=[pltpu.VMEM((LANES, LANES), BF16)],
    )
    info = routing_info(expert_slot, block_counts, entries, share_x)
    mine = (expert_slot == lax.axis_index(GROUP)).astype(F32)
    mark = lax.pad(mine, jnp.zeros((), F32), ((P_LANE, 16, 0),))[None]
    spread = exchange(packed, GROUP).reshape(groups * BLK, LANES)
    spread, up_right, down_left = lax.optimization_barrier((spread, up_right, down_left))
    sent, pick = call(
        select_kernel,
        (
            jax.ShapeDtypeStruct((4 * total, 128), BF16),
            jax.ShapeDtypeStruct((total, groups * BLK), BF16),
        ),
        (spread, info),
        scratch_shapes=[pltpu.VMEM((4 * total, 128), F32)],
    )
    ups = [up, up_right, shift(up_right, 1), shift(up, 3)]
    downs = [down, shift(down, 1), shift(down_left, 3), down_left]
    pieces = (share_x * groups, 4 * picked // share_x, 128)
    tiles = exchange(sent.reshape(pieces), OWNERS).reshape(share_x, 4 * count, 128)

    def before(d, x):
        return (lax.rem(x[0] + share_x - d, share_x), 0, 0)

    def after(d, x):
        return (lax.rem(x[0] + d, share_x), 0, 0)

    def whole(*shape):
        return pl.BlockSpec(shape, lambda *_: (0,) * len(shape))

    tile_block = (1, 4 * count, 128)
    gate_block = (1, width, hid)
    act_shape = (share_y, 3 * count, hid // share_y)
    *rows, parts, prob = call(
        hidden_kernel,
        (jax.ShapeDtypeStruct((count, LANES), BF16),) * 4
        + (jax.ShapeDtypeStruct(act_shape, BF16), jax.ShapeDtypeStruct((count, 128), F32)),
        (order, tiles, mark, gates, *ups, *downs),
        VMEM_LARGE,
        grid_spec=pltpu.PrefetchScalarGridSpec(
            num_scalar_prefetch=1,
            grid=(share_x,),
            in_specs=[
                pl.BlockSpec(tile_block, before),
                whole(1, 256),
                pl.BlockSpec(gate_block, before),
            ]
            + [whole(width, hid)] * 8,
            out_specs=[whole(count, LANES)] * 4 + [whole(*act_shape), whole(count, 128)],
            scratch_shapes=[
                pltpu.VMEM((3, count, hid), F32),
                pltpu.VMEM((4 * count, 128), F32),
            ],
        ),
    )
    parts = exchange(parts, "y")
    rows = [rows[0]] + [shift(rows[d], share_x - d) for d in range(1, share_x)]
    parts, *rows = lax.optimization_barrier((parts, *rows))
    act = call(point_kernel, jax.ShapeDtypeStruct(act_shape[1:], BF16), (parts,))
    act = lax.all_gather(act, "y", axis=0, tiled=False)
    all_act = lax.all_gather(act, "x", axis=0, tiled=False)
    results = call(
        result_kernel,
        jax.ShapeDtypeStruct((share_x, 4 * count, 128), BF16),
        (order, act, prob, gates, *ups, *downs),
        VMEM_LARGE,
        grid_spec=pltpu.PrefetchScalarGridSpec(
            num_scalar_prefetch=1,
            grid=(share_x,),
            in_specs=[whole(*act_shape), whole(count, 128), pl.BlockSpec(gate_block, before)]
            + [whole(width, hid)] * 8,
            out_specs=pl.BlockSpec(tile_block, before),
            scratch_shapes=[pltpu.VMEM((count, LANES), F32), pltpu.VMEM((4 * count, 128), F32)],
        ),
    )
    weights = call(
        weight_kernel,
        (jax.ShapeDtypeStruct((width, hid), BF16),) * 3,
        (order, all_act, *rows),
        VMEM_LARGE,
        grid_spec=pltpu.PrefetchScalarGridSpec(
            num_scalar_prefetch=1,
            grid=(share_x,),
            in_specs=[pl.BlockSpec((1,) + act_shape, lambda d, x: after(d, x) + (0,))]
            + [whole(count, LANES)] * 4,
            out_specs=[whole(width, hid)] * 3,
            scratch_shapes=[pltpu.VMEM((3, width, hid), F32)],
        ),
    )
    back = exchange(results.reshape(pieces), OWNERS).reshape(4 * total, 128)
    summed = call(
        combine_kernel,
        jax.ShapeDtypeStruct((groups * BLK, LANES), BF16),
        (pick, back),
        scratch_shapes=[pltpu.VMEM((4 * total, 128), F32)],
    )
    home = exchange(summed.reshape(groups, BLK, LANES), GROUP).reshape(groups * BLK, LANES)
    out, dx = call(
        unpack_kernel,
        (jax.ShapeDtypeStruct((width, groups * BLK), BF16),) * 2,
        (home,),
    )
    return (
        out.T,
        dx.T,
        weights[0][None],
        weights[1][None],
        weights[2].T[None],
    )


def solution(mesh):
    devices = mesh.devices.reshape(8, 2, 8, 4)
    inner = Mesh(devices, ("z", "core", "y", "x"))
    member = ("y", "x")
    in_specs = (
        P(GROUP, member),
        P(GROUP, member),
        P(GROUP, None),
        P(GROUP, member, None),
        P(GROUP, member, None),
        P(GROUP, None, member),
        P(),
        P(),
        P(GROUP, None, None),
    )
    out_specs = (
        P(GROUP, member),
        P(GROUP, member),
        P(GROUP, member, None),
        P(GROUP, member, None),
        P(GROUP, None, member),
    )
    return jax.shard_map(body, mesh=inner, in_specs=in_specs, out_specs=out_specs, check_vma=False)
```

```python
import jax
import jax.numpy as jnp
from jax import lax
from jax.experimental import pallas as pl
from jax.experimental.pallas import tpu as pltpu
from jax.sharding import Mesh, PartitionSpec as P

BLK = 32
USERS = 2
LANES = 512
P_LANE = 224
DY_LANE = 256
LIST_LANE = 480
GROUP = ("z", "core")
OWNERS = ("x", "z", "core")
F32 = jnp.float32
BF16 = jnp.bfloat16
VMEM_LIMIT = 24 * 1024 * 1024
VMEM_LARGE = 56 * 1024 * 1024


def dot(a, b, ca, cb):
    return lax.dot_general(a, b, (((ca,), (cb,)), ((), ())), preferred_element_type=F32)


def call(kernel, out_shape, args, limit=VMEM_LIMIT, **kw):
    return pl.pallas_call(
        kernel,
        out_shape=out_shape,
        compiler_params=pltpu.CompilerParams(vmem_limit_bytes=limit),
        **kw,
    )(*args)


def token_permutation(rows):
    o = lax.broadcasted_iota(jnp.int32, (rows, rows), 0)
    t = lax.broadcasted_iota(jnp.int32, (rows, rows), 1)
    source = ((o >> 1) & 15) * BLK + (o >> 5) * 2 + (o & 1)
    return (t == source).astype(BF16)


def pack_kernel(tok_ref, dy_ref, prob_ref, list_ref, out_ref, all_ref):
    width = tok_ref.shape[0]
    all_ref[...] = jnp.zeros_like(all_ref)
    all_ref[0:width] = tok_ref[...]
    all_ref[P_LANE : P_LANE + 16] = prob_ref[...]
    all_ref[DY_LANE : DY_LANE + width] = dy_ref[...]
    packed = dot(token_permutation(LANES), all_ref[...], 1, 1)
    lists = list_ref[:, 0, :].astype(F32).astype(BF16)
    entry = lax.broadcasted_iota(jnp.int32, (lists.shape[0], LANES), 0)
    lane = lax.broadcasted_iota(jnp.int32, (lists.shape[0], LANES), 1)
    lists = dot(lists, (lane == entry + LIST_LANE).astype(BF16), 0, 0)
    lists = jnp.concatenate([lists, jnp.zeros((BLK - lists.shape[0], LANES), F32)], axis=0)
    out_ref[...] = (packed.reshape(out_ref.shape) + lists[None]).astype(BF16)


def split_lanes(tmp_ref, rows):
    count = rows.shape[0]
    for c in range(4):
        tmp_ref[pl.ds(c, count, stride=4), :] = rows[:, c * 128 : (c + 1) * 128]
    return tmp_ref[...].astype(BF16)


def join_lanes(tmp_ref, tiles):
    tmp_ref[...] = tiles.astype(F32)
    count = tmp_ref.shape[0] // 4
    return jnp.concatenate([tmp_ref[pl.ds(c, count, stride=4), :] for c in range(4)], axis=1)


def select_kernel(rows_ref, info_ref, out_ref, pick_ref, tmp_ref):
    rows = rows_ref[...]
    total = info_ref.shape[0]
    columns = lax.broadcasted_iota(jnp.int32, (total, rows.shape[0]), 1)
    list_rows = (columns == info_ref[:, 0:1]).astype(BF16)
    lists = dot(list_rows, rows[:, 384:512], 1, 0)
    lanes = lax.broadcasted_iota(jnp.int32, lists.shape, 1) + 384
    block = jnp.sum(jnp.where(lanes == info_ref[:, 2:3], lists, 0.0), axis=1, keepdims=True)
    column = info_ref[:, 1:2] + 2 * block.astype(jnp.int32)
    pick = (columns == column).astype(BF16)
    pick_ref[...] = pick
    out_ref[...] = split_lanes(tmp_ref, dot(pick, rows, 1, 0))


def hidden_kernel(x_ref, tiles_ref, mark_ref, gate_ref, *refs):
    up_refs, down_refs, refs = refs[:4], refs[4:8], refs[8:]
    row_refs, (out_ref, prob_ref, acc_ref, tmp_ref) = refs[:4], refs[4:]
    step = pl.program_id(0)
    rows = join_lanes(tmp_ref, tiles_ref[0])
    count = rows.shape[0]
    width, hid = gate_ref.shape[1:]
    prob = jnp.sum(rows[:, 0:256] * mark_ref[...], axis=1, keepdims=True)
    x = rows[:, 0:256].astype(BF16)
    grad = (prob * rows[:, DY_LANE:LANES]).astype(BF16)
    prob_ref[...] = jnp.broadcast_to(prob, prob_ref.shape)

    @pl.when(step == 0)
    def _():
        acc_ref[...] = jnp.zeros_like(acc_ref)

    acc_ref[0] += dot(x[:, 0:width], gate_ref[0], 1, 0)
    for d in range(4):

        @pl.when(step == d)
        def _():
            row_refs[d][:, 0:DY_LANE] = x
            row_refs[d][:, DY_LANE:LANES] = grad
            acc_ref[1] += dot(x[:, 0:width], up_refs[d][...], 1, 0)
            acc_ref[2] += dot(grad[:, 0:width], down_refs[d][...], 1, 0)

    @pl.when(step == pl.num_programs(0) - 1)
    def _():
        for part in range(3):
            for piece in range(hid // 128):
                out_ref[piece, part * count : (part + 1) * count] = acc_ref[
                    part, :, piece * 128 : (piece + 1) * 128
                ].astype(BF16)


def point_kernel(parts_ref, out_ref):
    count = out_ref.shape[0] // 3
    total = jnp.sum(parts_ref[...].astype(F32), axis=0)
    gate, up, grad = total[0:count], total[count : 2 * count], total[2 * count :]
    sigma = jax.nn.sigmoid(gate)
    out_ref[0:count] = (gate * sigma * up).astype(BF16)
    out_ref[count : 2 * count] = (grad * up * sigma * (1.0 + gate * (1.0 - sigma))).astype(BF16)
    out_ref[2 * count :] = (grad * gate * sigma).astype(BF16)


def hidden_parts(act, parts):
    count = act.shape[1] // parts
    return [
        jnp.concatenate([act[k, i * count : (i + 1) * count] for k in range(act.shape[0])], axis=1)
        for i in range(parts)
    ]


def result_kernel(x_ref, act_ref, prob_ref, gate_ref, *refs):
    up_refs, down_refs, (out_ref, res_ref, tmp_ref) = refs[:4], refs[4:8], refs[8:]
    step = pl.program_id(0)
    width = gate_ref.shape[1]
    hidden, gate_grad, up_grad = hidden_parts(act_ref, 3)

    @pl.when(step == 0)
    def _():
        res_ref[...] = jnp.zeros_like(res_ref)

    dx = dot(gate_grad, gate_ref[0], 1, 1)
    for d in range(4):

        @pl.when(step == d)
        def _():
            res_ref[:, 0:width] = prob_ref[:, 0:1] * dot(hidden, down_refs[d][...], 1, 1)
            res_ref[:, DY_LANE : DY_LANE + width] = dx + dot(up_grad, up_refs[d][...], 1, 1)

    out_ref[0] = split_lanes(tmp_ref, res_ref[...])


def gate_grad_kernel(x_ref, act_ref, *refs):
    row_refs, out_refs, acc_ref = refs[:4], refs[4:6], refs[6]
    step = pl.program_id(0)
    width = out_refs[0].shape[0]
    grads = hidden_parts(act_ref.at[0], 2)

    @pl.when(step == 0)
    def _():
        acc_ref[...] = jnp.zeros_like(acc_ref)

    for d in range(4):

        @pl.when(step == d)
        def _():
            x = row_refs[d][:, 0:width]
            for part in range(2):
                acc_ref[part] += dot(x, grads[part], 0, 0)

    @pl.when(step == pl.num_programs(0) - 1)
    def _():
        for part in range(2):
            out_refs[part][...] = acc_ref[part].astype(BF16)


def down_grad_kernel(*refs):
    act_refs, row_refs, out_ref = refs[:4], refs[4:8], refs[8]
    width = out_ref.shape[0]
    total = 0.0
    for d in range(4):
        grad = row_refs[d][:, DY_LANE : DY_LANE + width]
        total += dot(grad, hidden_parts(act_refs[d], 1)[0], 0, 0)
    out_ref[...] = total.astype(BF16)


def combine_kernel(pick_ref, tiles_ref, out_ref, tmp_ref):
    rows = join_lanes(tmp_ref, tiles_ref[...]).astype(BF16)
    out_ref[...] = dot(pick_ref[...], rows, 0, 0).astype(BF16)


def unpack_kernel(rows_ref, out_ref, dx_ref):
    result = dot(rows_ref[...], token_permutation(LANES), 0, 0).astype(BF16)
    out_ref[...] = result[0:P_LANE]
    dx_ref[...] = result[DY_LANE : DY_LANE + P_LANE]


def routing_info(expert_slot, block_counts, entries, share_x):
    groups, experts = block_counts.shape
    ids = jnp.arange(experts, dtype=jnp.int32)
    slot_is = (expert_slot[:, None] == ids[None, :]).astype(jnp.int32)
    slot_expert = jnp.sum(slot_is * ids[:, None], axis=0)
    counts = jnp.sum(block_counts[:, :, None] * slot_is[None], axis=1)
    used = (counts > 0).astype(jnp.int32)
    before = (ids[:, None] < ids[None, :]).astype(jnp.int32)
    rank = jnp.sum(used[:, None, :] * before[:, :, None], axis=0)
    user_ids = jnp.arange(USERS, dtype=jnp.int32)[:, None, None]
    chosen = used[None] * (rank[None] == user_ids).astype(jnp.int32)
    user_group = jnp.sum(chosen * ids[None, :, None], axis=1)
    user_count = jnp.sum(chosen * counts[None], axis=1)
    per_x = USERS * entries * 2 // share_x
    shape = (share_x, groups, per_x)
    member = lax.broadcasted_iota(jnp.int32, shape, 0) * per_x
    member = member + lax.broadcasted_iota(jnp.int32, shape, 2)
    first = member < entries * 2
    entry = (member >> 1) - jnp.where(first, 0, entries)
    group = jnp.where(first, user_group[0][None, :, None], user_group[1][None, :, None])
    limit = jnp.where(first, user_count[0][None, :, None], user_count[1][None, :, None])
    list_row = group * BLK + slot_expert[None, :, None]
    base = jnp.where(entry < limit, group * BLK + (member & 1), -100000)
    info = jnp.stack([list_row, base, entry + LIST_LANE], axis=-1)
    return info.reshape(-1, 3)


def exchange(array, axis):
    return lax.all_to_all(array, axis, split_axis=0, concat_axis=0, tiled=True)


def body(
    tokens, grad_output, gate_prob, w_gate, w_up, w_down, expert_slot, block_counts, block_lists
):
    groups = lax.axis_size(GROUP)
    share_y = lax.axis_size("y")
    share_x = lax.axis_size("x")
    width = tokens.shape[1]
    hid = w_gate.shape[2]
    entries = block_lists.shape[2]
    picked = USERS * entries * 2
    total = groups * picked
    count = total // share_x

    me_x = lax.axis_index("x")
    order = me_x[None].astype(jnp.int32)
    shifts = [[(i, (i + d) % share_x) for i in range(share_x)] for d in range(share_x)]

    def shift(array, d):
        return lax.ppermute(array, "x", shifts[d])

    gates = lax.all_gather(w_gate[0], "x", axis=0, tiled=False)
    up, down = w_up[0], w_down[0].T
    packed = call(
        pack_kernel,
        jax.ShapeDtypeStruct((groups, BLK, LANES), BF16),
        (tokens.T, grad_output.T, gate_prob.T, block_lists.transpose(2, 0, 1)),
        VMEM_LARGE,
        scratch_shapes=[pltpu.VMEM((LANES, LANES), BF16)],
    )
    info = routing_info(expert_slot, block_counts, entries, share_x)
    mine = (expert_slot == lax.axis_index(GROUP)).astype(F32)
    mark = lax.pad(mine, jnp.zeros((), F32), ((P_LANE, 16, 0),))[None]
    spread = exchange(packed, GROUP).reshape(groups * BLK, LANES)
    info, up_late, down_late = lax.optimization_barrier((info, up, down))
    up_right, down_left = shift(up_late, 1), shift(down_late, 3)
    down_right, up_left = shift(down_late, 1), shift(up_late, 3)
    spread, up_right, down_left = lax.optimization_barrier((spread, up_right, down_left))
    sent, pick = call(
        select_kernel,
        (
            jax.ShapeDtypeStruct((4 * total, 128), BF16),
            jax.ShapeDtypeStruct((total, groups * BLK), BF16),
        ),
        (spread, info),
        scratch_shapes=[pltpu.VMEM((4 * total, 128), F32)],
    )
    sent, down_right, up_left = lax.optimization_barrier((sent, down_right, up_left))
    ups = [up, up_right, shift(up_right, 1), up_left]
    downs = [down, down_right, shift(down_left, 3), down_left]
    pieces = (share_x * groups, 4 * picked // share_x, 128)
    tiles = exchange(sent.reshape(pieces), OWNERS).reshape(share_x, 4 * count, 128)

    def before(d, x):
        return (lax.rem(x[0] + share_x - d, share_x), 0, 0)

    def after(d, x):
        return (lax.rem(x[0] + d, share_x), 0, 0)

    def whole(*shape):
        return pl.BlockSpec(shape, lambda *_: (0,) * len(shape))

    tile_block = (1, 4 * count, 128)
    gate_block = (1, width, hid)
    act_shape = (share_y, 3 * count, hid // share_y)
    *rows, parts, prob = call(
        hidden_kernel,
        (jax.ShapeDtypeStruct((count, LANES), BF16),) * 4
        + (jax.ShapeDtypeStruct(act_shape, BF16), jax.ShapeDtypeStruct((count, 128), F32)),
        (order, tiles, mark, gates, *ups, *downs),
        VMEM_LARGE,
        grid_spec=pltpu.PrefetchScalarGridSpec(
            num_scalar_prefetch=1,
            grid=(share_x,),
            in_specs=[
                pl.BlockSpec(tile_block, before),
                whole(1, 256),
                pl.BlockSpec(gate_block, before),
            ]
            + [whole(width, hid)] * 8,
            out_specs=[whole(count, LANES)] * 4 + [whole(*act_shape), whole(count, 128)],
            scratch_shapes=[
                pltpu.VMEM((3, count, hid), F32),
                pltpu.VMEM((4 * count, 128), F32),
            ],
        ),
    )
    parts = exchange(parts, "y")
    rows = [rows[0]] + [shift(rows[d], share_x - d) for d in range(1, share_x)]
    parts, *rows = lax.optimization_barrier((parts, *rows))
    act = call(point_kernel, jax.ShapeDtypeStruct(act_shape[1:], BF16), (parts,))
    act = lax.all_gather(act, "y", axis=0, tiled=False)
    grads = lax.all_gather(act[:, count:], "x", axis=0, tiled=False)
    results = call(
        result_kernel,
        jax.ShapeDtypeStruct((share_x, 4 * count, 128), BF16),
        (order, act, prob, gates, *ups, *downs),
        VMEM_LARGE,
        grid_spec=pltpu.PrefetchScalarGridSpec(
            num_scalar_prefetch=1,
            grid=(share_x,),
            in_specs=[whole(*act_shape), whole(count, 128), pl.BlockSpec(gate_block, before)]
            + [whole(width, hid)] * 8,
            out_specs=pl.BlockSpec(tile_block, before),
            scratch_shapes=[pltpu.VMEM((count, LANES), F32), pltpu.VMEM((4 * count, 128), F32)],
        ),
    )
    back = exchange(results.reshape(pieces), OWNERS).reshape(4 * total, 128)
    own = act[:, 0:count]
    hidden = [own] + [shift(own, share_x - d) for d in range(1, share_x)]
    back, *hidden = lax.optimization_barrier((back, *hidden))
    down_grad = call(down_grad_kernel, jax.ShapeDtypeStruct((width, hid), BF16), (*hidden, *rows))
    grad_block = (1, share_y, 2 * count, hid // share_y)
    gate_grad, up_grad = call(
        gate_grad_kernel,
        (jax.ShapeDtypeStruct((width, hid), BF16),) * 2,
        (order, grads, *rows),
        VMEM_LARGE,
        grid_spec=pltpu.PrefetchScalarGridSpec(
            num_scalar_prefetch=1,
            grid=(share_x,),
            in_specs=[pl.BlockSpec(grad_block, lambda d, x: after(d, x) + (0,))]
            + [whole(count, LANES)] * 4,
            out_specs=[whole(width, hid)] * 2,
            scratch_shapes=[pltpu.VMEM((2, width, hid), F32)],
        ),
    )
    summed = call(
        combine_kernel,
        jax.ShapeDtypeStruct((groups * BLK, LANES), BF16),
        (pick, back),
        scratch_shapes=[pltpu.VMEM((4 * total, 128), F32)],
    )
    home = exchange(summed.reshape(groups, BLK, LANES), GROUP).reshape(groups * BLK, LANES)
    home, gate_grad, up_grad, down_grad = lax.optimization_barrier(
        (home, gate_grad, up_grad, down_grad)
    )
    out, dx = call(
        unpack_kernel,
        (jax.ShapeDtypeStruct((width, groups * BLK), BF16),) * 2,
        (home,),
    )
    return (
        out.T,
        dx.T,
        gate_grad[None],
        up_grad[None],
        down_grad.T[None],
    )


def solution(mesh):
    devices = mesh.devices.reshape(8, 2, 8, 4)
    inner = Mesh(devices, ("z", "core", "y", "x"))
    member = ("y", "x")
    in_specs = (
        P(GROUP, member),
        P(GROUP, member),
        P(GROUP, None),
        P(GROUP, member, None),
        P(GROUP, member, None),
        P(GROUP, None, member),
        P(),
        P(),
        P(GROUP, None, None),
    )
    out_specs = (
        P(GROUP, member),
        P(GROUP, member),
        P(GROUP, member, None),
        P(GROUP, member, None),
        P(GROUP, None, member),
    )
    return jax.shard_map(body, mesh=inner, in_specs=in_specs, out_specs=out_specs, check_vma=False)
```

```python
import jax
import jax.numpy as jnp
from jax import lax
from jax.experimental import pallas as pl
from jax.experimental.pallas import tpu as pltpu
from jax.sharding import Mesh, PartitionSpec as P

BLK = 32
USERS = 2
LANES = 512
P_LANE = 224
DY_LANE = 256
LIST_LANE = 480
GROUP = ("z", "core")
OWNERS = ("x", "z", "core")
F32 = jnp.float32
BF16 = jnp.bfloat16
VMEM_LIMIT = 24 * 1024 * 1024
VMEM_LARGE = 56 * 1024 * 1024


def dot(a, b, ca, cb):
    return lax.dot_general(a, b, (((ca,), (cb,)), ((), ())), preferred_element_type=F32)


def call(kernel, out_shape, args, limit=VMEM_LIMIT, **kw):
    return pl.pallas_call(
        kernel,
        out_shape=out_shape,
        compiler_params=pltpu.CompilerParams(vmem_limit_bytes=limit),
        **kw,
    )(*args)


def token_permutation(rows):
    o = lax.broadcasted_iota(jnp.int32, (rows, rows), 0)
    t = lax.broadcasted_iota(jnp.int32, (rows, rows), 1)
    source = ((o >> 1) & 15) * BLK + (o >> 5) * 2 + (o & 1)
    return (t == source).astype(BF16)


def pack_kernel(tok_ref, dy_ref, prob_ref, list_ref, out_ref, all_ref):
    width = tok_ref.shape[0]
    all_ref[...] = jnp.zeros_like(all_ref)
    all_ref[0:width] = tok_ref[...]
    all_ref[P_LANE : P_LANE + 16] = prob_ref[...]
    all_ref[DY_LANE : DY_LANE + width] = dy_ref[...]
    packed = dot(token_permutation(LANES), all_ref[...], 1, 1)
    lists = list_ref[:, 0, :].astype(F32).astype(BF16)
    entry = lax.broadcasted_iota(jnp.int32, (lists.shape[0], LANES), 0)
    lane = lax.broadcasted_iota(jnp.int32, (lists.shape[0], LANES), 1)
    lists = dot(lists, (lane == entry + LIST_LANE).astype(BF16), 0, 0)
    lists = jnp.concatenate([lists, jnp.zeros((BLK - lists.shape[0], LANES), F32)], axis=0)
    out_ref[...] = (packed.reshape(out_ref.shape) + lists[None]).astype(BF16)


def split_lanes(tmp_ref, rows):
    count = rows.shape[0]
    for c in range(4):
        tmp_ref[pl.ds(c, count, stride=4), :] = rows[:, c * 128 : (c + 1) * 128]
    return tmp_ref[...].astype(BF16)


def join_lanes(tmp_ref, tiles):
    tmp_ref[...] = tiles.astype(F32)
    count = tmp_ref.shape[0] // 4
    return jnp.concatenate([tmp_ref[pl.ds(c, count, stride=4), :] for c in range(4)], axis=1)


def select_kernel(rows_ref, info_ref, out_ref, pick_ref, tmp_ref):
    rows = rows_ref[...]
    total = info_ref.shape[0]
    columns = lax.broadcasted_iota(jnp.int32, (total, rows.shape[0]), 1)
    list_rows = (columns == info_ref[:, 0:1]).astype(BF16)
    lists = dot(list_rows, rows[:, 384:512], 1, 0)
    lanes = lax.broadcasted_iota(jnp.int32, lists.shape, 1) + 384
    block = jnp.sum(jnp.where(lanes == info_ref[:, 2:3], lists, 0.0), axis=1, keepdims=True)
    column = info_ref[:, 1:2] + 2 * block.astype(jnp.int32)
    pick = (columns == column).astype(BF16)
    pick_ref[...] = pick
    out_ref[...] = split_lanes(tmp_ref, dot(pick, rows, 1, 0))


def store_parts(out_ref, acc_ref):
    parts, count = acc_ref.shape[:2]
    for part in range(parts):
        for piece in range(out_ref.shape[0]):
            out_ref[piece, part * count : (part + 1) * count] = acc_ref[
                part, :, piece * 128 : (piece + 1) * 128
            ].astype(BF16)


def gate_kernel(x_ref, tiles_ref, mark_ref, gate_ref, *refs):
    row_refs, (out_ref, prob_ref, acc_ref, tmp_ref) = refs[:4], refs[4:]
    step = pl.program_id(0)
    rows = join_lanes(tmp_ref, tiles_ref[0])
    width = gate_ref.shape[1] // 2
    prob = jnp.sum(rows[:, 0:256] * mark_ref[...], axis=1, keepdims=True)
    x = rows[:, 0:256].astype(BF16)
    grad = (prob * rows[:, DY_LANE:LANES]).astype(BF16)
    prob_ref[...] = jnp.broadcast_to(prob, prob_ref.shape)
    for d in range(4):

        @pl.when(step == d)
        def _():
            row_refs[d][:, 0:DY_LANE] = x
            row_refs[d][:, DY_LANE:LANES] = grad

    @pl.when(step == 0)
    def _():
        acc_ref[...] = jnp.zeros_like(acc_ref)

    acc_ref[0] += dot(x[:, 0:width], gate_ref[0, 0:width], 1, 0)
    acc_ref[1] += dot(x[:, 0:width], gate_ref[0, width : 2 * width], 1, 0)

    @pl.when(step == pl.num_programs(0) - 1)
    def _():
        store_parts(out_ref, acc_ref)


def hidden_grad_kernel(x_ref, down_ref, *refs):
    row_refs, (out_ref, acc_ref) = refs[:4], refs[4:]
    step = pl.program_id(0)
    width = down_ref.shape[1]

    @pl.when(step == 0)
    def _():
        acc_ref[...] = jnp.zeros_like(acc_ref)

    for d in range(4):

        @pl.when(step == d)
        def _():
            grad = row_refs[d][:, DY_LANE : DY_LANE + width]
            acc_ref[0] += dot(grad, down_ref[0], 1, 0)

    @pl.when(step == pl.num_programs(0) - 1)
    def _():
        store_parts(out_ref, acc_ref)


def point_kernel(parts_ref, grads_ref, out_ref):
    count = out_ref.shape[0] // 3
    total = jnp.sum(parts_ref[...].astype(F32), axis=0)
    grad = jnp.sum(grads_ref[...].astype(F32), axis=0)
    gate, up = total[0:count], total[count : 2 * count]
    sigma = jax.nn.sigmoid(gate)
    out_ref[0:count] = (gate * sigma * up).astype(BF16)
    out_ref[count : 2 * count] = (grad * up * sigma * (1.0 + gate * (1.0 - sigma))).astype(BF16)
    out_ref[2 * count :] = (grad * gate * sigma).astype(BF16)


def hidden_parts(act):
    count = act.shape[1] // 3
    return [
        jnp.concatenate([act[k, i * count : (i + 1) * count] for k in range(act.shape[0])], axis=1)
        for i in range(3)
    ]


def result_kernel(x_ref, act_ref, prob_ref, gate_ref, down_ref, out_ref, res_ref, tmp_ref):
    width = down_ref.shape[1]
    hidden, gate_grad, up_grad = hidden_parts(act_ref)

    @pl.when(pl.program_id(0) == 0)
    def _():
        res_ref[...] = jnp.zeros_like(res_ref)

    res_ref[:, 0:width] = prob_ref[:, 0:1] * dot(hidden, down_ref[0], 1, 1)
    dx = dot(gate_grad, gate_ref[0, 0:width], 1, 1)
    dx += dot(up_grad, gate_ref[0, width : 2 * width], 1, 1)
    res_ref[:, DY_LANE : DY_LANE + width] = dx
    out_ref[0] = split_lanes(tmp_ref, res_ref[...])


def weight_kernel(x_ref, act_ref, *refs):
    row_refs, out_refs, acc_ref = refs[:4], refs[4:7], refs[7]
    step = pl.program_id(0)
    width = out_refs[0].shape[0]
    hidden, gate_grad, up_grad = hidden_parts(act_ref.at[0])

    @pl.when(step == 0)
    def _():
        acc_ref[...] = jnp.zeros_like(acc_ref)

    for d in range(4):

        @pl.when(step == d)
        def _():
            x = row_refs[d][:, 0:width]
            grad = row_refs[d][:, DY_LANE : DY_LANE + width]
            acc_ref[0] += dot(x, gate_grad, 0, 0)
            acc_ref[1] += dot(x, up_grad, 0, 0)
            acc_ref[2] += dot(grad, hidden, 0, 0)

    @pl.when(step == pl.num_programs(0) - 1)
    def _():
        for part in range(3):
            out_refs[part][...] = acc_ref[part].astype(BF16)


def combine_kernel(pick_ref, tiles_ref, out_ref, tmp_ref):
    rows = join_lanes(tmp_ref, tiles_ref[...]).astype(BF16)
    out_ref[...] = dot(pick_ref[...], rows, 0, 0).astype(BF16)


def unpack_kernel(rows_ref, out_ref, dx_ref):
    result = dot(rows_ref[...], token_permutation(LANES), 0, 0).astype(BF16)
    out_ref[...] = result[0:P_LANE]
    dx_ref[...] = result[DY_LANE : DY_LANE + P_LANE]


def routing_info(expert_slot, block_counts, entries, share_x):
    groups, experts = block_counts.shape
    ids = jnp.arange(experts, dtype=jnp.int32)
    slot_is = (expert_slot[:, None] == ids[None, :]).astype(jnp.int32)
    slot_expert = jnp.sum(slot_is * ids[:, None], axis=0)
    counts = jnp.sum(block_counts[:, :, None] * slot_is[None], axis=1)
    used = (counts > 0).astype(jnp.int32)
    before = (ids[:, None] < ids[None, :]).astype(jnp.int32)
    rank = jnp.sum(used[:, None, :] * before[:, :, None], axis=0)
    user_ids = jnp.arange(USERS, dtype=jnp.int32)[:, None, None]
    chosen = used[None] * (rank[None] == user_ids).astype(jnp.int32)
    user_group = jnp.sum(chosen * ids[None, :, None], axis=1)
    user_count = jnp.sum(chosen * counts[None], axis=1)
    per_x = USERS * entries * 2 // share_x
    shape = (share_x, groups, per_x)
    member = lax.broadcasted_iota(jnp.int32, shape, 0) * per_x
    member = member + lax.broadcasted_iota(jnp.int32, shape, 2)
    first = member < entries * 2
    entry = (member >> 1) - jnp.where(first, 0, entries)
    group = jnp.where(first, user_group[0][None, :, None], user_group[1][None, :, None])
    limit = jnp.where(first, user_count[0][None, :, None], user_count[1][None, :, None])
    list_row = group * BLK + slot_expert[None, :, None]
    base = jnp.where(entry < limit, group * BLK + (member & 1), -100000)
    info = jnp.stack([list_row, base, entry + LIST_LANE], axis=-1)
    return info.reshape(-1, 3)


def exchange(array, axis):
    return lax.all_to_all(array, axis, split_axis=0, concat_axis=0, tiled=True)


def body(
    tokens, grad_output, gate_prob, w_gate, w_up, w_down, expert_slot, block_counts, block_lists
):
    groups = lax.axis_size(GROUP)
    share_y = lax.axis_size("y")
    share_x = lax.axis_size("x")
    width = tokens.shape[1]
    hid = w_gate.shape[2]
    entries = block_lists.shape[2]
    picked = USERS * entries * 2
    total = groups * picked
    count = total // share_x

    me_x = lax.axis_index("x")
    order = me_x[None].astype(jnp.int32)
    shifts = [[(i, (i + d) % share_x) for i in range(share_x)] for d in range(share_x)]

    def shift(array, d):
        return lax.ppermute(array, "x", shifts[d])

    gates = jnp.concatenate([w_gate[0], w_up[0]], axis=0)
    gates = lax.all_gather(gates, "x", axis=0, tiled=False)

    packed = call(
        pack_kernel,
        jax.ShapeDtypeStruct((groups, BLK, LANES), BF16),
        (tokens.T, grad_output.T, gate_prob.T, block_lists.transpose(2, 0, 1)),
        VMEM_LARGE,
        scratch_shapes=[pltpu.VMEM((LANES, LANES), BF16)],
    )
    info = routing_info(expert_slot, block_counts, entries, share_x)
    mine = (expert_slot == lax.axis_index(GROUP)).astype(F32)
    mark = lax.pad(mine, jnp.zeros((), F32), ((P_LANE, 16, 0),))[None]
    spread = exchange(packed, GROUP).reshape(groups * BLK, LANES)
    spread, info, down = lax.optimization_barrier((spread, info, w_down[0].T))
    downs = lax.all_gather(down, "x", axis=0, tiled=False)
    sent, pick = call(
        select_kernel,
        (
            jax.ShapeDtypeStruct((4 * total, 128), BF16),
            jax.ShapeDtypeStruct((total, groups * BLK), BF16),
        ),
        (spread, info),
        scratch_shapes=[pltpu.VMEM((4 * total, 128), F32)],
    )
    pieces = (share_x * groups, 4 * picked // share_x, 128)
    tiles = exchange(sent.reshape(pieces), OWNERS).reshape(share_x, 4 * count, 128)

    def before(d, x):
        return (lax.rem(x[0] + share_x - d, share_x), 0, 0)

    def after(d, x):
        return (lax.rem(x[0] + d, share_x), 0, 0)

    def whole(*shape):
        return pl.BlockSpec(shape, lambda *_: (0,) * len(shape))

    tile_block = (1, 4 * count, 128)
    gate_block = (1, 2 * width, hid)
    down_block = (1, width, hid)
    act_shape = (share_y, 3 * count, hid // share_y)
    gate_shape = (share_y, 2 * count, hid // share_y)
    grad_shape = (share_y, count, hid // share_y)
    *rows, parts, prob = call(
        gate_kernel,
        (jax.ShapeDtypeStruct((count, LANES), BF16),) * 4
        + (jax.ShapeDtypeStruct(gate_shape, BF16), jax.ShapeDtypeStruct((count, 128), F32)),
        (order, tiles, mark, gates),
        VMEM_LARGE,
        grid_spec=pltpu.PrefetchScalarGridSpec(
            num_scalar_prefetch=1,
            grid=(share_x,),
            in_specs=[
                pl.BlockSpec(tile_block, before),
                whole(1, 256),
                pl.BlockSpec(gate_block, before),
            ],
            out_specs=[whole(count, LANES)] * 4 + [whole(*gate_shape), whole(count, 128)],
            scratch_shapes=[
                pltpu.VMEM((2, count, hid), F32),
                pltpu.VMEM((4 * count, 128), F32),
            ],
        ),
    )
    parts = exchange(parts, "y")
    grad_parts = call(
        hidden_grad_kernel,
        jax.ShapeDtypeStruct(grad_shape, BF16),
        (order, downs, *rows),
        VMEM_LARGE,
        grid_spec=pltpu.PrefetchScalarGridSpec(
            num_scalar_prefetch=1,
            grid=(share_x,),
            in_specs=[pl.BlockSpec(down_block, before)] + [whole(count, LANES)] * 4,
            out_specs=whole(*grad_shape),
            scratch_shapes=[pltpu.VMEM((1, count, hid), F32)],
        ),
    )
    parts, grad_parts = lax.optimization_barrier((parts, grad_parts))
    grad_parts = exchange(grad_parts, "y")
    rows = [rows[0]] + [shift(rows[d], share_x - d) for d in range(1, share_x)]
    parts, grad_parts, *rows = lax.optimization_barrier((parts, grad_parts, *rows))
    act = call(
        point_kernel, jax.ShapeDtypeStruct(act_shape[1:], BF16), (parts, grad_parts)
    )
    act = lax.all_gather(act, "y", axis=0, tiled=False)
    all_act = lax.all_gather(act, "x", axis=0, tiled=False)
    results = call(
        result_kernel,
        jax.ShapeDtypeStruct((share_x, 4 * count, 128), BF16),
        (order, act, prob, gates, downs),
        VMEM_LARGE,
        grid_spec=pltpu.PrefetchScalarGridSpec(
            num_scalar_prefetch=1,
            grid=(share_x,),
            in_specs=[
                whole(*act_shape),
                whole(count, 128),
                pl.BlockSpec(gate_block, before),
                pl.BlockSpec(down_block, before),
            ],
            out_specs=pl.BlockSpec(tile_block, before),
            scratch_shapes=[pltpu.VMEM((count, LANES), F32), pltpu.VMEM((4 * count, 128), F32)],
        ),
    )
    weights = call(
        weight_kernel,
        (jax.ShapeDtypeStruct((width, hid), BF16),) * 3,
        (order, all_act, *rows),
        VMEM_LARGE,
        grid_spec=pltpu.PrefetchScalarGridSpec(
            num_scalar_prefetch=1,
            grid=(share_x,),
            in_specs=[pl.BlockSpec((1,) + act_shape, lambda d, x: after(d, x) + (0,))]
            + [whole(count, LANES)] * 4,
            out_specs=[whole(width, hid)] * 3,
            scratch_shapes=[pltpu.VMEM((3, width, hid), F32)],
        ),
    )
    back = exchange(results.reshape(pieces), OWNERS).reshape(4 * total, 128)
    summed = call(
        combine_kernel,
        jax.ShapeDtypeStruct((groups * BLK, LANES), BF16),
        (pick, back),
        scratch_shapes=[pltpu.VMEM((4 * total, 128), F32)],
    )
    home = exchange(summed.reshape(groups, BLK, LANES), GROUP).reshape(groups * BLK, LANES)
    out, dx = call(
        unpack_kernel,
        (jax.ShapeDtypeStruct((width, groups * BLK), BF16),) * 2,
        (home,),
    )
    return (
        out.T,
        dx.T,
        weights[0][None],
        weights[1][None],
        weights[2].T[None],
    )


def solution(mesh):
    devices = mesh.devices.reshape(8, 2, 8, 4)
    inner = Mesh(devices, ("z", "core", "y", "x"))
    member = ("y", "x")
    in_specs = (
        P(GROUP, member),
        P(GROUP, member),
        P(GROUP, None),
        P(GROUP, member, None),
        P(GROUP, member, None),
        P(GROUP, None, member),
        P(),
        P(),
        P(GROUP, None, None),
    )
    out_specs = (
        P(GROUP, member),
        P(GROUP, member),
        P(GROUP, member, None),
        P(GROUP, member, None),
        P(GROUP, None, member),
    )
    return jax.shard_map(body, mesh=inner, in_specs=in_specs, out_specs=out_specs, check_vma=False)
```

```python
import jax
import jax.numpy as jnp
from jax import lax
from jax.experimental import pallas as pl
from jax.experimental.pallas import tpu as pltpu
from jax.sharding import Mesh, PartitionSpec as P

BLK = 32
USERS = 2
LANES = 512
STEPS = (0, 3, 1, 2)
P_LANE = 224
DY_LANE = 256
LIST_LANE = 480
GROUP = ("z", "core")
OWNERS = ("x", "z", "core")
F32 = jnp.float32
BF16 = jnp.bfloat16
VMEM_LIMIT = 24 * 1024 * 1024
VMEM_LARGE = 56 * 1024 * 1024


def dot(a, b, ca, cb):
    return lax.dot_general(a, b, (((ca,), (cb,)), ((), ())), preferred_element_type=F32)


def call(kernel, out_shape, args, limit=VMEM_LIMIT, **kw):
    return pl.pallas_call(
        kernel,
        out_shape=out_shape,
        compiler_params=pltpu.CompilerParams(vmem_limit_bytes=limit),
        **kw,
    )(*args)


def token_permutation(rows):
    o = lax.broadcasted_iota(jnp.int32, (rows, rows), 0)
    t = lax.broadcasted_iota(jnp.int32, (rows, rows), 1)
    source = ((o >> 1) & 15) * BLK + (o >> 5) * 2 + (o & 1)
    return (t == source).astype(BF16)


def pack_kernel(tok_ref, dy_ref, prob_ref, list_ref, out_ref, all_ref):
    width = tok_ref.shape[0]
    all_ref[...] = jnp.zeros_like(all_ref)
    all_ref[0:width] = tok_ref[...]
    all_ref[P_LANE : P_LANE + 16] = prob_ref[...]
    all_ref[DY_LANE : DY_LANE + width] = dy_ref[...]
    packed = dot(token_permutation(LANES), all_ref[...], 1, 1)
    lists = list_ref[:, 0, :].astype(F32).astype(BF16)
    entry = lax.broadcasted_iota(jnp.int32, (lists.shape[0], LANES), 0)
    lane = lax.broadcasted_iota(jnp.int32, (lists.shape[0], LANES), 1)
    lists = dot(lists, (lane == entry + LIST_LANE).astype(BF16), 0, 0)
    lists = jnp.concatenate([lists, jnp.zeros((BLK - lists.shape[0], LANES), F32)], axis=0)
    out_ref[...] = (packed.reshape(out_ref.shape) + lists[None]).astype(BF16)


def split_lanes(tmp_ref, rows):
    count = rows.shape[0]
    for c in range(4):
        tmp_ref[pl.ds(c, count, stride=4), :] = rows[:, c * 128 : (c + 1) * 128]
    return tmp_ref[...].astype(BF16)


def join_lanes(tmp_ref, tiles):
    tmp_ref[...] = tiles.astype(F32)
    count = tmp_ref.shape[0] // 4
    return jnp.concatenate([tmp_ref[pl.ds(c, count, stride=4), :] for c in range(4)], axis=1)


def select_kernel(rows_ref, info_ref, out_ref, pick_ref, tmp_ref):
    rows = rows_ref[...]
    total = info_ref.shape[0]
    columns = lax.broadcasted_iota(jnp.int32, (total, rows.shape[0]), 1)
    list_rows = (columns == info_ref[:, 0:1]).astype(BF16)
    lists = dot(list_rows, rows[:, 384:512], 1, 0)
    lanes = lax.broadcasted_iota(jnp.int32, lists.shape, 1) + 384
    block = jnp.sum(jnp.where(lanes == info_ref[:, 2:3], lists, 0.0), axis=1, keepdims=True)
    column = info_ref[:, 1:2] + 2 * block.astype(jnp.int32)
    pick = (columns == column).astype(BF16)
    pick_ref[...] = pick
    out_ref[...] = split_lanes(tmp_ref, dot(pick, rows, 1, 0))


def panel_copies(sources, panel_ref, sems):
    half = panel_ref.shape[2] // 2
    targets = [panel_ref.at[d] for d in range(3)]
    targets += [panel_ref.at[3, :, pl.ds(i * half, half)] for i in range(2)]
    copies = [
        pltpu.make_async_copy(source, target, sems.at[i])
        for i, (source, target) in enumerate(zip(sources, targets))
    ]
    for copy in copies:
        copy.start()
    return [copies[:1], copies[1:2], copies[2:3], copies[3:]]


def hidden_kernel(x_ref, tiles_ref, mark_ref, *refs):
    sources, row_refs = refs[:5], refs[5:9]
    out_ref, prob_ref, acc_ref, tmp_ref, panel_ref, sems = refs[9:]
    copies = panel_copies(sources, panel_ref, sems)
    width = panel_ref.shape[1] // 3
    parts = acc_ref.shape[0]
    count = acc_ref.shape[1]
    for d, step in enumerate(STEPS):
        rows = join_lanes(tmp_ref, tiles_ref[lax.rem(x_ref[0] + step, 4)])
        prob = jnp.sum(rows[:, 0:256] * mark_ref[...], axis=1, keepdims=True)
        x = rows[:, 0:256].astype(BF16)
        grad = (prob * rows[:, DY_LANE:LANES]).astype(BF16)
        row_refs[d][:, 0:DY_LANE] = x
        row_refs[d][:, DY_LANE:LANES] = grad
        if d == 0:
            prob_ref[...] = jnp.broadcast_to(prob, prob_ref.shape)
        for copy in copies[d]:
            copy.wait()
        for part in range(parts):
            left = grad if part == 2 else x
            term = dot(left[:, 0:width], panel_ref[d, part * width : (part + 1) * width], 1, 0)
            if d == 0:
                acc_ref[part] = term
            else:
                acc_ref[part] += term
    for part in range(parts):
        for piece in range(out_ref.shape[0]):
            out_ref[piece, part * count : (part + 1) * count] = acc_ref[
                part, :, piece * 128 : (piece + 1) * 128
            ].astype(BF16)


def point_kernel(parts_ref, out_ref):
    count = out_ref.shape[0] // 3
    total = jnp.sum(parts_ref[...].astype(F32), axis=0)
    gate, up, grad = total[0:count], total[count : 2 * count], total[2 * count :]
    sigma = jax.nn.sigmoid(gate)
    out_ref[0:count] = (gate * sigma * up).astype(BF16)
    out_ref[count : 2 * count] = (grad * up * sigma * (1.0 + gate * (1.0 - sigma))).astype(BF16)
    out_ref[2 * count :] = (grad * gate * sigma).astype(BF16)


def hidden_parts(act):
    count = act.shape[1] // 3
    return [
        jnp.concatenate([act[k, i * count : (i + 1) * count] for k in range(act.shape[0])], axis=1)
        for i in range(3)
    ]


def result_kernel(x_ref, act_ref, prob_ref, *refs):
    sources, (out_ref, res_ref, tmp_ref, panel_ref, sems) = refs[:5], refs[5:]
    copies = panel_copies(sources, panel_ref, sems)
    width = panel_ref.shape[1] // 3
    hidden, gate_grad, up_grad = hidden_parts(act_ref)
    res_ref[...] = jnp.zeros_like(res_ref)
    for d, step in enumerate(STEPS):
        for copy in copies[d]:
            copy.wait()
        outcome = prob_ref[:, 0:1] * dot(hidden, panel_ref[d, 2 * width :], 1, 1)
        dx = dot(gate_grad, panel_ref[d, 0:width], 1, 1)
        dx += dot(up_grad, panel_ref[d, width : 2 * width], 1, 1)
        res_ref[:, 0:width] = outcome
        res_ref[:, DY_LANE : DY_LANE + width] = dx
        out_ref[lax.rem(x_ref[0] + step, 4)] = split_lanes(tmp_ref, res_ref[...])


def weight_kernel(x_ref, act_ref, *refs):
    row_refs, out_refs, acc_ref = refs[:4], refs[4:7], refs[7]
    step = pl.program_id(0)
    width = out_refs[0].shape[0]
    hidden, gate_grad, up_grad = hidden_parts(act_ref.at[0])

    @pl.when(step == 0)
    def _():
        acc_ref[...] = jnp.zeros_like(acc_ref)

    for d in range(4):

        @pl.when(step == d)
        def _():
            x = row_refs[d][:, 0:width]
            grad = row_refs[d][:, DY_LANE : DY_LANE + width]
            acc_ref[0] += dot(x, gate_grad, 0, 0)
            acc_ref[1] += dot(x, up_grad, 0, 0)
            acc_ref[2] += dot(grad, hidden, 0, 0)

    @pl.when(step == pl.num_programs(0) - 1)
    def _():
        for part in range(3):
            out_refs[part][...] = acc_ref[part].astype(BF16)


def combine_kernel(pick_ref, tiles_ref, out_ref, tmp_ref):
    rows = join_lanes(tmp_ref, tiles_ref[...]).astype(BF16)
    out_ref[...] = dot(pick_ref[...], rows, 0, 0).astype(BF16)


def unpack_kernel(rows_ref, out_ref, dx_ref):
    result = dot(rows_ref[...], token_permutation(LANES), 0, 0).astype(BF16)
    out_ref[...] = result[0:P_LANE]
    dx_ref[...] = result[DY_LANE : DY_LANE + P_LANE]


def routing_info(expert_slot, block_counts, entries, share_x):
    groups, experts = block_counts.shape
    ids = jnp.arange(experts, dtype=jnp.int32)
    slot_is = (expert_slot[:, None] == ids[None, :]).astype(jnp.int32)
    slot_expert = jnp.sum(slot_is * ids[:, None], axis=0)
    counts = jnp.sum(block_counts[:, :, None] * slot_is[None], axis=1)
    used = (counts > 0).astype(jnp.int32)
    before = (ids[:, None] < ids[None, :]).astype(jnp.int32)
    rank = jnp.sum(used[:, None, :] * before[:, :, None], axis=0)
    user_ids = jnp.arange(USERS, dtype=jnp.int32)[:, None, None]
    chosen = used[None] * (rank[None] == user_ids).astype(jnp.int32)
    user_group = jnp.sum(chosen * ids[None, :, None], axis=1)
    user_count = jnp.sum(chosen * counts[None], axis=1)
    per_x = USERS * entries * 2 // share_x
    shape = (share_x, groups, per_x)
    member = lax.broadcasted_iota(jnp.int32, shape, 0) * per_x
    member = member + lax.broadcasted_iota(jnp.int32, shape, 2)
    first = member < entries * 2
    entry = (member >> 1) - jnp.where(first, 0, entries)
    group = jnp.where(first, user_group[0][None, :, None], user_group[1][None, :, None])
    limit = jnp.where(first, user_count[0][None, :, None], user_count[1][None, :, None])
    list_row = group * BLK + slot_expert[None, :, None]
    base = jnp.where(entry < limit, group * BLK + (member & 1), -100000)
    info = jnp.stack([list_row, base, entry + LIST_LANE], axis=-1)
    return info.reshape(-1, 3)


def exchange(array, axis):
    return lax.all_to_all(array, axis, split_axis=0, concat_axis=0, tiled=True)


def body(
    tokens, grad_output, gate_prob, w_gate, w_up, w_down, expert_slot, block_counts, block_lists
):
    groups = lax.axis_size(GROUP)
    share_y = lax.axis_size("y")
    share_x = lax.axis_size("x")
    width = tokens.shape[1]
    hid = w_gate.shape[2]
    entries = block_lists.shape[2]
    picked = USERS * entries * 2
    total = groups * picked
    count = total // share_x

    me_x = lax.axis_index("x")
    order = me_x[None].astype(jnp.int32)
    shifts = [[(i, (i + d) % share_x) for i in range(share_x)] for d in range(share_x)]

    def shift(array, d):
        return lax.ppermute(array, "x", shifts[d])

    panel = jnp.concatenate([w_gate[0], w_up[0], w_down[0].T], axis=0)
    right, left = shift(panel, 1), shift(panel, 3)

    packed = call(
        pack_kernel,
        jax.ShapeDtypeStruct((groups, BLK, LANES), BF16),
        (tokens.T, grad_output.T, gate_prob.T, block_lists.transpose(2, 0, 1)),
        VMEM_LARGE,
        scratch_shapes=[pltpu.VMEM((LANES, LANES), BF16)],
    )
    info = routing_info(expert_slot, block_counts, entries, share_x)
    mine = (expert_slot == lax.axis_index(GROUP)).astype(F32)
    mark = lax.pad(mine, jnp.zeros((), F32), ((P_LANE, 16, 0),))[None]
    spread = exchange(packed, GROUP).reshape(groups * BLK, LANES)
    spread, info = lax.optimization_barrier((spread, info))
    sent, pick = call(
        select_kernel,
        (
            jax.ShapeDtypeStruct((4 * total, 128), BF16),
            jax.ShapeDtypeStruct((total, groups * BLK), BF16),
        ),
        (spread, info),
        scratch_shapes=[pltpu.VMEM((4 * total, 128), F32)],
    )
    sent, right, left = lax.optimization_barrier((sent, right, left))
    half = hid // 2
    panels = [panel, right, left, shift(right[:, 0:half], 1), shift(left[:, half:], 3)]
    pieces = (share_x * groups, 4 * picked // share_x, 128)
    tiles = exchange(sent.reshape(pieces), OWNERS).reshape(share_x, 4 * count, 128)

    def before(d, x):
        return (lax.rem(x[0] + share_x - d, share_x), 0, 0)

    def whole(*shape):
        return pl.BlockSpec(shape, lambda *_: (0,) * len(shape))

    tile_block = (1, 4 * count, 128)
    act_shape = (share_y, 3 * count, hid // share_y)
    scalar_spec = pl.BlockSpec(memory_space=pltpu.SMEM)
    vmem_spec = pl.BlockSpec(memory_space=pltpu.VMEM)
    panel_specs = [pl.BlockSpec(memory_space=pl.ANY)] * 5
    panel_scratch = [pltpu.VMEM((4, 3 * width, hid), BF16), pltpu.SemaphoreType.DMA((5,))]
    *rows, parts, prob = call(
        hidden_kernel,
        (jax.ShapeDtypeStruct((count, LANES), BF16),) * 4
        + (jax.ShapeDtypeStruct(act_shape, BF16), jax.ShapeDtypeStruct((count, 128), F32)),
        (order, tiles, mark, *panels),
        VMEM_LARGE,
        in_specs=[scalar_spec, vmem_spec, vmem_spec] + panel_specs,
        scratch_shapes=[pltpu.VMEM((3, count, hid), F32), pltpu.VMEM((4 * count, 128), F32)]
        + panel_scratch,
    )
    parts = exchange(parts, "y")
    rows = [shift(rows[d], STEPS[d]) if STEPS[d] else rows[d] for d in range(share_x)]
    parts, *rows = lax.optimization_barrier((parts, *rows))
    act = call(point_kernel, jax.ShapeDtypeStruct(act_shape[1:], BF16), (parts,))
    act = lax.all_gather(act, "y", axis=0, tiled=False)
    all_act = lax.all_gather(act, "x", axis=0, tiled=False)
    results = call(
        result_kernel,
        jax.ShapeDtypeStruct((share_x, 4 * count, 128), BF16),
        (order, act, prob, *panels),
        VMEM_LARGE,
        in_specs=[scalar_spec, vmem_spec, vmem_spec] + panel_specs,
        scratch_shapes=[pltpu.VMEM((count, LANES), F32), pltpu.VMEM((4 * count, 128), F32)]
        + panel_scratch,
    )
    weights = call(
        weight_kernel,
        (jax.ShapeDtypeStruct((width, hid), BF16),) * 3,
        (order, all_act, *(rows[STEPS.index(d)] for d in range(share_x))),
        VMEM_LARGE,
        grid_spec=pltpu.PrefetchScalarGridSpec(
            num_scalar_prefetch=1,
            grid=(share_x,),
            in_specs=[pl.BlockSpec((1,) + act_shape, lambda d, x: before(d, x) + (0,))]
            + [whole(count, LANES)] * 4,
            out_specs=[whole(width, hid)] * 3,
            scratch_shapes=[pltpu.VMEM((3, width, hid), F32)],
        ),
    )
    back = exchange(results.reshape(pieces), OWNERS).reshape(4 * total, 128)
    summed = call(
        combine_kernel,
        jax.ShapeDtypeStruct((groups * BLK, LANES), BF16),
        (pick, back),
        scratch_shapes=[pltpu.VMEM((4 * total, 128), F32)],
    )
    home = exchange(summed.reshape(groups, BLK, LANES), GROUP).reshape(groups * BLK, LANES)
    out, dx = call(
        unpack_kernel,
        (jax.ShapeDtypeStruct((width, groups * BLK), BF16),) * 2,
        (home,),
    )
    return (
        out.T,
        dx.T,
        weights[0][None],
        weights[1][None],
        weights[2].T[None],
    )


def solution(mesh):
    devices = mesh.devices.reshape(8, 2, 8, 4)
    inner = Mesh(devices, ("z", "core", "y", "x"))
    member = ("y", "x")
    in_specs = (
        P(GROUP, member),
        P(GROUP, member),
        P(GROUP, None),
        P(GROUP, member, None),
        P(GROUP, member, None),
        P(GROUP, None, member),
        P(),
        P(),
        P(GROUP, None, None),
    )
    out_specs = (
        P(GROUP, member),
        P(GROUP, member),
        P(GROUP, member, None),
        P(GROUP, member, None),
        P(GROUP, None, member),
    )
    return jax.shard_map(body, mesh=inner, in_specs=in_specs, out_specs=out_specs, check_vma=False)
```

```python
import jax
import jax.numpy as jnp
from jax import lax
from jax.experimental import pallas as pl
from jax.experimental.pallas import tpu as pltpu
from jax.sharding import Mesh, PartitionSpec as P

BLK = 32
USERS = 2
LANES = 512
STEPS = (0, 3, 1, 2)
P_LANE = 224
DY_LANE = 256
LIST_LANE = 480
GROUP = ("z", "core")
OWNERS = ("x", "z", "core")
F32 = jnp.float32
BF16 = jnp.bfloat16
VMEM_LIMIT = 24 * 1024 * 1024
VMEM_LARGE = 56 * 1024 * 1024


def dot(a, b, ca, cb):
    return lax.dot_general(a, b, (((ca,), (cb,)), ((), ())), preferred_element_type=F32)


def call(kernel, out_shape, args, limit=VMEM_LIMIT, **kw):
    return pl.pallas_call(
        kernel,
        out_shape=out_shape,
        compiler_params=pltpu.CompilerParams(vmem_limit_bytes=limit),
        **kw,
    )(*args)


def token_permutation(rows):
    o = lax.broadcasted_iota(jnp.int32, (rows, rows), 0)
    t = lax.broadcasted_iota(jnp.int32, (rows, rows), 1)
    source = ((o >> 1) & 15) * BLK + (o >> 5) * 2 + (o & 1)
    return (t == source).astype(BF16)


def pack_kernel(tok_ref, dy_ref, prob_ref, list_ref, out_ref, all_ref):
    width = tok_ref.shape[0]
    all_ref[...] = jnp.zeros_like(all_ref)
    all_ref[0:width] = tok_ref[...]
    all_ref[P_LANE : P_LANE + 16] = prob_ref[...]
    all_ref[DY_LANE : DY_LANE + width] = dy_ref[...]
    packed = dot(token_permutation(LANES), all_ref[...], 1, 1)
    lists = list_ref[:, 0, :].astype(F32).astype(BF16)
    entry = lax.broadcasted_iota(jnp.int32, (lists.shape[0], LANES), 0)
    lane = lax.broadcasted_iota(jnp.int32, (lists.shape[0], LANES), 1)
    lists = dot(lists, (lane == entry + LIST_LANE).astype(BF16), 0, 0)
    lists = jnp.concatenate([lists, jnp.zeros((BLK - lists.shape[0], LANES), F32)], axis=0)
    out_ref[...] = (packed.reshape(out_ref.shape) + lists[None]).astype(BF16)


def split_lanes(tmp_ref, rows):
    count = rows.shape[0]
    for c in range(4):
        tmp_ref[pl.ds(c, count, stride=4), :] = rows[:, c * 128 : (c + 1) * 128]
    return tmp_ref[...].astype(BF16)


def join_lanes(tmp_ref, tiles):
    tmp_ref[...] = tiles.astype(F32)
    count = tmp_ref.shape[0] // 4
    return jnp.concatenate([tmp_ref[pl.ds(c, count, stride=4), :] for c in range(4)], axis=1)


def select_kernel(rows_ref, info_ref, out_ref, pick_ref, tmp_ref):
    rows = rows_ref[...]
    total = info_ref.shape[0]
    columns = lax.broadcasted_iota(jnp.int32, (total, rows.shape[0]), 1)
    list_rows = (columns == info_ref[:, 0:1]).astype(BF16)
    lists = dot(list_rows, rows[:, 384:512], 1, 0)
    lanes = lax.broadcasted_iota(jnp.int32, lists.shape, 1) + 384
    block = jnp.sum(jnp.where(lanes == info_ref[:, 2:3], lists, 0.0), axis=1, keepdims=True)
    column = info_ref[:, 1:2] + 2 * block.astype(jnp.int32)
    pick = (columns == column).astype(BF16)
    pick_ref[...] = pick
    out_ref[...] = split_lanes(tmp_ref, dot(pick, rows, 1, 0))


def panel_copies(x_ref, sources, gate_ref, down_ref, sems):
    half = down_ref.shape[2] // 2
    pairs = []
    for d, step in enumerate(STEPS):
        pairs.append((sources[0].at[lax.rem(x_ref[0] + step, 4)], gate_ref.at[d]))
        if d < 3:
            pairs.append((sources[1 + d], down_ref.at[d]))
    for i in range(2):
        pairs.append((sources[4 + i], down_ref.at[3, :, pl.ds(i * half, half)]))
    copies = [
        pltpu.make_async_copy(source, target, sems.at[i])
        for i, (source, target) in enumerate(pairs)
    ]
    for copy in copies:
        copy.start()
    return [copies[0:2], copies[2:4], copies[4:6], copies[6:9]]


def hidden_kernel(x_ref, tiles_ref, mark_ref, *refs):
    sources, row_refs = refs[:6], refs[6:10]
    out_ref, prob_ref, acc_ref, tmp_ref, gate_ref, down_ref, sems = refs[10:]
    copies = panel_copies(x_ref, sources, gate_ref, down_ref, sems)
    width = down_ref.shape[1]
    parts, count = acc_ref.shape[:2]
    for d, step in enumerate(STEPS):
        rows = join_lanes(tmp_ref, tiles_ref[lax.rem(x_ref[0] + step, 4)])
        prob = jnp.sum(rows[:, 0:256] * mark_ref[...], axis=1, keepdims=True)
        x = rows[:, 0:256].astype(BF16)
        grad = (prob * rows[:, DY_LANE:LANES]).astype(BF16)
        row_refs[d][:, 0:DY_LANE] = x
        row_refs[d][:, DY_LANE:LANES] = grad
        if d == 0:
            prob_ref[...] = jnp.broadcast_to(prob, prob_ref.shape)
        for copy in copies[d]:
            copy.wait()
        terms = [
            dot(x[:, 0:width], gate_ref[d, 0:width], 1, 0),
            dot(x[:, 0:width], gate_ref[d, width : 2 * width], 1, 0),
            dot(grad[:, 0:width], down_ref[d], 1, 0),
        ]
        for part, term in enumerate(terms):
            if d == 0:
                acc_ref[part] = term
            elif d < 3:
                acc_ref[part] += term
            else:
                total = (acc_ref[part] + term).astype(BF16)
                for piece in range(out_ref.shape[0]):
                    out_ref[piece, part * count : (part + 1) * count] = total[
                        :, piece * 128 : (piece + 1) * 128
                    ]


def point_kernel(parts_ref, out_ref):
    count = out_ref.shape[0] // 3
    total = jnp.sum(parts_ref[...].astype(F32), axis=0)
    gate, up, grad = total[0:count], total[count : 2 * count], total[2 * count :]
    sigma = jax.nn.sigmoid(gate)
    out_ref[0:count] = (gate * sigma * up).astype(BF16)
    out_ref[count : 2 * count] = (grad * up * sigma * (1.0 + gate * (1.0 - sigma))).astype(BF16)
    out_ref[2 * count :] = (grad * gate * sigma).astype(BF16)


def hidden_parts(act):
    count = act.shape[1] // 3
    return [
        jnp.concatenate([act[k, i * count : (i + 1) * count] for k in range(act.shape[0])], axis=1)
        for i in range(3)
    ]


def result_kernel(x_ref, act_ref, prob_ref, *refs):
    sources, (out_ref, res_ref, tmp_ref, gate_ref, down_ref, sems) = refs[:6], refs[6:]
    copies = panel_copies(x_ref, sources, gate_ref, down_ref, sems)
    width = down_ref.shape[1]
    hidden, gate_grad, up_grad = hidden_parts(act_ref)
    res_ref[...] = jnp.zeros_like(res_ref)
    for d, step in enumerate(STEPS):
        for copy in copies[d]:
            copy.wait()
        outcome = prob_ref[:, 0:1] * dot(hidden, down_ref[d], 1, 1)
        dx = dot(gate_grad, gate_ref[d, 0:width], 1, 1)
        dx += dot(up_grad, gate_ref[d, width : 2 * width], 1, 1)
        res_ref[:, 0:width] = outcome
        res_ref[:, DY_LANE : DY_LANE + width] = dx
        out_ref[lax.rem(x_ref[0] + step, 4)] = split_lanes(tmp_ref, res_ref[...])


def weight_kernel(x_ref, act_ref, *refs):
    row_refs, out_refs, acc_ref = refs[:4], refs[4:7], refs[7]
    step = pl.program_id(0)
    width = out_refs[0].shape[0]
    hidden, gate_grad, up_grad = hidden_parts(act_ref.at[0])

    @pl.when(step == 0)
    def _():
        acc_ref[...] = jnp.zeros_like(acc_ref)

    for d in range(4):

        @pl.when(step == d)
        def _():
            x = row_refs[d][:, 0:width]
            grad = row_refs[d][:, DY_LANE : DY_LANE + width]
            acc_ref[0] += dot(x, gate_grad, 0, 0)
            acc_ref[1] += dot(x, up_grad, 0, 0)
            acc_ref[2] += dot(grad, hidden, 0, 0)

    @pl.when(step == pl.num_programs(0) - 1)
    def _():
        for part in range(3):
            out_refs[part][...] = acc_ref[part].astype(BF16)


def combine_kernel(pick_ref, tiles_ref, out_ref, tmp_ref):
    rows = join_lanes(tmp_ref, tiles_ref[...]).astype(BF16)
    out_ref[...] = dot(pick_ref[...], rows, 0, 0).astype(BF16)


def unpack_kernel(rows_ref, out_ref, dx_ref):
    result = dot(rows_ref[...], token_permutation(LANES), 0, 0).astype(BF16)
    out_ref[...] = result[0:P_LANE]
    dx_ref[...] = result[DY_LANE : DY_LANE + P_LANE]


def routing_info(expert_slot, block_counts, entries, share_x):
    groups, experts = block_counts.shape
    ids = jnp.arange(experts, dtype=jnp.int32)
    slot_is = (expert_slot[:, None] == ids[None, :]).astype(jnp.int32)
    slot_expert = jnp.sum(slot_is * ids[:, None], axis=0)
    counts = jnp.sum(block_counts[:, :, None] * slot_is[None], axis=1)
    used = (counts > 0).astype(jnp.int32)
    before = (ids[:, None] < ids[None, :]).astype(jnp.int32)
    rank = jnp.sum(used[:, None, :] * before[:, :, None], axis=0)
    user_ids = jnp.arange(USERS, dtype=jnp.int32)[:, None, None]
    chosen = used[None] * (rank[None] == user_ids).astype(jnp.int32)
    user_group = jnp.sum(chosen * ids[None, :, None], axis=1)
    user_count = jnp.sum(chosen * counts[None], axis=1)
    per_x = USERS * entries * 2 // share_x
    shape = (share_x, groups, per_x)
    member = lax.broadcasted_iota(jnp.int32, shape, 0) * per_x
    member = member + lax.broadcasted_iota(jnp.int32, shape, 2)
    first = member < entries * 2
    entry = (member >> 1) - jnp.where(first, 0, entries)
    group = jnp.where(first, user_group[0][None, :, None], user_group[1][None, :, None])
    limit = jnp.where(first, user_count[0][None, :, None], user_count[1][None, :, None])
    list_row = group * BLK + slot_expert[None, :, None]
    base = jnp.where(entry < limit, group * BLK + (member & 1), -100000)
    info = jnp.stack([list_row, base, entry + LIST_LANE], axis=-1)
    return info.reshape(-1, 3)


def exchange(array, axis):
    return lax.all_to_all(array, axis, split_axis=0, concat_axis=0, tiled=True)


def body(
    tokens, grad_output, gate_prob, w_gate, w_up, w_down, expert_slot, block_counts, block_lists
):
    groups = lax.axis_size(GROUP)
    share_y = lax.axis_size("y")
    share_x = lax.axis_size("x")
    width = tokens.shape[1]
    hid = w_gate.shape[2]
    entries = block_lists.shape[2]
    picked = USERS * entries * 2
    total = groups * picked
    count = total // share_x

    me_x = lax.axis_index("x")
    order = me_x[None].astype(jnp.int32)
    shifts = [[(i, (i + d) % share_x) for i in range(share_x)] for d in range(share_x)]

    def shift(array, d):
        return lax.ppermute(array, "x", shifts[d])

    gates = jnp.concatenate([w_gate[0], w_up[0]], axis=0)
    gates = lax.all_gather(gates, "x", axis=0, tiled=False)
    down = w_down[0].T
    right, left = shift(down, 1), shift(down, 3)

    packed = call(
        pack_kernel,
        jax.ShapeDtypeStruct((groups, BLK, LANES), BF16),
        (tokens.T, grad_output.T, gate_prob.T, block_lists.transpose(2, 0, 1)),
        VMEM_LARGE,
        scratch_shapes=[pltpu.VMEM((LANES, LANES), BF16)],
    )
    info = routing_info(expert_slot, block_counts, entries, share_x)
    mine = (expert_slot == lax.axis_index(GROUP)).astype(F32)
    mark = lax.pad(mine, jnp.zeros((), F32), ((P_LANE, 16, 0),))[None]
    spread = exchange(packed, GROUP).reshape(groups * BLK, LANES)
    spread, info, right, left = lax.optimization_barrier((spread, info, right, left))
    sent, pick = call(
        select_kernel,
        (
            jax.ShapeDtypeStruct((4 * total, 128), BF16),
            jax.ShapeDtypeStruct((total, groups * BLK), BF16),
        ),
        (spread, info),
        scratch_shapes=[pltpu.VMEM((4 * total, 128), F32)],
    )
    half = hid // 2
    panels = [gates, down, right, left, shift(right[:, 0:half], 1), shift(left[:, half:], 3)]
    pieces = (share_x * groups, 4 * picked // share_x, 128)
    tiles = exchange(sent.reshape(pieces), OWNERS).reshape(share_x, 4 * count, 128)

    def before(d, x):
        return (lax.rem(x[0] + share_x - d, share_x), 0, 0)

    def whole(*shape):
        return pl.BlockSpec(shape, lambda *_: (0,) * len(shape))

    tile_block = (1, 4 * count, 128)
    act_shape = (share_y, 3 * count, hid // share_y)
    scalar_spec = pl.BlockSpec(memory_space=pltpu.SMEM)
    vmem_spec = pl.BlockSpec(memory_space=pltpu.VMEM)
    panel_specs = [pl.BlockSpec(memory_space=pl.ANY)] * 6
    panel_scratch = [
        pltpu.VMEM((4, 2 * width, hid), BF16),
        pltpu.VMEM((4, width, hid), BF16),
        pltpu.SemaphoreType.DMA((9,)),
    ]
    *rows, parts, prob = call(
        hidden_kernel,
        (jax.ShapeDtypeStruct((count, LANES), BF16),) * 4
        + (jax.ShapeDtypeStruct(act_shape, BF16), jax.ShapeDtypeStruct((count, 128), F32)),
        (order, tiles, mark, *panels),
        VMEM_LARGE,
        in_specs=[scalar_spec, vmem_spec, vmem_spec] + panel_specs,
        scratch_shapes=[pltpu.VMEM((3, count, hid), F32), pltpu.VMEM((4 * count, 128), F32)]
        + panel_scratch,
    )
    parts = exchange(parts, "y")
    rows = [shift(rows[d], STEPS[d]) if STEPS[d] else rows[d] for d in range(share_x)]
    parts, *rows = lax.optimization_barrier((parts, *rows))
    act = call(point_kernel, jax.ShapeDtypeStruct(act_shape[1:], BF16), (parts,))
    act = lax.all_gather(act, "y", axis=0, tiled=False)
    all_act = lax.all_gather(act, "x", axis=0, tiled=False)
    results = call(
        result_kernel,
        jax.ShapeDtypeStruct((share_x, 4 * count, 128), BF16),
        (order, act, prob, *panels),
        VMEM_LARGE,
        in_specs=[scalar_spec, vmem_spec, vmem_spec] + panel_specs,
        scratch_shapes=[pltpu.VMEM((count, LANES), F32), pltpu.VMEM((4 * count, 128), F32)]
        + panel_scratch,
    )
    weights = call(
        weight_kernel,
        (jax.ShapeDtypeStruct((width, hid), BF16),) * 3,
        (order, all_act, *(rows[STEPS.index(d)] for d in range(share_x))),
        VMEM_LARGE,
        grid_spec=pltpu.PrefetchScalarGridSpec(
            num_scalar_prefetch=1,
            grid=(share_x,),
            in_specs=[pl.BlockSpec((1,) + act_shape, lambda d, x: before(d, x) + (0,))]
            + [whole(count, LANES)] * 4,
            out_specs=[whole(width, hid)] * 3,
            scratch_shapes=[pltpu.VMEM((3, width, hid), F32)],
        ),
    )
    back = exchange(results.reshape(pieces), OWNERS).reshape(4 * total, 128)
    summed = call(
        combine_kernel,
        jax.ShapeDtypeStruct((groups * BLK, LANES), BF16),
        (pick, back),
        scratch_shapes=[pltpu.VMEM((4 * total, 128), F32)],
    )
    home = exchange(summed.reshape(groups, BLK, LANES), GROUP).reshape(groups * BLK, LANES)
    out, dx = call(
        unpack_kernel,
        (jax.ShapeDtypeStruct((width, groups * BLK), BF16),) * 2,
        (home,),
    )
    return (
        out.T,
        dx.T,
        weights[0][None],
        weights[1][None],
        weights[2].T[None],
    )


def solution(mesh):
    devices = mesh.devices.reshape(8, 2, 8, 4)
    inner = Mesh(devices, ("z", "core", "y", "x"))
    member = ("y", "x")
    in_specs = (
        P(GROUP, member),
        P(GROUP, member),
        P(GROUP, None),
        P(GROUP, member, None),
        P(GROUP, member, None),
        P(GROUP, None, member),
        P(),
        P(),
        P(GROUP, None, None),
    )
    out_specs = (
        P(GROUP, member),
        P(GROUP, member),
        P(GROUP, member, None),
        P(GROUP, member, None),
        P(GROUP, None, member),
    )
    return jax.shard_map(body, mesh=inner, in_specs=in_specs, out_specs=out_specs, check_vma=False)
```

```python
import jax
import jax.numpy as jnp
from jax import lax
from jax.experimental import pallas as pl
from jax.experimental.pallas import tpu as pltpu
from jax.sharding import Mesh, PartitionSpec as P

BLK = 32
USERS = 2
LANES = 512
STEPS = (0, 3, 1, 2)
P_LANE = 224
DY_LANE = 256
LIST_LANE = 480
GROUP = ("z", "core")
OWNERS = ("x", "z", "core")
F32 = jnp.float32
BF16 = jnp.bfloat16
VMEM_LIMIT = 24 * 1024 * 1024
VMEM_LARGE = 56 * 1024 * 1024


def dot(a, b, ca, cb):
    return lax.dot_general(a, b, (((ca,), (cb,)), ((), ())), preferred_element_type=F32)


def call(kernel, out_shape, args, limit=VMEM_LIMIT, **kw):
    return pl.pallas_call(
        kernel,
        out_shape=out_shape,
        compiler_params=pltpu.CompilerParams(vmem_limit_bytes=limit),
        **kw,
    )(*args)


def token_permutation(rows):
    o = lax.broadcasted_iota(jnp.int32, (rows, rows), 0)
    t = lax.broadcasted_iota(jnp.int32, (rows, rows), 1)
    source = ((o >> 1) & 15) * BLK + (o >> 5) * 2 + (o & 1)
    return (t == source).astype(BF16)


def pack_kernel(
    tok_ref, dy_ref, prob_ref, list_ref, gate_ref, up_ref, down_ref, out_ref, a_ref, b_ref, *refs
):
    all_ref, sems = refs
    width = tok_ref.shape[0]
    hid = gate_ref.shape[1]
    half = hid // 2
    copies = [
        pltpu.make_async_copy(source, target, sems.at[i])
        for i, (source, target) in enumerate(
            (
                (gate_ref, a_ref.at[:, pl.ds(0, hid)]),
                (up_ref.at[:, pl.ds(0, half)], a_ref.at[:, pl.ds(hid, half)]),
                (down_ref, b_ref.at[:, pl.ds(0, hid)]),
                (up_ref.at[:, pl.ds(half, half)], b_ref.at[:, pl.ds(hid, half)]),
            )
        )
    ]
    for copy in copies:
        copy.start()
    all_ref[...] = jnp.zeros_like(all_ref)
    all_ref[0:width] = tok_ref[...]
    all_ref[P_LANE : P_LANE + 16] = prob_ref[...]
    all_ref[DY_LANE : DY_LANE + width] = dy_ref[...]
    packed = dot(token_permutation(LANES), all_ref[...], 1, 1)
    lists = list_ref[:, 0, :].astype(F32).astype(BF16)
    entry = lax.broadcasted_iota(jnp.int32, (lists.shape[0], LANES), 0)
    lane = lax.broadcasted_iota(jnp.int32, (lists.shape[0], LANES), 1)
    lists = dot(lists, (lane == entry + LIST_LANE).astype(BF16), 0, 0)
    lists = jnp.concatenate([lists, jnp.zeros((BLK - lists.shape[0], LANES), F32)], axis=0)
    out_ref[...] = (packed.reshape(out_ref.shape) + lists[None]).astype(BF16)
    for copy in copies:
        copy.wait()


def split_lanes(tmp_ref, rows):
    count = rows.shape[0]
    for c in range(4):
        tmp_ref[pl.ds(c, count, stride=4), :] = rows[:, c * 128 : (c + 1) * 128]
    return tmp_ref[...].astype(BF16)


def join_lanes(tmp_ref, tiles):
    tmp_ref[...] = tiles.astype(F32)
    count = tmp_ref.shape[0] // 4
    return jnp.concatenate([tmp_ref[pl.ds(c, count, stride=4), :] for c in range(4)], axis=1)


def select_kernel(rows_ref, info_ref, out_ref, pick_ref, tmp_ref):
    rows = rows_ref[...]
    total = info_ref.shape[0]
    columns = lax.broadcasted_iota(jnp.int32, (total, rows.shape[0]), 1)
    list_rows = (columns == info_ref[:, 0:1]).astype(BF16)
    lists = dot(list_rows, rows[:, 384:512], 1, 0)
    lanes = lax.broadcasted_iota(jnp.int32, lists.shape, 1) + 384
    block = jnp.sum(jnp.where(lanes == info_ref[:, 2:3], lists, 0.0), axis=1, keepdims=True)
    column = info_ref[:, 1:2] + 2 * block.astype(jnp.int32)
    pick = (columns == column).astype(BF16)
    pick_ref[...] = pick
    out_ref[...] = split_lanes(tmp_ref, dot(pick, rows, 1, 0))


def panel_copies(x_ref, sources, a_ref, b_ref, sems):
    half = b_ref.shape[2] // 2
    pairs = []
    for d, step in enumerate(STEPS):
        pairs.append((sources[0].at[lax.rem(x_ref[0] + step, 4)], a_ref.at[d]))
        if d < 3:
            pairs.append((sources[1 + d], b_ref.at[d]))
    for i in range(2):
        pairs.append((sources[4 + i], b_ref.at[3, :, pl.ds(i * half, half)]))
    copies = [
        pltpu.make_async_copy(source, target, sems.at[i])
        for i, (source, target) in enumerate(pairs)
    ]
    for copy in copies:
        copy.start()
    return [copies[0:2], copies[2:4], copies[4:6], copies[6:9]]


def hidden_kernel(x_ref, tiles_ref, mark_ref, *refs):
    sources, row_refs = refs[:6], refs[6:10]
    out_ref, prob_ref, acc_ref, tmp_ref, a_ref, b_ref, sems = refs[10:]
    copies = panel_copies(x_ref, sources, a_ref, b_ref, sems)
    width = a_ref.shape[1]
    parts, count, hid = acc_ref.shape
    half = hid // 2
    for d, step in enumerate(STEPS):
        rows = join_lanes(tmp_ref, tiles_ref[lax.rem(x_ref[0] + step, 4)])
        prob = jnp.sum(rows[:, 0:256] * mark_ref[...], axis=1, keepdims=True)
        x = rows[:, 0:256].astype(BF16)
        grad = (prob * rows[:, DY_LANE:LANES]).astype(BF16)
        row_refs[d][:, 0:DY_LANE] = x
        row_refs[d][:, DY_LANE:LANES] = grad
        if d == 0:
            prob_ref[...] = jnp.broadcast_to(prob, prob_ref.shape)
        for copy in copies[d]:
            copy.wait()
        x, grad = x[:, 0:width], grad[:, 0:width]
        terms = [
            (0, 0, hid, dot(x, a_ref[d, :, 0:hid], 1, 0)),
            (1, 0, half, dot(x, a_ref[d, :, hid:], 1, 0)),
            (1, half, hid, dot(x, b_ref[d, :, hid:], 1, 0)),
            (2, 0, hid, dot(grad, b_ref[d, :, 0:hid], 1, 0)),
        ]
        for part, low, high, term in terms:
            if d == 0:
                acc_ref[part, :, low:high] = term
            elif d < 3:
                acc_ref[part, :, low:high] += term
            else:
                total = (acc_ref[part, :, low:high] + term).astype(BF16)
                for piece in range(low // 128, high // 128):
                    lane = piece * 128 - low
                    out_ref[piece, part * count : (part + 1) * count] = total[:, lane : lane + 128]


def point_kernel(parts_ref, out_ref):
    count = out_ref.shape[0] // 3
    total = jnp.sum(parts_ref[...].astype(F32), axis=0)
    gate, up, grad = total[0:count], total[count : 2 * count], total[2 * count :]
    sigma = jax.nn.sigmoid(gate)
    out_ref[0:count] = (gate * sigma * up).astype(BF16)
    out_ref[count : 2 * count] = (grad * up * sigma * (1.0 + gate * (1.0 - sigma))).astype(BF16)
    out_ref[2 * count :] = (grad * gate * sigma).astype(BF16)


def hidden_parts(act):
    count = act.shape[1] // 3
    return [
        jnp.concatenate([act[k, i * count : (i + 1) * count] for k in range(act.shape[0])], axis=1)
        for i in range(3)
    ]


def result_kernel(x_ref, act_ref, prob_ref, *refs):
    sources, (out_ref, res_ref, tmp_ref, a_ref, b_ref, sems) = refs[:6], refs[6:]
    copies = panel_copies(x_ref, sources, a_ref, b_ref, sems)
    width = a_ref.shape[1]
    hidden, gate_grad, up_grad = hidden_parts(act_ref)
    hid = hidden.shape[1]
    half = hid // 2
    first = jnp.concatenate([gate_grad, up_grad[:, 0:half]], axis=1)
    res_ref[...] = jnp.zeros_like(res_ref)
    for d, step in enumerate(STEPS):
        for copy in copies[d]:
            copy.wait()
        outcome = prob_ref[:, 0:1] * dot(hidden, b_ref[d, :, 0:hid], 1, 1)
        dx = dot(first, a_ref[d], 1, 1) + dot(up_grad[:, half:], b_ref[d, :, hid:], 1, 1)
        res_ref[:, 0:width] = outcome
        res_ref[:, DY_LANE : DY_LANE + width] = dx
        out_ref[lax.rem(x_ref[0] + step, 4)] = split_lanes(tmp_ref, res_ref[...])


def weight_kernel(x_ref, act_ref, *refs):
    row_refs, out_refs, acc_ref = refs[:4], refs[4:7], refs[7]
    step = pl.program_id(0)
    width = out_refs[0].shape[0]
    hidden, gate_grad, up_grad = hidden_parts(act_ref.at[0])

    @pl.when(step == 0)
    def _():
        acc_ref[...] = jnp.zeros_like(acc_ref)

    for d in range(4):

        @pl.when(step == d)
        def _():
            x = row_refs[d][:, 0:width]
            grad = row_refs[d][:, DY_LANE : DY_LANE + width]
            acc_ref[0] += dot(x, gate_grad, 0, 0)
            acc_ref[1] += dot(x, up_grad, 0, 0)
            acc_ref[2] += dot(grad, hidden, 0, 0)

    @pl.when(step == pl.num_programs(0) - 1)
    def _():
        for part in range(3):
            out_refs[part][...] = acc_ref[part].astype(BF16)


def combine_kernel(pick_ref, tiles_ref, out_ref, tmp_ref):
    rows = join_lanes(tmp_ref, tiles_ref[...]).astype(BF16)
    out_ref[...] = dot(pick_ref[...], rows, 0, 0).astype(BF16)


def unpack_kernel(rows_ref, out_ref, dx_ref):
    result = dot(rows_ref[...], token_permutation(LANES), 0, 0).astype(BF16)
    out_ref[...] = result[0:P_LANE]
    dx_ref[...] = result[DY_LANE : DY_LANE + P_LANE]


def routing_info(expert_slot, block_counts, entries, share_x):
    groups, experts = block_counts.shape
    ids = jnp.arange(experts, dtype=jnp.int32)
    slot_is = (expert_slot[:, None] == ids[None, :]).astype(jnp.int32)
    slot_expert = jnp.sum(slot_is * ids[:, None], axis=0)
    counts = jnp.sum(block_counts[:, :, None] * slot_is[None], axis=1)
    used = (counts > 0).astype(jnp.int32)
    before = (ids[:, None] < ids[None, :]).astype(jnp.int32)
    rank = jnp.sum(used[:, None, :] * before[:, :, None], axis=0)
    user_ids = jnp.arange(USERS, dtype=jnp.int32)[:, None, None]
    chosen = used[None] * (rank[None] == user_ids).astype(jnp.int32)
    user_group = jnp.sum(chosen * ids[None, :, None], axis=1)
    user_count = jnp.sum(chosen * counts[None], axis=1)
    per_x = USERS * entries * 2 // share_x
    shape = (share_x, groups, per_x)
    member = lax.broadcasted_iota(jnp.int32, shape, 0) * per_x
    member = member + lax.broadcasted_iota(jnp.int32, shape, 2)
    first = member < entries * 2
    entry = (member >> 1) - jnp.where(first, 0, entries)
    group = jnp.where(first, user_group[0][None, :, None], user_group[1][None, :, None])
    limit = jnp.where(first, user_count[0][None, :, None], user_count[1][None, :, None])
    list_row = group * BLK + slot_expert[None, :, None]
    base = jnp.where(entry < limit, group * BLK + (member & 1), -100000)
    info = jnp.stack([list_row, base, entry + LIST_LANE], axis=-1)
    return info.reshape(-1, 3)


def exchange(array, axis):
    return lax.all_to_all(array, axis, split_axis=0, concat_axis=0, tiled=True)


def body(
    tokens, grad_output, gate_prob, w_gate, w_up, w_down, expert_slot, block_counts, block_lists
):
    groups = lax.axis_size(GROUP)
    share_y = lax.axis_size("y")
    share_x = lax.axis_size("x")
    width = tokens.shape[1]
    hid = w_gate.shape[2]
    entries = block_lists.shape[2]
    picked = USERS * entries * 2
    total = groups * picked
    count = total // share_x

    me_x = lax.axis_index("x")
    order = me_x[None].astype(jnp.int32)
    shifts = [[(i, (i + d) % share_x) for i in range(share_x)] for d in range(share_x)]

    def shift(array, d):
        return lax.ppermute(array, "x", shifts[d])

    vmem_spec = pl.BlockSpec(memory_space=pltpu.VMEM)
    any_spec = pl.BlockSpec(memory_space=pl.ANY)
    both = jax.ShapeDtypeStruct((width, 3 * hid // 2), BF16)
    packed, panel_a, panel_b = call(
        pack_kernel,
        (jax.ShapeDtypeStruct((groups, BLK, LANES), BF16), both, both),
        (
            tokens.T,
            grad_output.T,
            gate_prob.T,
            block_lists.transpose(2, 0, 1),
            w_gate[0],
            w_up[0],
            w_down[0].T,
        ),
        VMEM_LARGE,
        in_specs=[vmem_spec] * 4 + [any_spec] * 3,
        out_specs=[vmem_spec, any_spec, any_spec],
        scratch_shapes=[pltpu.VMEM((LANES, LANES), BF16), pltpu.SemaphoreType.DMA((4,))],
    )
    all_a = lax.all_gather(panel_a, "x", axis=0, tiled=False)
    right, left = shift(panel_b, 1), shift(panel_b, 3)
    info = routing_info(expert_slot, block_counts, entries, share_x)
    mine = (expert_slot == lax.axis_index(GROUP)).astype(F32)
    mark = lax.pad(mine, jnp.zeros((), F32), ((P_LANE, 16, 0),))[None]
    spread = exchange(packed, GROUP).reshape(groups * BLK, LANES)
    spread, info, right, left = lax.optimization_barrier((spread, info, right, left))
    sent, pick = call(
        select_kernel,
        (
            jax.ShapeDtypeStruct((4 * total, 128), BF16),
            jax.ShapeDtypeStruct((total, groups * BLK), BF16),
        ),
        (spread, info),
        scratch_shapes=[pltpu.VMEM((4 * total, 128), F32)],
    )
    half = 3 * hid // 4
    panels = [all_a, panel_b, right, left, shift(right[:, 0:half], 1), shift(left[:, half:], 3)]
    pieces = (share_x * groups, 4 * picked // share_x, 128)
    tiles = exchange(sent.reshape(pieces), OWNERS).reshape(share_x, 4 * count, 128)

    def before(d, x):
        return (lax.rem(x[0] + share_x - d, share_x), 0, 0)

    def whole(*shape):
        return pl.BlockSpec(shape, lambda *_: (0,) * len(shape))

    tile_block = (1, 4 * count, 128)
    act_shape = (share_y, 3 * count, hid // share_y)
    scalar_spec = pl.BlockSpec(memory_space=pltpu.SMEM)
    panel_specs = [any_spec] * 6
    panel_scratch = [pltpu.VMEM((4,) + both.shape, BF16)] * 2 + [pltpu.SemaphoreType.DMA((9,))]
    *rows, parts, prob = call(
        hidden_kernel,
        (jax.ShapeDtypeStruct((count, LANES), BF16),) * 4
        + (jax.ShapeDtypeStruct(act_shape, BF16), jax.ShapeDtypeStruct((count, 128), F32)),
        (order, tiles, mark, *panels),
        VMEM_LARGE,
        in_specs=[scalar_spec, vmem_spec, vmem_spec] + panel_specs,
        scratch_shapes=[pltpu.VMEM((3, count, hid), F32), pltpu.VMEM((4 * count, 128), F32)]
        + panel_scratch,
    )
    parts = exchange(parts, "y")
    rows = [shift(rows[d], STEPS[d]) if STEPS[d] else rows[d] for d in range(share_x)]
    parts, *rows = lax.optimization_barrier((parts, *rows))
    act = call(point_kernel, jax.ShapeDtypeStruct(act_shape[1:], BF16), (parts,))
    act = lax.all_gather(act, "y", axis=0, tiled=False)
    all_act = lax.all_gather(act, "x", axis=0, tiled=False)
    results = call(
        result_kernel,
        jax.ShapeDtypeStruct((share_x, 4 * count, 128), BF16),
        (order, act, prob, *panels),
        VMEM_LARGE,
        in_specs=[scalar_spec, vmem_spec, vmem_spec] + panel_specs,
        scratch_shapes=[pltpu.VMEM((count, LANES), F32), pltpu.VMEM((4 * count, 128), F32)]
        + panel_scratch,
    )
    weights = call(
        weight_kernel,
        (jax.ShapeDtypeStruct((width, hid), BF16),) * 3,
        (order, all_act, *(rows[STEPS.index(d)] for d in range(share_x))),
        VMEM_LARGE,
        grid_spec=pltpu.PrefetchScalarGridSpec(
            num_scalar_prefetch=1,
            grid=(share_x,),
            in_specs=[pl.BlockSpec((1,) + act_shape, lambda d, x: before(d, x) + (0,))]
            + [whole(count, LANES)] * 4,
            out_specs=[whole(width, hid)] * 3,
            scratch_shapes=[pltpu.VMEM((3, width, hid), F32)],
        ),
    )
    back = exchange(results.reshape(pieces), OWNERS).reshape(4 * total, 128)
    summed = call(
        combine_kernel,
        jax.ShapeDtypeStruct((groups * BLK, LANES), BF16),
        (pick, back),
        scratch_shapes=[pltpu.VMEM((4 * total, 128), F32)],
    )
    home = exchange(summed.reshape(groups, BLK, LANES), GROUP).reshape(groups * BLK, LANES)
    out, dx = call(
        unpack_kernel,
        (jax.ShapeDtypeStruct((width, groups * BLK), BF16),) * 2,
        (home,),
    )
    return (
        out.T,
        dx.T,
        weights[0][None],
        weights[1][None],
        weights[2].T[None],
    )


def solution(mesh):
    devices = mesh.devices.reshape(8, 2, 8, 4)
    inner = Mesh(devices, ("z", "core", "y", "x"))
    member = ("y", "x")
    in_specs = (
        P(GROUP, member),
        P(GROUP, member),
        P(GROUP, None),
        P(GROUP, member, None),
        P(GROUP, member, None),
        P(GROUP, None, member),
        P(),
        P(),
        P(GROUP, None, None),
    )
    out_specs = (
        P(GROUP, member),
        P(GROUP, member),
        P(GROUP, member, None),
        P(GROUP, member, None),
        P(GROUP, None, member),
    )
    return jax.shard_map(body, mesh=inner, in_specs=in_specs, out_specs=out_specs, check_vma=False)
```

```python
import jax
import jax.numpy as jnp
from jax import lax
from jax.experimental import pallas as pl
from jax.experimental.pallas import tpu as pltpu
from jax.sharding import Mesh, PartitionSpec as P

BLK = 32
USERS = 2
LANES = 512
STEPS = (0, 3, 1, 2)
P_LANE = 224
DY_LANE = 256
LIST_LANE = 480
GROUP = ("z", "core")
OWNERS = ("x", "z", "core")
F32 = jnp.float32
BF16 = jnp.bfloat16
VMEM_LIMIT = 24 * 1024 * 1024
VMEM_LARGE = 56 * 1024 * 1024


def dot(a, b, ca, cb):
    return lax.dot_general(a, b, (((ca,), (cb,)), ((), ())), preferred_element_type=F32)


def call(kernel, out_shape, args, limit=VMEM_LIMIT, **kw):
    return pl.pallas_call(
        kernel,
        out_shape=out_shape,
        compiler_params=pltpu.CompilerParams(vmem_limit_bytes=limit),
        **kw,
    )(*args)


def token_permutation(rows):
    o = lax.broadcasted_iota(jnp.int32, (rows, rows), 0)
    t = lax.broadcasted_iota(jnp.int32, (rows, rows), 1)
    source = ((o >> 1) & 15) * BLK + (o >> 5) * 2 + (o & 1)
    return (t == source).astype(BF16)


def pack_kernel(tok_ref, dy_ref, prob_ref, list_ref, out_ref, all_ref):
    width = tok_ref.shape[0]
    all_ref[...] = jnp.zeros_like(all_ref)
    all_ref[0:width] = tok_ref[...]
    all_ref[P_LANE : P_LANE + 16] = prob_ref[...]
    all_ref[DY_LANE : DY_LANE + width] = dy_ref[...]
    packed = dot(token_permutation(LANES), all_ref[...], 1, 1)
    lists = list_ref[:, 0, :].astype(F32).astype(BF16)
    entry = lax.broadcasted_iota(jnp.int32, (lists.shape[0], LANES), 0)
    lane = lax.broadcasted_iota(jnp.int32, (lists.shape[0], LANES), 1)
    lists = dot(lists, (lane == entry + LIST_LANE).astype(BF16), 0, 0)
    lists = jnp.concatenate([lists, jnp.zeros((BLK - lists.shape[0], LANES), F32)], axis=0)
    out_ref[...] = (packed.reshape(out_ref.shape) + lists[None]).astype(BF16)


def split_lanes(tmp_ref, rows):
    count = rows.shape[0]
    for c in range(4):
        tmp_ref[pl.ds(c, count, stride=4), :] = rows[:, c * 128 : (c + 1) * 128]
    return tmp_ref[...].astype(BF16)


def join_lanes(tmp_ref, tiles):
    tmp_ref[...] = tiles.astype(F32)
    count = tmp_ref.shape[0] // 4
    return jnp.concatenate([tmp_ref[pl.ds(c, count, stride=4), :] for c in range(4)], axis=1)


def select_kernel(rows_ref, info_ref, out_ref, pick_ref, tmp_ref):
    rows = rows_ref[...]
    total = info_ref.shape[0]
    columns = lax.broadcasted_iota(jnp.int32, (total, rows.shape[0]), 1)
    list_rows = (columns == info_ref[:, 0:1]).astype(BF16)
    lists = dot(list_rows, rows[:, 384:512], 1, 0)
    lanes = lax.broadcasted_iota(jnp.int32, lists.shape, 1) + 384
    block = jnp.sum(jnp.where(lanes == info_ref[:, 2:3], lists, 0.0), axis=1, keepdims=True)
    column = info_ref[:, 1:2] + 2 * block.astype(jnp.int32)
    pick = (columns == column).astype(BF16)
    pick_ref[...] = pick
    out_ref[...] = split_lanes(tmp_ref, dot(pick, rows, 1, 0))


def panel_copies(x_ref, sources, gate_ref, down_ref, sems):
    half = down_ref.shape[2] // 2
    pairs = []
    for d, step in enumerate(STEPS):
        pairs.append((sources[0].at[lax.rem(x_ref[0] + step, 4)], gate_ref.at[d]))
        if d < 3:
            pairs.append((sources[1 + d], down_ref.at[d]))
    for i in range(2):
        pairs.append((sources[4 + i], down_ref.at[3, :, pl.ds(i * half, half)]))
    copies = [
        pltpu.make_async_copy(source, target, sems.at[i])
        for i, (source, target) in enumerate(pairs)
    ]
    for copy in copies:
        copy.start()
    return [copies[0:2], copies[2:4], copies[4:6], copies[6:9]]


def hidden_kernel(x_ref, tiles_ref, mark_ref, *refs):
    sources, row_refs = refs[:6], refs[6:10]
    out_ref, prob_ref, acc_ref, tmp_ref, gate_ref, down_ref, sems = refs[10:]
    copies = panel_copies(x_ref, sources, gate_ref, down_ref, sems)
    width = down_ref.shape[1]
    parts, count = acc_ref.shape[:2]
    for d, step in enumerate(STEPS):
        rows = join_lanes(tmp_ref, tiles_ref[lax.rem(x_ref[0] + step, 4)])
        prob = jnp.sum(rows[:, 0:256] * mark_ref[...], axis=1, keepdims=True)
        x = rows[:, 0:256].astype(BF16)
        grad = (prob * rows[:, DY_LANE:LANES]).astype(BF16)
        row_refs[d][:, 0:DY_LANE] = x
        row_refs[d][:, DY_LANE:LANES] = grad
        if d == 0:
            prob_ref[...] = jnp.broadcast_to(prob, prob_ref.shape)
        for copy in copies[d]:
            copy.wait()
        terms = [
            dot(x[:, 0:width], gate_ref[d, 0:width], 1, 0),
            dot(x[:, 0:width], gate_ref[d, width : 2 * width], 1, 0),
            dot(grad[:, 0:width], down_ref[d], 1, 0),
        ]
        for part, term in enumerate(terms):
            if d == 0:
                acc_ref[part] = term
            elif d < 3:
                acc_ref[part] += term
            else:
                total = (acc_ref[part] + term).astype(BF16)
                for piece in range(out_ref.shape[0]):
                    out_ref[piece, part * count : (part + 1) * count] = total[
                        :, piece * 128 : (piece + 1) * 128
                    ]


def point_kernel(parts_ref, out_ref):
    count = out_ref.shape[0] // 3
    total = jnp.sum(parts_ref[...].astype(F32), axis=0)
    gate, up, grad = total[0:count], total[count : 2 * count], total[2 * count :]
    sigma = jax.nn.sigmoid(gate)
    out_ref[0:count] = (gate * sigma * up).astype(BF16)
    out_ref[count : 2 * count] = (grad * up * sigma * (1.0 + gate * (1.0 - sigma))).astype(BF16)
    out_ref[2 * count :] = (grad * gate * sigma).astype(BF16)


def hidden_parts(act):
    count = act.shape[1] // 3
    return [
        jnp.concatenate([act[k, i * count : (i + 1) * count] for k in range(act.shape[0])], axis=1)
        for i in range(3)
    ]


def result_kernel(x_ref, act_ref, prob_ref, *refs):
    sources, (out_ref, res_ref, tmp_ref, gate_ref, down_ref, sems) = refs[:6], refs[6:]
    copies = panel_copies(x_ref, sources, gate_ref, down_ref, sems)
    width = down_ref.shape[1]
    hidden, gate_grad, up_grad = hidden_parts(act_ref)
    res_ref[...] = jnp.zeros_like(res_ref)
    for d, step in enumerate(STEPS):
        for copy in copies[d]:
            copy.wait()
        outcome = prob_ref[:, 0:1] * dot(hidden, down_ref[d], 1, 1)
        dx = dot(gate_grad, gate_ref[d, 0:width], 1, 1)
        dx += dot(up_grad, gate_ref[d, width : 2 * width], 1, 1)
        res_ref[:, 0:width] = outcome
        res_ref[:, DY_LANE : DY_LANE + width] = dx
        out_ref[lax.rem(x_ref[0] + step, 4)] = split_lanes(tmp_ref, res_ref[...])


def weight_kernel(x_ref, act_ref, *refs):
    row_refs, out_refs, (buf_ref, sems) = refs[:4], refs[4:7], refs[7:]
    width = out_refs[0].shape[0]
    count = row_refs[0].shape[0]
    parts = (1, 2, 0)
    copies = [
        [
            pltpu.make_async_copy(
                act_ref.at[lax.rem(x_ref[0] + 4 - d, 4), :, pl.ds(part * count, count)],
                buf_ref.at[part, d],
                sems.at[part, d],
            )
            for d in range(4)
        ]
        for part in parts
    ]
    for group in copies:
        for copy in group:
            copy.start()
    x, grad = (
        jnp.concatenate([ref[:, lane : lane + width] for ref in row_refs], axis=0)
        for lane in (0, DY_LANE)
    )
    for i, part in enumerate(parts):
        for copy in copies[i]:
            copy.wait()
        right = jnp.concatenate(
            [
                jnp.concatenate([buf_ref[part, d, k] for k in range(buf_ref.shape[2])], axis=1)
                for d in range(4)
            ],
            axis=0,
        )
        out_refs[i][...] = dot(grad if part == 0 else x, right, 0, 0).astype(BF16)


def combine_kernel(pick_ref, tiles_ref, out_ref, tmp_ref):
    rows = join_lanes(tmp_ref, tiles_ref[...]).astype(BF16)
    out_ref[...] = dot(pick_ref[...], rows, 0, 0).astype(BF16)


def unpack_kernel(rows_ref, out_ref, dx_ref):
    result = dot(rows_ref[...], token_permutation(LANES), 0, 0).astype(BF16)
    out_ref[...] = result[0:P_LANE]
    dx_ref[...] = result[DY_LANE : DY_LANE + P_LANE]


def routing_info(expert_slot, block_counts, entries, share_x):
    groups, experts = block_counts.shape
    ids = jnp.arange(experts, dtype=jnp.int32)
    slot_is = (expert_slot[:, None] == ids[None, :]).astype(jnp.int32)
    slot_expert = jnp.sum(slot_is * ids[:, None], axis=0)
    counts = jnp.sum(block_counts[:, :, None] * slot_is[None], axis=1)
    used = (counts > 0).astype(jnp.int32)
    before = (ids[:, None] < ids[None, :]).astype(jnp.int32)
    rank = jnp.sum(used[:, None, :] * before[:, :, None], axis=0)
    user_ids = jnp.arange(USERS, dtype=jnp.int32)[:, None, None]
    chosen = used[None] * (rank[None] == user_ids).astype(jnp.int32)
    user_group = jnp.sum(chosen * ids[None, :, None], axis=1)
    user_count = jnp.sum(chosen * counts[None], axis=1)
    per_x = USERS * entries * 2 // share_x
    shape = (share_x, groups, per_x)
    member = lax.broadcasted_iota(jnp.int32, shape, 0) * per_x
    member = member + lax.broadcasted_iota(jnp.int32, shape, 2)
    first = member < entries * 2
    entry = (member >> 1) - jnp.where(first, 0, entries)
    group = jnp.where(first, user_group[0][None, :, None], user_group[1][None, :, None])
    limit = jnp.where(first, user_count[0][None, :, None], user_count[1][None, :, None])
    list_row = group * BLK + slot_expert[None, :, None]
    base = jnp.where(entry < limit, group * BLK + (member & 1), -100000)
    info = jnp.stack([list_row, base, entry + LIST_LANE], axis=-1)
    return info.reshape(-1, 3)


def exchange(array, axis):
    return lax.all_to_all(array, axis, split_axis=0, concat_axis=0, tiled=True)


def body(
    tokens, grad_output, gate_prob, w_gate, w_up, w_down, expert_slot, block_counts, block_lists
):
    groups = lax.axis_size(GROUP)
    share_y = lax.axis_size("y")
    share_x = lax.axis_size("x")
    width = tokens.shape[1]
    hid = w_gate.shape[2]
    entries = block_lists.shape[2]
    picked = USERS * entries * 2
    total = groups * picked
    count = total // share_x

    me_x = lax.axis_index("x")
    order = me_x[None].astype(jnp.int32)
    shifts = [[(i, (i + d) % share_x) for i in range(share_x)] for d in range(share_x)]

    def shift(array, d):
        return lax.ppermute(array, "x", shifts[d])

    gates = jnp.concatenate([w_gate[0], w_up[0]], axis=0)
    gates = lax.all_gather(gates, "x", axis=0, tiled=False)
    down = w_down[0].T

    packed = call(
        pack_kernel,
        jax.ShapeDtypeStruct((groups, BLK, LANES), BF16),
        (tokens.T, grad_output.T, gate_prob.T, block_lists.transpose(2, 0, 1)),
        VMEM_LARGE,
        scratch_shapes=[pltpu.VMEM((LANES, LANES), BF16)],
    )
    info = routing_info(expert_slot, block_counts, entries, share_x)
    mine = (expert_slot == lax.axis_index(GROUP)).astype(F32)
    mark = lax.pad(mine, jnp.zeros((), F32), ((P_LANE, 16, 0),))[None]
    spread = exchange(packed, GROUP).reshape(groups * BLK, LANES)
    info, down_late = lax.optimization_barrier((info, down))
    right, left = shift(down_late, 1), shift(down_late, 3)
    spread, info = lax.optimization_barrier((spread, info))
    sent, pick = call(
        select_kernel,
        (
            jax.ShapeDtypeStruct((4 * total, 128), BF16),
            jax.ShapeDtypeStruct((total, groups * BLK), BF16),
        ),
        (spread, info),
        scratch_shapes=[pltpu.VMEM((4 * total, 128), F32)],
    )
    sent, right, left = lax.optimization_barrier((sent, right, left))
    half = hid // 2
    panels = [gates, down, right, left, shift(right[:, 0:half], 1), shift(left[:, half:], 3)]
    pieces = (share_x * groups, 4 * picked // share_x, 128)
    tiles = exchange(sent.reshape(pieces), OWNERS).reshape(share_x, 4 * count, 128)

    act_shape = (share_y, 3 * count, hid // share_y)
    scalar_spec = pl.BlockSpec(memory_space=pltpu.SMEM)
    vmem_spec = pl.BlockSpec(memory_space=pltpu.VMEM)
    panel_specs = [pl.BlockSpec(memory_space=pl.ANY)] * 6
    panel_scratch = [
        pltpu.VMEM((4, 2 * width, hid), BF16),
        pltpu.VMEM((4, width, hid), BF16),
        pltpu.SemaphoreType.DMA((9,)),
    ]
    *rows, parts, prob = call(
        hidden_kernel,
        (jax.ShapeDtypeStruct((count, LANES), BF16),) * 4
        + (jax.ShapeDtypeStruct(act_shape, BF16), jax.ShapeDtypeStruct((count, 128), F32)),
        (order, tiles, mark, *panels),
        VMEM_LARGE,
        in_specs=[scalar_spec, vmem_spec, vmem_spec] + panel_specs,
        scratch_shapes=[pltpu.VMEM((3, count, hid), F32), pltpu.VMEM((4 * count, 128), F32)]
        + panel_scratch,
    )
    parts = exchange(parts, "y")
    rows = [shift(rows[d], STEPS[d]) if STEPS[d] else rows[d] for d in range(share_x)]
    parts, *rows = lax.optimization_barrier((parts, *rows))
    act = call(point_kernel, jax.ShapeDtypeStruct(act_shape[1:], BF16), (parts,))
    act = lax.all_gather(act, "y", axis=0, tiled=False)
    all_act = lax.all_gather(act, "x", axis=0, tiled=False)
    results = call(
        result_kernel,
        jax.ShapeDtypeStruct((share_x, 4 * count, 128), BF16),
        (order, act, prob, *panels),
        VMEM_LARGE,
        in_specs=[scalar_spec, vmem_spec, vmem_spec] + panel_specs,
        scratch_shapes=[pltpu.VMEM((count, LANES), F32), pltpu.VMEM((4 * count, 128), F32)]
        + panel_scratch,
    )
    weights = call(
        weight_kernel,
        (jax.ShapeDtypeStruct((width, hid), BF16),) * 3,
        (order, all_act, *(rows[STEPS.index(d)] for d in range(share_x))),
        VMEM_LARGE,
        in_specs=[scalar_spec, panel_specs[0]] + [vmem_spec] * 4,
        scratch_shapes=[
            pltpu.VMEM((3, share_x, share_y, count, hid // share_y), BF16),
            pltpu.SemaphoreType.DMA((3, share_x)),
        ],
    )
    back = exchange(results.reshape(pieces), OWNERS).reshape(4 * total, 128)
    summed = call(
        combine_kernel,
        jax.ShapeDtypeStruct((groups * BLK, LANES), BF16),
        (pick, back),
        scratch_shapes=[pltpu.VMEM((4 * total, 128), F32)],
    )
    home = exchange(summed.reshape(groups, BLK, LANES), GROUP).reshape(groups * BLK, LANES)
    out, dx = call(
        unpack_kernel,
        (jax.ShapeDtypeStruct((width, groups * BLK), BF16),) * 2,
        (home,),
    )
    return (
        out.T,
        dx.T,
        weights[0][None],
        weights[1][None],
        weights[2].T[None],
    )


def solution(mesh):
    devices = mesh.devices.reshape(8, 2, 8, 4)
    inner = Mesh(devices, ("z", "core", "y", "x"))
    member = ("y", "x")
    in_specs = (
        P(GROUP, member),
        P(GROUP, member),
        P(GROUP, None),
        P(GROUP, member, None),
        P(GROUP, member, None),
        P(GROUP, None, member),
        P(),
        P(),
        P(GROUP, None, None),
    )
    out_specs = (
        P(GROUP, member),
        P(GROUP, member),
        P(GROUP, member, None),
        P(GROUP, member, None),
        P(GROUP, None, member),
    )
    return jax.shard_map(body, mesh=inner, in_specs=in_specs, out_specs=out_specs, check_vma=False)
```

```python
import jax
import jax.numpy as jnp
from jax import lax
from jax.experimental import pallas as pl
from jax.experimental.pallas import tpu as pltpu
from jax.sharding import Mesh, PartitionSpec as P

BLK = 32
USERS = 2
LANES = 512
STEPS = (0, 3, 1, 2)
P_LANE = 224
DY_LANE = 256
LIST_LANE = 480
GROUP = ("z", "core")
OWNERS = ("x", "z", "core")
F32 = jnp.float32
BF16 = jnp.bfloat16
VMEM_LIMIT = 24 * 1024 * 1024
VMEM_LARGE = 56 * 1024 * 1024


def dot(a, b, ca, cb):
    return lax.dot_general(a, b, (((ca,), (cb,)), ((), ())), preferred_element_type=F32)


def call(kernel, out_shape, args, limit=VMEM_LIMIT, **kw):
    return pl.pallas_call(
        kernel,
        out_shape=out_shape,
        compiler_params=pltpu.CompilerParams(vmem_limit_bytes=limit),
        **kw,
    )(*args)


def token_permutation(rows):
    o = lax.broadcasted_iota(jnp.int32, (rows, rows), 0)
    t = lax.broadcasted_iota(jnp.int32, (rows, rows), 1)
    source = ((o >> 1) & 15) * BLK + (o >> 5) * 2 + (o & 1)
    return (t == source).astype(BF16)


def pack_kernel(tok_ref, dy_ref, prob_ref, list_ref, out_ref, all_ref):
    width = tok_ref.shape[0]
    all_ref[...] = jnp.zeros_like(all_ref)
    all_ref[0:width] = tok_ref[...]
    all_ref[P_LANE : P_LANE + 16] = prob_ref[...]
    all_ref[DY_LANE : DY_LANE + width] = dy_ref[...]
    packed = dot(token_permutation(LANES), all_ref[...], 1, 1)
    lists = list_ref[:, 0, :].astype(F32).astype(BF16)
    entry = lax.broadcasted_iota(jnp.int32, (lists.shape[0], LANES), 0)
    lane = lax.broadcasted_iota(jnp.int32, (lists.shape[0], LANES), 1)
    lists = dot(lists, (lane == entry + LIST_LANE).astype(BF16), 0, 0)
    lists = jnp.concatenate([lists, jnp.zeros((BLK - lists.shape[0], LANES), F32)], axis=0)
    out_ref[...] = (packed.reshape(out_ref.shape) + lists[None]).astype(BF16)


def split_lanes(tmp_ref, rows):
    count = rows.shape[0]
    for c in range(4):
        tmp_ref[pl.ds(c, count, stride=4), :] = rows[:, c * 128 : (c + 1) * 128]
    return tmp_ref[...].astype(BF16)


def join_lanes(tmp_ref, tiles):
    tmp_ref[...] = tiles.astype(F32)
    count = tmp_ref.shape[0] // 4
    return jnp.concatenate([tmp_ref[pl.ds(c, count, stride=4), :] for c in range(4)], axis=1)


def select_kernel(rows_ref, info_ref, out_ref, pick_ref, tmp_ref):
    rows = rows_ref[...]
    total = info_ref.shape[0]
    columns = lax.broadcasted_iota(jnp.int32, (total, rows.shape[0]), 1)
    list_rows = (columns == info_ref[:, 0:1]).astype(BF16)
    lists = dot(list_rows, rows[:, 384:512], 1, 0)
    lanes = lax.broadcasted_iota(jnp.int32, lists.shape, 1) + 384
    block = jnp.sum(jnp.where(lanes == info_ref[:, 2:3], lists, 0.0), axis=1, keepdims=True)
    column = info_ref[:, 1:2] + 2 * block.astype(jnp.int32)
    pick = (columns == column).astype(BF16)
    pick_ref[...] = pick
    out_ref[...] = split_lanes(tmp_ref, dot(pick, rows, 1, 0))


def panel_copies(x_ref, sources, gate_ref, down_ref, sems):
    half = down_ref.shape[2] // 2
    pairs = []
    for d, step in enumerate(STEPS):
        pairs.append((sources[0].at[lax.rem(x_ref[0] + step, 4)], gate_ref.at[d]))
        if d < 3:
            pairs.append((sources[1 + d], down_ref.at[d]))
    for i in range(2):
        pairs.append((sources[4 + i], down_ref.at[3, :, pl.ds(i * half, half)]))
    copies = [
        pltpu.make_async_copy(source, target, sems.at[i])
        for i, (source, target) in enumerate(pairs)
    ]
    for copy in copies:
        copy.start()
    return [copies[0:2], copies[2:4], copies[4:6], copies[6:9]]


def hidden_kernel(x_ref, tiles_ref, mark_ref, *refs):
    sources, row_refs = refs[:6], refs[6:10]
    out_ref, prob_ref, acc_ref, tmp_ref, gate_ref, down_ref, sems = refs[10:]
    copies = panel_copies(x_ref, sources, gate_ref, down_ref, sems)
    width = down_ref.shape[1]
    parts, count = acc_ref.shape[:2]
    for d, step in enumerate(STEPS):
        rows = join_lanes(tmp_ref, tiles_ref[lax.rem(x_ref[0] + step, 4)])
        prob = jnp.sum(rows[:, 0:256] * mark_ref[...], axis=1, keepdims=True)
        x = rows[:, 0:256].astype(BF16)
        grad = (prob * rows[:, DY_LANE:LANES]).astype(BF16)
        row_refs[d][:, 0:DY_LANE] = x
        row_refs[d][:, DY_LANE:LANES] = grad
        if d == 0:
            prob_ref[...] = jnp.broadcast_to(prob, prob_ref.shape)
        for copy in copies[d]:
            copy.wait()
        terms = [
            dot(x[:, 0:width], gate_ref[d, 0:width], 1, 0),
            dot(x[:, 0:width], gate_ref[d, width : 2 * width], 1, 0),
            dot(grad[:, 0:width], down_ref[d], 1, 0),
        ]
        for part, term in enumerate(terms):
            if d == 0:
                acc_ref[part] = term
            elif d < 3:
                acc_ref[part] += term
            else:
                total = (acc_ref[part] + term).astype(BF16)
                for piece in range(out_ref.shape[0]):
                    out_ref[piece, part * count : (part + 1) * count] = total[
                        :, piece * 128 : (piece + 1) * 128
                    ]


def point_kernel(parts_ref, out_ref):
    count = out_ref.shape[0] // 3
    total = jnp.sum(parts_ref[...].astype(F32), axis=0)
    gate, up, grad = total[0:count], total[count : 2 * count], total[2 * count :]
    sigma = jax.nn.sigmoid(gate)
    out_ref[0:count] = (gate * sigma * up).astype(BF16)
    out_ref[count : 2 * count] = (grad * up * sigma * (1.0 + gate * (1.0 - sigma))).astype(BF16)
    out_ref[2 * count :] = (grad * gate * sigma).astype(BF16)


def hidden_parts(act):
    count = act.shape[1] // 3
    return [
        jnp.concatenate([act[k, i * count : (i + 1) * count] for k in range(act.shape[0])], axis=1)
        for i in range(3)
    ]


def result_kernel(x_ref, act_ref, prob_ref, *refs):
    sources, (out_ref, res_ref, tmp_ref, gate_ref, down_ref, sems) = refs[:6], refs[6:]
    copies = panel_copies(x_ref, sources, gate_ref, down_ref, sems)
    width = down_ref.shape[1]
    hidden, gate_grad, up_grad = hidden_parts(act_ref)
    res_ref[...] = jnp.zeros_like(res_ref)
    for d, step in enumerate(STEPS):
        for copy in copies[d]:
            copy.wait()
        outcome = prob_ref[:, 0:1] * dot(hidden, down_ref[d], 1, 1)
        dx = dot(gate_grad, gate_ref[d, 0:width], 1, 1)
        dx += dot(up_grad, gate_ref[d, width : 2 * width], 1, 1)
        res_ref[:, 0:width] = outcome
        res_ref[:, DY_LANE : DY_LANE + width] = dx
        out_ref[lax.rem(x_ref[0] + step, 4)] = split_lanes(tmp_ref, res_ref[...])


def weight_kernel(x_ref, act_ref, *refs):
    row_refs, out_refs, (buf_ref, sems) = refs[:4], refs[4:7], refs[7:]
    width = out_refs[0].shape[0]
    count = row_refs[0].shape[0]
    parts = (1, 2, 0)
    copies = [
        [
            pltpu.make_async_copy(
                act_ref.at[lax.rem(x_ref[0] + 4 - d, 4), :, pl.ds(part * count, count)],
                buf_ref.at[part, d],
                sems.at[part, d],
            )
            for d in range(4)
        ]
        for part in parts
    ]
    for group in copies:
        for copy in group:
            copy.start()
    x, grad = (
        jnp.concatenate([ref[:, lane : lane + width] for ref in row_refs], axis=0)
        for lane in (0, DY_LANE)
    )
    for i, part in enumerate(parts):
        for copy in copies[i]:
            copy.wait()
        right = jnp.concatenate(
            [
                jnp.concatenate([buf_ref[part, d, k] for k in range(buf_ref.shape[2])], axis=1)
                for d in range(4)
            ],
            axis=0,
        )
        out_refs[i][...] = dot(grad if part == 0 else x, right, 0, 0).astype(BF16)


def combine_kernel(pick_ref, tiles_ref, out_ref, tmp_ref):
    rows = join_lanes(tmp_ref, tiles_ref[...]).astype(BF16)
    out_ref[...] = dot(pick_ref[...], rows, 0, 0).astype(BF16)


def unpack_kernel(rows_ref, out_ref, dx_ref):
    result = dot(rows_ref[...], token_permutation(LANES), 0, 0).astype(BF16)
    out_ref[...] = result[0:P_LANE]
    dx_ref[...] = result[DY_LANE : DY_LANE + P_LANE]


def routing_info(expert_slot, block_counts, entries, share_x):
    groups, experts = block_counts.shape
    ids = jnp.arange(experts, dtype=jnp.int32)
    slot_is = (expert_slot[:, None] == ids[None, :]).astype(jnp.int32)
    slot_expert = jnp.sum(slot_is * ids[:, None], axis=0)
    counts = jnp.sum(block_counts[:, :, None] * slot_is[None], axis=1)
    used = (counts > 0).astype(jnp.int32)
    before = (ids[:, None] < ids[None, :]).astype(jnp.int32)
    rank = jnp.sum(used[:, None, :] * before[:, :, None], axis=0)
    user_ids = jnp.arange(USERS, dtype=jnp.int32)[:, None, None]
    chosen = used[None] * (rank[None] == user_ids).astype(jnp.int32)
    user_group = jnp.sum(chosen * ids[None, :, None], axis=1)
    user_count = jnp.sum(chosen * counts[None], axis=1)
    per_x = USERS * entries * 2 // share_x
    shape = (share_x, groups, per_x)
    member = lax.broadcasted_iota(jnp.int32, shape, 0) * per_x
    member = member + lax.broadcasted_iota(jnp.int32, shape, 2)
    first = member < entries * 2
    entry = (member >> 1) - jnp.where(first, 0, entries)
    group = jnp.where(first, user_group[0][None, :, None], user_group[1][None, :, None])
    limit = jnp.where(first, user_count[0][None, :, None], user_count[1][None, :, None])
    list_row = group * BLK + slot_expert[None, :, None]
    base = jnp.where(entry < limit, group * BLK + (member & 1), -100000)
    info = jnp.stack([list_row, base, entry + LIST_LANE], axis=-1)
    return info.reshape(-1, 3)


def exchange(array, axis):
    return lax.all_to_all(array, axis, split_axis=0, concat_axis=0, tiled=True)


def body(
    tokens, grad_output, gate_prob, w_gate, w_up, w_down, expert_slot, block_counts, block_lists
):
    groups = lax.axis_size(GROUP)
    share_y = lax.axis_size("y")
    share_x = lax.axis_size("x")
    width = tokens.shape[1]
    hid = w_gate.shape[2]
    entries = block_lists.shape[2]
    picked = USERS * entries * 2
    total = groups * picked
    count = total // share_x

    me_x = lax.axis_index("x")
    order = me_x[None].astype(jnp.int32)
    shifts = [[(i, (i + d) % share_x) for i in range(share_x)] for d in range(share_x)]

    def shift(array, d):
        return lax.ppermute(array, "x", shifts[d])

    gates = jnp.concatenate([w_gate[0], w_up[0]], axis=0)
    gates = lax.all_gather(gates, "x", axis=0, tiled=False)
    down = w_down[0].T
    right, left = shift(down, 1), shift(down, 3)

    packed = call(
        pack_kernel,
        jax.ShapeDtypeStruct((groups, BLK, LANES), BF16),
        (tokens.T, grad_output.T, gate_prob.T, block_lists.transpose(2, 0, 1)),
        VMEM_LARGE,
        scratch_shapes=[pltpu.VMEM((LANES, LANES), BF16)],
    )
    info = routing_info(expert_slot, block_counts, entries, share_x)
    mine = (expert_slot == lax.axis_index(GROUP)).astype(F32)
    mark = lax.pad(mine, jnp.zeros((), F32), ((P_LANE, 16, 0),))[None]
    spread = exchange(packed, GROUP).reshape(groups * BLK, LANES)
    spread, info, right, left = lax.optimization_barrier((spread, info, right, left))
    sent, pick = call(
        select_kernel,
        (
            jax.ShapeDtypeStruct((4 * total, 128), BF16),
            jax.ShapeDtypeStruct((total, groups * BLK), BF16),
        ),
        (spread, info),
        scratch_shapes=[pltpu.VMEM((4 * total, 128), F32)],
    )
    half = hid // 2
    panels = [gates, down, right, left, shift(right[:, 0:half], 1), shift(left[:, half:], 3)]
    pieces = (share_x * groups, 4 * picked // share_x, 128)
    tiles = exchange(sent.reshape(pieces), OWNERS).reshape(share_x, 4 * count, 128)

    act_shape = (share_y, 3 * count, hid // share_y)
    scalar_spec = pl.BlockSpec(memory_space=pltpu.SMEM)
    vmem_spec = pl.BlockSpec(memory_space=pltpu.VMEM)
    panel_specs = [pl.BlockSpec(memory_space=pl.ANY)] * 6
    panel_scratch = [
        pltpu.VMEM((4, 2 * width, hid), BF16),
        pltpu.VMEM((4, width, hid), BF16),
        pltpu.SemaphoreType.DMA((9,)),
    ]
    *rows, parts, prob = call(
        hidden_kernel,
        (jax.ShapeDtypeStruct((count, LANES), BF16),) * 4
        + (jax.ShapeDtypeStruct(act_shape, BF16), jax.ShapeDtypeStruct((count, 128), F32)),
        (order, tiles, mark, *panels),
        VMEM_LARGE,
        in_specs=[scalar_spec, vmem_spec, vmem_spec] + panel_specs,
        scratch_shapes=[pltpu.VMEM((3, count, hid), F32), pltpu.VMEM((4 * count, 128), F32)]
        + panel_scratch,
    )
    parts = exchange(parts, "y")
    rows = [shift(rows[d], STEPS[d]) if STEPS[d] else rows[d] for d in range(share_x)]
    parts, *rows = lax.optimization_barrier((parts, *rows))
    act = call(point_kernel, jax.ShapeDtypeStruct(act_shape[1:], BF16), (parts,))
    act = lax.all_gather(act, "y", axis=0, tiled=False)
    all_act = lax.all_gather(act, "x", axis=0, tiled=False)
    results = call(
        result_kernel,
        jax.ShapeDtypeStruct((share_x, 4 * count, 128), BF16),
        (order, act, prob, *panels),
        VMEM_LARGE,
        in_specs=[scalar_spec, vmem_spec, vmem_spec] + panel_specs,
        scratch_shapes=[pltpu.VMEM((count, LANES), F32), pltpu.VMEM((4 * count, 128), F32)]
        + panel_scratch,
    )
    weights = call(
        weight_kernel,
        (jax.ShapeDtypeStruct((width, hid), BF16),) * 3,
        (order, all_act, *(rows[STEPS.index(d)] for d in range(share_x))),
        VMEM_LARGE,
        in_specs=[scalar_spec, panel_specs[0]] + [vmem_spec] * 4,
        scratch_shapes=[
            pltpu.VMEM((3, share_x, share_y, count, hid // share_y), BF16),
            pltpu.SemaphoreType.DMA((3, share_x)),
        ],
    )
    back = exchange(results.reshape(pieces), OWNERS).reshape(4 * total, 128)
    summed = call(
        combine_kernel,
        jax.ShapeDtypeStruct((groups * BLK, LANES), BF16),
        (pick, back),
        scratch_shapes=[pltpu.VMEM((4 * total, 128), F32)],
    )
    home = exchange(summed.reshape(groups, BLK, LANES), GROUP).reshape(groups * BLK, LANES)
    home, *weights = lax.optimization_barrier((home, *weights))
    out, dx = call(
        unpack_kernel,
        (jax.ShapeDtypeStruct((width, groups * BLK), BF16),) * 2,
        (home,),
    )
    return (
        out.T,
        dx.T,
        weights[0][None],
        weights[1][None],
        weights[2].T[None],
    )


def solution(mesh):
    devices = mesh.devices.reshape(8, 2, 8, 4)
    inner = Mesh(devices, ("z", "core", "y", "x"))
    member = ("y", "x")
    in_specs = (
        P(GROUP, member),
        P(GROUP, member),
        P(GROUP, None),
        P(GROUP, member, None),
        P(GROUP, member, None),
        P(GROUP, None, member),
        P(),
        P(),
        P(GROUP, None, None),
    )
    out_specs = (
        P(GROUP, member),
        P(GROUP, member),
        P(GROUP, member, None),
        P(GROUP, member, None),
        P(GROUP, None, member),
    )
    return jax.shard_map(body, mesh=inner, in_specs=in_specs, out_specs=out_specs, check_vma=False)
```

```python
import jax
import jax.numpy as jnp
from jax import lax
from jax.experimental import pallas as pl
from jax.experimental.pallas import tpu as pltpu
from jax.sharding import Mesh, PartitionSpec as P

BLK = 32
USERS = 2
LANES = 512
STEPS = (0, 3, 1, 2)
P_LANE = 224
DY_LANE = 256
LIST_LANE = 480
GROUP = ("z", "core")
OWNERS = ("x", "z", "core")
F32 = jnp.float32
BF16 = jnp.bfloat16
VMEM_LIMIT = 24 * 1024 * 1024
VMEM_LARGE = 56 * 1024 * 1024


def dot(a, b, ca, cb):
    return lax.dot_general(a, b, (((ca,), (cb,)), ((), ())), preferred_element_type=F32)


def call(kernel, out_shape, args, limit=VMEM_LIMIT, **kw):
    return pl.pallas_call(
        kernel,
        out_shape=out_shape,
        compiler_params=pltpu.CompilerParams(vmem_limit_bytes=limit),
        **kw,
    )(*args)


def token_permutation(rows):
    o = lax.broadcasted_iota(jnp.int32, (rows, rows), 0)
    t = lax.broadcasted_iota(jnp.int32, (rows, rows), 1)
    source = ((o >> 1) & 15) * BLK + (o >> 5) * 2 + (o & 1)
    return (t == source).astype(BF16)


def pack_kernel(tok_ref, dy_ref, prob_ref, list_ref, out_ref, all_ref):
    width = tok_ref.shape[0]
    all_ref[...] = jnp.zeros_like(all_ref)
    all_ref[0:width] = tok_ref[...]
    all_ref[P_LANE : P_LANE + 16] = prob_ref[...]
    all_ref[DY_LANE : DY_LANE + width] = dy_ref[...]
    packed = dot(token_permutation(LANES), all_ref[...], 1, 1)
    lists = list_ref[:, 0, :].astype(F32).astype(BF16)
    entry = lax.broadcasted_iota(jnp.int32, (lists.shape[0], LANES), 0)
    lane = lax.broadcasted_iota(jnp.int32, (lists.shape[0], LANES), 1)
    lists = dot(lists, (lane == entry + LIST_LANE).astype(BF16), 0, 0)
    lists = jnp.concatenate([lists, jnp.zeros((BLK - lists.shape[0], LANES), F32)], axis=0)
    out_ref[...] = (packed.reshape(out_ref.shape) + lists[None]).astype(BF16)


def split_lanes(tmp_ref, rows):
    count = rows.shape[0]
    for c in range(4):
        tmp_ref[pl.ds(c, count, stride=4), :] = rows[:, c * 128 : (c + 1) * 128]
    return tmp_ref[...].astype(BF16)


def join_lanes(tmp_ref, tiles):
    tmp_ref[...] = tiles.astype(F32)
    count = tmp_ref.shape[0] // 4
    return jnp.concatenate([tmp_ref[pl.ds(c, count, stride=4), :] for c in range(4)], axis=1)


def select_kernel(rows_ref, info_ref, out_ref, pick_ref, tmp_ref):
    rows = rows_ref[...]
    total = info_ref.shape[0]
    columns = lax.broadcasted_iota(jnp.int32, (total, rows.shape[0]), 1)
    list_rows = (columns == info_ref[:, 0:1]).astype(BF16)
    lists = dot(list_rows, rows[:, 384:512], 1, 0)
    lanes = lax.broadcasted_iota(jnp.int32, lists.shape, 1) + 384
    block = jnp.sum(jnp.where(lanes == info_ref[:, 2:3], lists, 0.0), axis=1, keepdims=True)
    column = info_ref[:, 1:2] + 2 * block.astype(jnp.int32)
    pick = (columns == column).astype(BF16)
    pick_ref[...] = pick
    out_ref[...] = split_lanes(tmp_ref, dot(pick, rows, 1, 0))


def join_kernel(gate_ref, up_ref, out_ref, buf_ref, sems):
    width = gate_ref.shape[0]
    half = width // 2
    loads, stores = [], []
    for i in range(4):
        source = (gate_ref, up_ref)[i // 2].at[pl.ds(i % 2 * half, half)]
        rows = pl.ds(i * half, half)
        loads.append(pltpu.make_async_copy(source, buf_ref.at[rows], sems.at[0, i]))
        stores.append(pltpu.make_async_copy(buf_ref.at[rows], out_ref.at[rows], sems.at[1, i]))
    for load in loads:
        load.start()
    for load, store in zip(loads, stores):
        load.wait()
        store.start()
    for store in stores:
        store.wait()


def panel_copies(x_ref, sources, gate_ref, down_ref, sems):
    half = down_ref.shape[2] // 2
    pairs = []
    for d, step in enumerate(STEPS):
        pairs.append((sources[0].at[lax.rem(x_ref[0] + step, 4)], gate_ref.at[d]))
        if d < 3:
            pairs.append((sources[1 + d], down_ref.at[d]))
    for i in range(2):
        pairs.append((sources[4 + i], down_ref.at[3, :, pl.ds(i * half, half)]))
    copies = [
        pltpu.make_async_copy(source, target, sems.at[i])
        for i, (source, target) in enumerate(pairs)
    ]
    for copy in copies:
        copy.start()
    return [copies[0:2], copies[2:4], copies[4:6], copies[6:9]]


def hidden_kernel(x_ref, tiles_ref, mark_ref, *refs):
    sources, row_refs = refs[:6], refs[6:10]
    out_ref, prob_ref, acc_ref, tmp_ref, gate_ref, down_ref, sems = refs[10:]
    copies = panel_copies(x_ref, sources, gate_ref, down_ref, sems)
    width = down_ref.shape[1]
    parts, count = acc_ref.shape[:2]
    for d, step in enumerate(STEPS):
        rows = join_lanes(tmp_ref, tiles_ref[lax.rem(x_ref[0] + step, 4)])
        prob = jnp.sum(rows[:, 0:256] * mark_ref[...], axis=1, keepdims=True)
        x = rows[:, 0:256].astype(BF16)
        grad = (prob * rows[:, DY_LANE:LANES]).astype(BF16)
        row_refs[d][:, 0:DY_LANE] = x
        row_refs[d][:, DY_LANE:LANES] = grad
        if d == 0:
            prob_ref[...] = jnp.broadcast_to(prob, prob_ref.shape)
        for copy in copies[d]:
            copy.wait()
        terms = [
            dot(x[:, 0:width], gate_ref[d, 0:width], 1, 0),
            dot(x[:, 0:width], gate_ref[d, width : 2 * width], 1, 0),
            dot(grad[:, 0:width], down_ref[d], 1, 0),
        ]
        for part, term in enumerate(terms):
            if d == 0:
                acc_ref[part] = term
            elif d < 3:
                acc_ref[part] += term
            else:
                total = (acc_ref[part] + term).astype(BF16)
                for piece in range(out_ref.shape[0]):
                    out_ref[piece, part * count : (part + 1) * count] = total[
                        :, piece * 128 : (piece + 1) * 128
                    ]


def point_kernel(parts_ref, out_ref):
    count = out_ref.shape[0] // 3
    total = jnp.sum(parts_ref[...].astype(F32), axis=0)
    gate, up, grad = total[0:count], total[count : 2 * count], total[2 * count :]
    sigma = jax.nn.sigmoid(gate)
    out_ref[0:count] = (gate * sigma * up).astype(BF16)
    out_ref[count : 2 * count] = (grad * up * sigma * (1.0 + gate * (1.0 - sigma))).astype(BF16)
    out_ref[2 * count :] = (grad * gate * sigma).astype(BF16)


def hidden_parts(act):
    count = act.shape[1] // 3
    return [
        jnp.concatenate([act[k, i * count : (i + 1) * count] for k in range(act.shape[0])], axis=1)
        for i in range(3)
    ]


def result_kernel(x_ref, act_ref, prob_ref, *refs):
    sources, (out_ref, res_ref, tmp_ref, gate_ref, down_ref, sems) = refs[:6], refs[6:]
    copies = panel_copies(x_ref, sources, gate_ref, down_ref, sems)
    width = down_ref.shape[1]
    hidden, gate_grad, up_grad = hidden_parts(act_ref)
    res_ref[...] = jnp.zeros_like(res_ref)
    for d, step in enumerate(STEPS):
        for copy in copies[d]:
            copy.wait()
        outcome = prob_ref[:, 0:1] * dot(hidden, down_ref[d], 1, 1)
        dx = dot(gate_grad, gate_ref[d, 0:width], 1, 1)
        dx += dot(up_grad, gate_ref[d, width : 2 * width], 1, 1)
        res_ref[:, 0:width] = outcome
        res_ref[:, DY_LANE : DY_LANE + width] = dx
        out_ref[lax.rem(x_ref[0] + step, 4)] = split_lanes(tmp_ref, res_ref[...])


def weight_kernel(x_ref, act_ref, *refs):
    row_refs, out_refs, (buf_ref, sems) = refs[:4], refs[4:7], refs[7:]
    width = out_refs[0].shape[0]
    count = row_refs[0].shape[0]
    parts = (1, 2, 0)
    copies = [
        [
            pltpu.make_async_copy(
                act_ref.at[lax.rem(x_ref[0] + 4 - d, 4), :, pl.ds(part * count, count)],
                buf_ref.at[part, d],
                sems.at[part, d],
            )
            for d in range(4)
        ]
        for part in parts
    ]
    for group in copies:
        for copy in group:
            copy.start()
    x, grad = (
        jnp.concatenate([ref[:, lane : lane + width] for ref in row_refs], axis=0)
        for lane in (0, DY_LANE)
    )
    for i, part in enumerate(parts):
        for copy in copies[i]:
            copy.wait()
        right = jnp.concatenate(
            [
                jnp.concatenate([buf_ref[part, d, k] for k in range(buf_ref.shape[2])], axis=1)
                for d in range(4)
            ],
            axis=0,
        )
        out_refs[i][...] = dot(grad if part == 0 else x, right, 0, 0).astype(BF16)


def combine_kernel(pick_ref, tiles_ref, out_ref, tmp_ref):
    rows = join_lanes(tmp_ref, tiles_ref[...]).astype(BF16)
    out_ref[...] = dot(pick_ref[...], rows, 0, 0).astype(BF16)


def unpack_kernel(rows_ref, out_ref, dx_ref):
    result = dot(rows_ref[...], token_permutation(LANES), 0, 0).astype(BF16)
    out_ref[...] = result[0:P_LANE]
    dx_ref[...] = result[DY_LANE : DY_LANE + P_LANE]


def routing_info(expert_slot, block_counts, entries, share_x):
    groups, experts = block_counts.shape
    ids = jnp.arange(experts, dtype=jnp.int32)
    slot_is = (expert_slot[:, None] == ids[None, :]).astype(jnp.int32)
    slot_expert = jnp.sum(slot_is * ids[:, None], axis=0)
    counts = jnp.sum(block_counts[:, :, None] * slot_is[None], axis=1)
    used = (counts > 0).astype(jnp.int32)
    before = (ids[:, None] < ids[None, :]).astype(jnp.int32)
    rank = jnp.sum(used[:, None, :] * before[:, :, None], axis=0)
    user_ids = jnp.arange(USERS, dtype=jnp.int32)[:, None, None]
    chosen = used[None] * (rank[None] == user_ids).astype(jnp.int32)
    user_group = jnp.sum(chosen * ids[None, :, None], axis=1)
    user_count = jnp.sum(chosen * counts[None], axis=1)
    per_x = USERS * entries * 2 // share_x
    shape = (share_x, groups, per_x)
    member = lax.broadcasted_iota(jnp.int32, shape, 0) * per_x
    member = member + lax.broadcasted_iota(jnp.int32, shape, 2)
    first = member < entries * 2
    entry = (member >> 1) - jnp.where(first, 0, entries)
    group = jnp.where(first, user_group[0][None, :, None], user_group[1][None, :, None])
    limit = jnp.where(first, user_count[0][None, :, None], user_count[1][None, :, None])
    list_row = group * BLK + slot_expert[None, :, None]
    base = jnp.where(entry < limit, group * BLK + (member & 1), -100000)
    info = jnp.stack([list_row, base, entry + LIST_LANE], axis=-1)
    return info.reshape(-1, 3)


def exchange(array, axis):
    return lax.all_to_all(array, axis, split_axis=0, concat_axis=0, tiled=True)


def body(
    tokens, grad_output, gate_prob, w_gate, w_up, w_down, expert_slot, block_counts, block_lists
):
    groups = lax.axis_size(GROUP)
    share_y = lax.axis_size("y")
    share_x = lax.axis_size("x")
    width = tokens.shape[1]
    hid = w_gate.shape[2]
    entries = block_lists.shape[2]
    picked = USERS * entries * 2
    total = groups * picked
    count = total // share_x

    me_x = lax.axis_index("x")
    order = me_x[None].astype(jnp.int32)
    shifts = [[(i, (i + d) % share_x) for i in range(share_x)] for d in range(share_x)]

    def shift(array, d):
        return lax.ppermute(array, "x", shifts[d])

    any_spec = pl.BlockSpec(memory_space=pl.ANY)
    gates = call(
        join_kernel,
        jax.ShapeDtypeStruct((2 * width, hid), BF16),
        (w_gate[0], w_up[0]),
        VMEM_LARGE,
        in_specs=[any_spec] * 2,
        out_specs=any_spec,
        scratch_shapes=[pltpu.VMEM((2 * width, hid), BF16), pltpu.SemaphoreType.DMA((2, 4))],
    )
    gates = lax.all_gather(gates, "x", axis=0, tiled=False)
    down = w_down[0].T
    right, left = shift(down, 1), shift(down, 3)

    packed = call(
        pack_kernel,
        jax.ShapeDtypeStruct((groups, BLK, LANES), BF16),
        (tokens.T, grad_output.T, gate_prob.T, block_lists.transpose(2, 0, 1)),
        VMEM_LARGE,
        scratch_shapes=[pltpu.VMEM((LANES, LANES), BF16)],
    )
    info = routing_info(expert_slot, block_counts, entries, share_x)
    mine = (expert_slot == lax.axis_index(GROUP)).astype(F32)
    mark = lax.pad(mine, jnp.zeros((), F32), ((P_LANE, 16, 0),))[None]
    spread = exchange(packed, GROUP).reshape(groups * BLK, LANES)
    spread, info, right, left = lax.optimization_barrier((spread, info, right, left))
    sent, pick = call(
        select_kernel,
        (
            jax.ShapeDtypeStruct((4 * total, 128), BF16),
            jax.ShapeDtypeStruct((total, groups * BLK), BF16),
        ),
        (spread, info),
        scratch_shapes=[pltpu.VMEM((4 * total, 128), F32)],
    )
    half = hid // 2
    panels = [gates, down, right, left, shift(right[:, 0:half], 1), shift(left[:, half:], 3)]
    pieces = (share_x * groups, 4 * picked // share_x, 128)
    tiles = exchange(sent.reshape(pieces), OWNERS).reshape(share_x, 4 * count, 128)

    act_shape = (share_y, 3 * count, hid // share_y)
    scalar_spec = pl.BlockSpec(memory_space=pltpu.SMEM)
    vmem_spec = pl.BlockSpec(memory_space=pltpu.VMEM)
    panel_specs = [pl.BlockSpec(memory_space=pl.ANY)] * 6
    panel_scratch = [
        pltpu.VMEM((4, 2 * width, hid), BF16),
        pltpu.VMEM((4, width, hid), BF16),
        pltpu.SemaphoreType.DMA((9,)),
    ]
    *rows, parts, prob = call(
        hidden_kernel,
        (jax.ShapeDtypeStruct((count, LANES), BF16),) * 4
        + (jax.ShapeDtypeStruct(act_shape, BF16), jax.ShapeDtypeStruct((count, 128), F32)),
        (order, tiles, mark, *panels),
        VMEM_LARGE,
        in_specs=[scalar_spec, vmem_spec, vmem_spec] + panel_specs,
        scratch_shapes=[pltpu.VMEM((3, count, hid), F32), pltpu.VMEM((4 * count, 128), F32)]
        + panel_scratch,
    )
    parts = exchange(parts, "y")
    rows = [shift(rows[d], STEPS[d]) if STEPS[d] else rows[d] for d in range(share_x)]
    parts, *rows = lax.optimization_barrier((parts, *rows))
    act = call(point_kernel, jax.ShapeDtypeStruct(act_shape[1:], BF16), (parts,))
    act = lax.all_gather(act, "y", axis=0, tiled=False)
    all_act = lax.all_gather(act, "x", axis=0, tiled=False)
    results = call(
        result_kernel,
        jax.ShapeDtypeStruct((share_x, 4 * count, 128), BF16),
        (order, act, prob, *panels),
        VMEM_LARGE,
        in_specs=[scalar_spec, vmem_spec, vmem_spec] + panel_specs,
        scratch_shapes=[pltpu.VMEM((count, LANES), F32), pltpu.VMEM((4 * count, 128), F32)]
        + panel_scratch,
    )
    weights = call(
        weight_kernel,
        (jax.ShapeDtypeStruct((width, hid), BF16),) * 3,
        (order, all_act, *(rows[STEPS.index(d)] for d in range(share_x))),
        VMEM_LARGE,
        in_specs=[scalar_spec, panel_specs[0]] + [vmem_spec] * 4,
        scratch_shapes=[
            pltpu.VMEM((3, share_x, share_y, count, hid // share_y), BF16),
            pltpu.SemaphoreType.DMA((3, share_x)),
        ],
    )
    back = exchange(results.reshape(pieces), OWNERS).reshape(4 * total, 128)
    summed = call(
        combine_kernel,
        jax.ShapeDtypeStruct((groups * BLK, LANES), BF16),
        (pick, back),
        scratch_shapes=[pltpu.VMEM((4 * total, 128), F32)],
    )
    home = exchange(summed.reshape(groups, BLK, LANES), GROUP).reshape(groups * BLK, LANES)
    home, *weights = lax.optimization_barrier((home, *weights))
    out, dx = call(
        unpack_kernel,
        (jax.ShapeDtypeStruct((width, groups * BLK), BF16),) * 2,
        (home,),
    )
    return (
        out.T,
        dx.T,
        weights[0][None],
        weights[1][None],
        weights[2].T[None],
    )


def solution(mesh):
    devices = mesh.devices.reshape(8, 2, 8, 4)
    inner = Mesh(devices, ("z", "core", "y", "x"))
    member = ("y", "x")
    in_specs = (
        P(GROUP, member),
        P(GROUP, member),
        P(GROUP, None),
        P(GROUP, member, None),
        P(GROUP, member, None),
        P(GROUP, None, member),
        P(),
        P(),
        P(GROUP, None, None),
    )
    out_specs = (
        P(GROUP, member),
        P(GROUP, member),
        P(GROUP, member, None),
        P(GROUP, member, None),
        P(GROUP, None, member),
    )
    return jax.shard_map(body, mesh=inner, in_specs=in_specs, out_specs=out_specs, check_vma=False)
```

```python
import jax
import jax.numpy as jnp
from jax import lax
from jax.experimental import pallas as pl
from jax.experimental.pallas import tpu as pltpu
from jax.sharding import Mesh, PartitionSpec as P

BLK = 32
USERS = 2
LANES = 512
STEPS = (0, 3, 1, 2)
P_LANE = 224
DY_LANE = 256
LIST_LANE = 480
GROUP = ("z", "core")
OWNERS = ("x", "z", "core")
F32 = jnp.float32
BF16 = jnp.bfloat16
VMEM_LIMIT = 24 * 1024 * 1024
VMEM_LARGE = 56 * 1024 * 1024


def dot(a, b, ca, cb):
    return lax.dot_general(a, b, (((ca,), (cb,)), ((), ())), preferred_element_type=F32)


def call(kernel, out_shape, args, limit=VMEM_LIMIT, **kw):
    return pl.pallas_call(
        kernel,
        out_shape=out_shape,
        compiler_params=pltpu.CompilerParams(vmem_limit_bytes=limit),
        **kw,
    )(*args)


def token_permutation(rows):
    o = lax.broadcasted_iota(jnp.int32, (rows, rows), 0)
    t = lax.broadcasted_iota(jnp.int32, (rows, rows), 1)
    source = ((o >> 1) & 15) * BLK + (o >> 5) * 2 + (o & 1)
    return (t == source).astype(BF16)


def pack_kernel(tok_ref, dy_ref, prob_ref, list_ref, out_ref, all_ref):
    width = tok_ref.shape[0]
    all_ref[...] = jnp.zeros_like(all_ref)
    all_ref[0:width] = tok_ref[...]
    all_ref[P_LANE : P_LANE + 16] = prob_ref[...]
    all_ref[DY_LANE : DY_LANE + width] = dy_ref[...]
    packed = dot(token_permutation(LANES), all_ref[...], 1, 1)
    lists = list_ref[:, 0, :].astype(F32).astype(BF16)
    entry = lax.broadcasted_iota(jnp.int32, (lists.shape[0], LANES), 0)
    lane = lax.broadcasted_iota(jnp.int32, (lists.shape[0], LANES), 1)
    lists = dot(lists, (lane == entry + LIST_LANE).astype(BF16), 0, 0)
    lists = jnp.concatenate([lists, jnp.zeros((BLK - lists.shape[0], LANES), F32)], axis=0)
    out_ref[...] = (packed.reshape(out_ref.shape) + lists[None]).astype(BF16)


def split_lanes(tmp_ref, rows):
    count = rows.shape[0]
    for c in range(4):
        tmp_ref[pl.ds(c, count, stride=4), :] = rows[:, c * 128 : (c + 1) * 128]
    return tmp_ref[...].astype(BF16)


def join_lanes(tmp_ref, tiles):
    tmp_ref[...] = tiles.astype(F32)
    count = tmp_ref.shape[0] // 4
    return jnp.concatenate([tmp_ref[pl.ds(c, count, stride=4), :] for c in range(4)], axis=1)


def select_kernel(rows_ref, info_ref, out_ref, pick_ref, tmp_ref):
    rows = rows_ref[...]
    total = info_ref.shape[0]
    columns = lax.broadcasted_iota(jnp.int32, (total, rows.shape[0]), 1)
    list_rows = (columns == info_ref[:, 0:1]).astype(BF16)
    lists = dot(list_rows, rows[:, 384:512], 1, 0)
    lanes = lax.broadcasted_iota(jnp.int32, lists.shape, 1) + 384
    block = jnp.sum(jnp.where(lanes == info_ref[:, 2:3], lists, 0.0), axis=1, keepdims=True)
    column = info_ref[:, 1:2] + 2 * block.astype(jnp.int32)
    pick = (columns == column).astype(BF16)
    pick_ref[...] = pick
    out_ref[...] = split_lanes(tmp_ref, dot(pick, rows, 1, 0))


def panel_copies(x_ref, sources, gate_ref, down_ref, sems):
    half = down_ref.shape[2] // 2
    pairs = []
    for d, step in enumerate(STEPS):
        pairs.append((sources[0].at[lax.rem(x_ref[0] + step, 4)], gate_ref.at[d]))
        if d < 3:
            pairs.append((sources[1 + d], down_ref.at[d]))
    for i in range(2):
        pairs.append((sources[4 + i], down_ref.at[3, :, pl.ds(i * half, half)]))
    copies = [
        pltpu.make_async_copy(source, target, sems.at[i])
        for i, (source, target) in enumerate(pairs)
    ]
    for copy in copies:
        copy.start()
    return [copies[0:2], copies[2:4], copies[4:6], copies[6:9]]


def hidden_kernel(x_ref, tiles_ref, mark_ref, *refs):
    sources, row_refs = refs[:6], refs[6:10]
    out_ref, prob_ref, acc_ref, tmp_ref, gate_ref, down_ref, sems = refs[10:]
    copies = panel_copies(x_ref, sources, gate_ref, down_ref, sems)
    width = down_ref.shape[1]
    parts, count = acc_ref.shape[:2]
    for d, step in enumerate(STEPS):
        rows = join_lanes(tmp_ref, tiles_ref[lax.rem(x_ref[0] + step, 4)])
        prob = jnp.sum(rows[:, 0:256] * mark_ref[...], axis=1, keepdims=True)
        x = rows[:, 0:256].astype(BF16)
        grad = (prob * rows[:, DY_LANE:LANES]).astype(BF16)
        row_refs[d][:, 0:DY_LANE] = x
        row_refs[d][:, DY_LANE:LANES] = grad
        if d == 0:
            prob_ref[...] = jnp.broadcast_to(prob, prob_ref.shape)
        for copy in copies[d]:
            copy.wait()
        terms = [
            dot(x[:, 0:width], gate_ref[d, 0:width], 1, 0),
            dot(x[:, 0:width], gate_ref[d, width : 2 * width], 1, 0),
            dot(grad[:, 0:width], down_ref[d], 1, 0),
        ]
        for part, term in enumerate(terms):
            if d == 0:
                acc_ref[part] = term
            elif d < 3:
                acc_ref[part] += term
            else:
                total = (acc_ref[part] + term).astype(BF16)
                for piece in range(out_ref.shape[0]):
                    out_ref[piece, part * count : (part + 1) * count] = total[
                        :, piece * 128 : (piece + 1) * 128
                    ]


def point_kernel(parts_ref, out_ref):
    count = out_ref.shape[0] // 3
    total = jnp.sum(parts_ref[...].astype(F32), axis=0)
    gate, up, grad = total[0:count], total[count : 2 * count], total[2 * count :]
    sigma = jax.nn.sigmoid(gate)
    out_ref[0:count] = (gate * sigma * up).astype(BF16)
    out_ref[count : 2 * count] = (grad * up * sigma * (1.0 + gate * (1.0 - sigma))).astype(BF16)
    out_ref[2 * count :] = (grad * gate * sigma).astype(BF16)


def hidden_parts(act):
    count = act.shape[1] // 3
    return [
        jnp.concatenate([act[k, i * count : (i + 1) * count] for k in range(act.shape[0])], axis=1)
        for i in range(3)
    ]


def result_kernel(x_ref, act_ref, prob_ref, *refs):
    sources, (out_ref, res_ref, tmp_ref, gate_ref, down_ref, sems) = refs[:6], refs[6:]
    copies = panel_copies(x_ref, sources, gate_ref, down_ref, sems)
    width = down_ref.shape[1]
    hidden, gate_grad, up_grad = hidden_parts(act_ref)
    res_ref[...] = jnp.zeros_like(res_ref)
    for d, step in enumerate(STEPS):
        for copy in copies[d]:
            copy.wait()
        outcome = prob_ref[:, 0:1] * dot(hidden, down_ref[d], 1, 1)
        dx = dot(gate_grad, gate_ref[d, 0:width], 1, 1)
        dx += dot(up_grad, gate_ref[d, width : 2 * width], 1, 1)
        res_ref[:, 0:width] = outcome
        res_ref[:, DY_LANE : DY_LANE + width] = dx
        out_ref[lax.rem(x_ref[0] + step, 4)] = split_lanes(tmp_ref, res_ref[...])


def weight_kernel(x_ref, act_ref, *refs):
    sources, out_refs, (buf_ref, row_refs, sems, row_sems) = refs[:4], refs[4:7], refs[7:]
    width = out_refs[0].shape[0]
    count = row_refs.shape[1]
    parts = (1, 2, 0)
    row_copies = [
        pltpu.make_async_copy(sources[d], row_refs.at[d], row_sems.at[d]) for d in range(4)
    ]
    for copy in row_copies:
        copy.start()
    copies = [
        [
            pltpu.make_async_copy(
                act_ref.at[lax.rem(x_ref[0] + 4 - d, 4), :, pl.ds(part * count, count)],
                buf_ref.at[part, d],
                sems.at[part, d],
            )
            for d in range(4)
        ]
        for part in parts
    ]
    for group in copies:
        for copy in group:
            copy.start()
    for copy in row_copies:
        copy.wait()
    x, grad = (
        jnp.concatenate([row_refs[d, :, lane : lane + width] for d in range(4)], axis=0)
        for lane in (0, DY_LANE)
    )
    for i, part in enumerate(parts):
        for copy in copies[i]:
            copy.wait()
        right = jnp.concatenate(
            [
                jnp.concatenate([buf_ref[part, d, k] for k in range(buf_ref.shape[2])], axis=1)
                for d in range(4)
            ],
            axis=0,
        )
        out_refs[i][...] = dot(grad if part == 0 else x, right, 0, 0).astype(BF16)


def combine_kernel(pick_ref, tiles_ref, out_ref, tmp_ref):
    rows = join_lanes(tmp_ref, tiles_ref[...]).astype(BF16)
    out_ref[...] = dot(pick_ref[...], rows, 0, 0).astype(BF16)


def unpack_kernel(rows_ref, out_ref, dx_ref):
    result = dot(rows_ref[...], token_permutation(LANES), 0, 0).astype(BF16)
    out_ref[...] = result[0:P_LANE]
    dx_ref[...] = result[DY_LANE : DY_LANE + P_LANE]


def routing_info(expert_slot, block_counts, entries, share_x):
    groups, experts = block_counts.shape
    ids = jnp.arange(experts, dtype=jnp.int32)
    slot_is = (expert_slot[:, None] == ids[None, :]).astype(jnp.int32)
    slot_expert = jnp.sum(slot_is * ids[:, None], axis=0)
    counts = jnp.sum(block_counts[:, :, None] * slot_is[None], axis=1)
    used = (counts > 0).astype(jnp.int32)
    before = (ids[:, None] < ids[None, :]).astype(jnp.int32)
    rank = jnp.sum(used[:, None, :] * before[:, :, None], axis=0)
    user_ids = jnp.arange(USERS, dtype=jnp.int32)[:, None, None]
    chosen = used[None] * (rank[None] == user_ids).astype(jnp.int32)
    user_group = jnp.sum(chosen * ids[None, :, None], axis=1)
    user_count = jnp.sum(chosen * counts[None], axis=1)
    per_x = USERS * entries * 2 // share_x
    shape = (share_x, groups, per_x)
    member = lax.broadcasted_iota(jnp.int32, shape, 0) * per_x
    member = member + lax.broadcasted_iota(jnp.int32, shape, 2)
    first = member < entries * 2
    entry = (member >> 1) - jnp.where(first, 0, entries)
    group = jnp.where(first, user_group[0][None, :, None], user_group[1][None, :, None])
    limit = jnp.where(first, user_count[0][None, :, None], user_count[1][None, :, None])
    list_row = group * BLK + slot_expert[None, :, None]
    base = jnp.where(entry < limit, group * BLK + (member & 1), -100000)
    info = jnp.stack([list_row, base, entry + LIST_LANE], axis=-1)
    return info.reshape(-1, 3)


def exchange(array, axis):
    return lax.all_to_all(array, axis, split_axis=0, concat_axis=0, tiled=True)


def body(
    tokens, grad_output, gate_prob, w_gate, w_up, w_down, expert_slot, block_counts, block_lists
):
    groups = lax.axis_size(GROUP)
    share_y = lax.axis_size("y")
    share_x = lax.axis_size("x")
    width = tokens.shape[1]
    hid = w_gate.shape[2]
    entries = block_lists.shape[2]
    picked = USERS * entries * 2
    total = groups * picked
    count = total // share_x

    me_x = lax.axis_index("x")
    order = me_x[None].astype(jnp.int32)
    shifts = [[(i, (i + d) % share_x) for i in range(share_x)] for d in range(share_x)]

    def shift(array, d):
        return lax.ppermute(array, "x", shifts[d])

    gates = jnp.concatenate([w_gate[0], w_up[0]], axis=0)
    gates = lax.all_gather(gates, "x", axis=0, tiled=False)
    down = w_down[0].T
    right, left = shift(down, 1), shift(down, 3)

    packed = call(
        pack_kernel,
        jax.ShapeDtypeStruct((groups, BLK, LANES), BF16),
        (tokens.T, grad_output.T, gate_prob.T, block_lists.transpose(2, 0, 1)),
        VMEM_LARGE,
        scratch_shapes=[pltpu.VMEM((LANES, LANES), BF16)],
    )
    info = routing_info(expert_slot, block_counts, entries, share_x)
    mine = (expert_slot == lax.axis_index(GROUP)).astype(F32)
    mark = lax.pad(mine, jnp.zeros((), F32), ((P_LANE, 16, 0),))[None]
    spread = exchange(packed, GROUP).reshape(groups * BLK, LANES)
    spread, info, right, left = lax.optimization_barrier((spread, info, right, left))
    sent, pick = call(
        select_kernel,
        (
            jax.ShapeDtypeStruct((4 * total, 128), BF16),
            jax.ShapeDtypeStruct((total, groups * BLK), BF16),
        ),
        (spread, info),
        scratch_shapes=[pltpu.VMEM((4 * total, 128), F32)],
    )
    half = hid // 2
    panels = [gates, down, right, left, shift(right[:, 0:half], 1), shift(left[:, half:], 3)]
    pieces = (share_x * groups, 4 * picked // share_x, 128)
    tiles = exchange(sent.reshape(pieces), OWNERS).reshape(share_x, 4 * count, 128)

    act_shape = (share_y, 3 * count, hid // share_y)
    scalar_spec = pl.BlockSpec(memory_space=pltpu.SMEM)
    vmem_spec = pl.BlockSpec(memory_space=pltpu.VMEM)
    panel_specs = [pl.BlockSpec(memory_space=pl.ANY)] * 6
    panel_scratch = [
        pltpu.VMEM((4, 2 * width, hid), BF16),
        pltpu.VMEM((4, width, hid), BF16),
        pltpu.SemaphoreType.DMA((9,)),
    ]
    *rows, parts, prob = call(
        hidden_kernel,
        (jax.ShapeDtypeStruct((count, LANES), BF16),) * 4
        + (jax.ShapeDtypeStruct(act_shape, BF16), jax.ShapeDtypeStruct((count, 128), F32)),
        (order, tiles, mark, *panels),
        VMEM_LARGE,
        in_specs=[scalar_spec, vmem_spec, vmem_spec] + panel_specs,
        scratch_shapes=[pltpu.VMEM((3, count, hid), F32), pltpu.VMEM((4 * count, 128), F32)]
        + panel_scratch,
    )
    parts = exchange(parts, "y")
    rows = [shift(rows[d], STEPS[d]) if STEPS[d] else rows[d] for d in range(share_x)]
    parts, *rows = lax.optimization_barrier((parts, *rows))
    act = call(point_kernel, jax.ShapeDtypeStruct(act_shape[1:], BF16), (parts,))
    act = lax.all_gather(act, "y", axis=0, tiled=False)
    all_act = lax.all_gather(act, "x", axis=0, tiled=False)
    results = call(
        result_kernel,
        jax.ShapeDtypeStruct((share_x, 4 * count, 128), BF16),
        (order, act, prob, *panels),
        VMEM_LARGE,
        in_specs=[scalar_spec, vmem_spec, vmem_spec] + panel_specs,
        scratch_shapes=[pltpu.VMEM((count, LANES), F32), pltpu.VMEM((4 * count, 128), F32)]
        + panel_scratch,
    )
    weights = call(
        weight_kernel,
        (jax.ShapeDtypeStruct((width, hid), BF16),) * 3,
        (order, all_act, *(rows[STEPS.index(d)] for d in range(share_x))),
        VMEM_LARGE,
        in_specs=[scalar_spec] + [panel_specs[0]] * 5,
        scratch_shapes=[
            pltpu.VMEM((3, share_x, share_y, count, hid // share_y), BF16),
            pltpu.VMEM((share_x, count, LANES), BF16),
            pltpu.SemaphoreType.DMA((3, share_x)),
            pltpu.SemaphoreType.DMA((share_x,)),
        ],
    )
    back = exchange(results.reshape(pieces), OWNERS).reshape(4 * total, 128)
    summed = call(
        combine_kernel,
        jax.ShapeDtypeStruct((groups * BLK, LANES), BF16),
        (pick, back),
        scratch_shapes=[pltpu.VMEM((4 * total, 128), F32)],
    )
    home = exchange(summed.reshape(groups, BLK, LANES), GROUP).reshape(groups * BLK, LANES)
    home, *weights = lax.optimization_barrier((home, *weights))
    out, dx = call(
        unpack_kernel,
        (jax.ShapeDtypeStruct((width, groups * BLK), BF16),) * 2,
        (home,),
    )
    return (
        out.T,
        dx.T,
        weights[0][None],
        weights[1][None],
        weights[2].T[None],
    )


def solution(mesh):
    devices = mesh.devices.reshape(8, 2, 8, 4)
    inner = Mesh(devices, ("z", "core", "y", "x"))
    member = ("y", "x")
    in_specs = (
        P(GROUP, member),
        P(GROUP, member),
        P(GROUP, None),
        P(GROUP, member, None),
        P(GROUP, member, None),
        P(GROUP, None, member),
        P(),
        P(),
        P(GROUP, None, None),
    )
    out_specs = (
        P(GROUP, member),
        P(GROUP, member),
        P(GROUP, member, None),
        P(GROUP, member, None),
        P(GROUP, None, member),
    )
    return jax.shard_map(body, mesh=inner, in_specs=in_specs, out_specs=out_specs, check_vma=False)
```
